32 devices in a mesh: head: 4 (over y, core), shard: 8 (over z, x).
Axes of the slice: x: 2, y: 2, z: 4, core: 2. Of those that a mesh axis runs over, the one named last changes fastest.
Arguments:
- inputs: bfloat16 [4, 8, 4, 64, 2048], P(None, 'shard', 'head'), may hold values from -6 to 6
- segments: int32 [4, 8, 4, 64], P(None, 'shard'), may hold values from 0 to 2047, as said below
- query_weight: bfloat16 [2048, 256], P(('head', 'shard')), may hold values from -0.125 to 0.125
- key_weight: bfloat16 [2048, 256], P(('head', 'shard')), may hold values from -0.125 to 0.125
- value_weight: bfloat16 [2048, 2048], P(('head', 'shard')), may hold values from -0.125 to 0.125
- project_weight: bfloat16 [2048, 2048], P(('head', 'shard')), may hold values from -1.5 to 1.5
- attend_gain: bfloat16 [2048], P(('head', 'shard')), may hold values from 0.5 to 1.5
- gate_weight: bfloat16 [2048, 5632], P('shard', 'head'), may hold values from -0.125 to 0.125
- up_weight: bfloat16 [2048, 5632], P('shard', 'head'), may hold values from -0.125 to 0.125
- down_weight: bfloat16 [5632, 2048], P('head', 'shard'), may hold values from -0.078125 to 0.078125
- forward_gain: bfloat16 [2048], P(('head', 'shard')), may hold values from 0.5 to 1.5
- upstream: bfloat16 [4, 8, 4, 64, 2048], P(None, 'shard', 'head'), may hold values from -6 to 6
Outputs:
- outputs: bfloat16 [4, 8, 4, 64, 2048], P(None, 'shard', 'head')
- inputs_grad: float32 [4, 8, 4, 64, 2048], P(None, 'shard', 'head')
- query_grad: float32 [2048, 256], P(('head', 'shard'))
- key_grad: float32 [2048, 256], P(('head', 'shard'))
- value_grad: float32 [2048, 2048], P(('head', 'shard'))
- project_grad: float32 [2048, 2048], P(('head', 'shard'))
- attend_grad: float32 [2048], P(('head', 'shard'))
- gate_grad: float32 [2048, 5632], P('shard', 'head')
- up_grad: float32 [2048, 5632], P('shard', 'head')
- down_grad: float32 [5632, 2048], P('head', 'shard')
- forward_grad: float32 [2048], P(('head', 'shard'))
The draws below stay inside these ranges and needn't reach their ends.
Inputs may be any that keep to these rules, and one draw needn't show every extreme that they name: `segments`: A token's segment number is the position within its sequence of the first token of its document, so the numbers start at 0 and never fall from one token to the next; one of the 4 sequences is a single document, and another ends with a document of one token.
All inputs are finite; a program needn't handle non-finite values.
Results may differ from the reference program's by a relative error of at most 0.017.
Values may be sent and summed in bfloat16 or wider, within the bound.
No kernel may reach another device: no remote copies, remote signals or barrier semaphores. Data moves between devices by JAX's collectives and lax.ppermute only.
A program may use at most 576 MiB of HBM per device.

```python
import math
import jax
import jax.numpy as jnp
from jax import lax

D = 2048
FF = 5632
HEADS = 16
QK = 16
VD = 128
SEQS = 4
SUB = 64
BLOCKS = 8
GROUPS = 4
SEQ_LEN = 2048


def draw_segments(key, part):
    rate_key, flag_key, pick_key = jax.random.split(jax.random.fold_in(key, 17), 3)
    region_len = math.gcd(SEQ_LEN, 64)
    exponents = jax.random.randint(rate_key, (SEQS, SEQ_LEN // region_len), 3, 11)
    per_pos = jnp.repeat(exponents, region_len, axis=1)
    raw_bits = jax.random.randint(flag_key, (SEQS, SEQ_LEN), 0, 1 << 20)
    starts = raw_bits % jnp.left_shift(1, per_pos) == 0
    position = jnp.arange(SEQ_LEN, dtype=jnp.int32)[None, :]
    single_doc = jax.random.randint(pick_key, (), 0, SEQS)
    ending_doc = (single_doc + 1) % SEQS
    seq_index = jnp.arange(SEQS)[:, None]
    starts = starts | (seq_index == ending_doc) & (position == SEQ_LEN - 1)
    starts = starts & (position > 0) & (seq_index != single_doc)
    first_pos = jnp.where(starts, position, jnp.zeros_like(position))
    seg_ids = lax.cummax(first_pos, axis=1).astype(jnp.int32)
    return seg_ids.reshape(SEQS, BLOCKS, GROUPS, SUB)


def block_levels(rng, dims, cuts, least, top_value):
    level = 1.0
    for axis_at, shards_of in cuts:
        steps = jax.random.uniform(jax.random.fold_in(jax.random.fold_in(rng, 6), axis_at), (shards_of,), jnp.float32, least / len(cuts), top_value / len(cuts))
        level = level * jnp.repeat(jnp.exp(steps), dims[axis_at] // shards_of).reshape((-1,) + (1,) * (len(dims) - 1 - axis_at))
    return level


def scatter_about(rng, shape, deviation, most, cuts=(), kind=jnp.bfloat16):
    level = block_levels(rng, shape, cuts, -0.22, 0.18) if cuts else 1.0
    values = jax.random.normal(rng, shape, jnp.float32) * deviation * level
    return jnp.minimum(jnp.maximum(values, -most), most).astype(kind)


def setup_inputs(seed: int = 0) -> dict:
    streams_of = jax.random.split(jax.random.key(seed), 13)
    return {
        "inputs": scatter_about(streams_of[0], (SEQS, BLOCKS, GROUPS, SUB, D), 1.0, 6.0, ((1, 8), (2, 4))),
        "segments": draw_segments(jax.random.fold_in(streams_of[12], 71), 0),
        "query_weight": scatter_about(streams_of[2], (D, HEADS * QK), D ** -0.5, 0.125, ((0, 32),)),
        "key_weight": scatter_about(streams_of[3], (D, HEADS * QK), D ** -0.5, 0.125, ((0, 32),)),
        "value_weight": scatter_about(streams_of[4], (D, HEADS * VD), D ** -0.5, 0.125, ((0, 32),)),
        "project_weight": scatter_about(streams_of[5], (HEADS * VD, D), 16 ** -0.5, 1.5, ((0, 32),)),
        "attend_gain": jnp.clip(1.0 + 0.1 * jax.random.normal(streams_of[6], (D,), jnp.float32), 0.5, 1.5).astype(jnp.bfloat16),
        "gate_weight": scatter_about(streams_of[7], (D, FF), D ** -0.5, 0.125, ((0, 8), (1, 4))),
        "up_weight": scatter_about(streams_of[8], (D, FF), D ** -0.5, 0.125, ((0, 8), (1, 4))),
        "down_weight": scatter_about(streams_of[9], (FF, D), FF ** -0.5, 0.078125, ((0, 4), (1, 8))),
        "forward_gain": jnp.clip(1.0 + 0.1 * jax.random.normal(streams_of[10], (D,), jnp.float32), 0.5, 1.5).astype(jnp.bfloat16),
        "upstream": scatter_about(streams_of[11], (SEQS, BLOCKS, GROUPS, SUB, D), 1.0, 6.0, ((1, 8), (2, 4))),
    }


EPS_NORM = 1e-05
HIGH = lax.Precision.HIGHEST

@jax.custom_vjp
def low(v):
    return lax.optimization_barrier(v.astype(jnp.bfloat16)).astype(jnp.float32)

@jax.custom_vjp
def low_back(v):
    return v

def low_keep(v):
    return (low(v), None)

def low_pass(kept, grad):
    return (grad,)

def back_keep(v):
    return (v, None)

def back_low(kept, grad):
    return (low(grad),)
low.defvjp(low_keep, low_pass)
low_back.defvjp(back_keep, back_low)

def rounded_both(values):
    return low_back(low(values))

def features(values):
    qk_size = values.shape[-1]
    square = (values[..., :, None] * values[..., None, :]).reshape(values.shape[:-1] + (qk_size * qk_size,))
    ones_col = jnp.ones(values.shape[:-1] + (1,), values.dtype)
    return jnp.concatenate([ones_col, values * qk_size ** (-0.25), square / math.sqrt(2.0 * qk_size)], axis=-1)

def attend_sequence(queries, key_heads, value_heads, seg_ids):
    seq_len = queries.shape[0]
    block_size = math.gcd(seq_len, 512)
    block_count = seq_len // block_size
    query_blocks = queries.reshape(block_count, block_size, HEADS, QK).transpose(0, 2, 1, 3)
    key_blocks = key_heads.reshape(block_count, block_size, HEADS, QK).transpose(0, 2, 1, 3)
    value_blocks = value_heads.reshape(block_count, block_size, HEADS, VD).transpose(0, 2, 1, 3)
    seg_blocks = seg_ids.reshape(block_count, block_size)
    causal = lax.broadcasted_iota(jnp.int32, (block_size, block_size), 0) >= lax.broadcasted_iota(jnp.int32, (block_size, block_size), 1)
    feat_count = 1 + QK + QK * QK

    def advance(carried, pieces):
        state_now, normer, last_seg = carried
        query_b, key_b, value_b, seg_b = pieces
        visible = (causal & (seg_b[:, None] == seg_b[None, :])).astype(query_b.dtype)
        scores = jnp.einsum('htd,hsd->hts', query_b, key_b, precision=HIGH) / math.sqrt(QK)
        weights = (1.0 + scores + 0.5 * scores * scores) * visible[None]
        feat_query = features(query_b)
        feat_key = features(key_b)
        use_in = (seg_b == last_seg).astype(query_b.dtype)
        numerator = jnp.einsum('hts,hsc->htc', weights, value_b, precision=HIGH) + use_in[None, :, None] * jnp.einsum('htf,hfc->htc', feat_query, state_now, precision=HIGH)
        denominator = lax.optimization_barrier(jnp.sum(weights, axis=-1)) + use_in[None, :] * jnp.einsum('htf,hf->ht', feat_query, normer, precision=HIGH)
        attended = numerator / denominator[..., None]
        block_last = seg_b[-1]
        last_mask = (seg_b == block_last).astype(query_b.dtype)
        masked_key = feat_key * last_mask[None, :, None]
        keep_old = (block_last <= last_seg).astype(query_b.dtype)
        state_next = keep_old * state_now + jnp.einsum('htf,htc->hfc', masked_key, value_b, precision=HIGH)
        normer_next = keep_old * normer + lax.optimization_barrier(jnp.sum(masked_key, axis=1))
        return ((state_next, normer_next, block_last), attended)
    initial = (jnp.zeros((HEADS, feat_count, VD), queries.dtype), jnp.zeros((HEADS, feat_count), queries.dtype), jnp.asarray(-1.0, seg_ids.dtype))
    final_carry, results = lax.scan(jax.checkpoint(advance), initial, (query_blocks, key_blocks, value_blocks, seg_blocks))
    return results.transpose(0, 2, 1, 3).reshape(seq_len, HEADS * VD)

def reference(inputs, segments, query_weight, key_weight, value_weight, project_weight, attend_gain, gate_weight, up_weight, down_weight, forward_gain, upstream):
    seq_count = inputs.shape[0]
    seq_len = inputs.shape[1] * inputs.shape[2] * inputs.shape[3]
    hidden_in = inputs.reshape(seq_count, seq_len, D).astype(jnp.float32)
    seg_float = segments.reshape(seq_count, seq_len).astype(jnp.float32)

    def normalize(rows_in):
        return rows_in * lax.rsqrt(lax.optimization_barrier(jnp.mean(rows_in * rows_in, axis=-1, keepdims=True)) + EPS_NORM)

    def project(rows_in, matrix):
        return jnp.einsum('std,de->ste', rows_in, matrix, precision=HIGH)

    def forward(hidden, query_mat, key_mat, value_mat, project_mat, gain_one, gate_mat, up_mat, down_mat, gain_two):
        active_one = low(normalize(hidden) * gain_one)
        queries = rounded_both(project(active_one, query_mat))
        key_rows = rounded_both(project(active_one, key_mat))
        value_rows = rounded_both(project(active_one, value_mat))
        attended = jax.vmap(attend_sequence)(queries.reshape(seq_count, seq_len, HEADS, QK), key_rows.reshape(seq_count, seq_len, HEADS, QK), value_rows.reshape(seq_count, seq_len, HEADS, VD), seg_float)
        mixed = rounded_both(attended)
        attend_out = low_back(project(mixed, project_mat))
        residual = hidden + attend_out
        active_two = low(normalize(residual) * gain_two)
        gate_pre = low_back(project(active_two, gate_mat))
        upward = low_back(project(active_two, up_mat))
        hidden_act = low(jax.nn.silu(gate_pre) * upward)
        return residual + project(hidden_act, down_mat)
    result, pullback = jax.vjp(forward, hidden_in, query_weight.astype(jnp.float32), key_weight.astype(jnp.float32), value_weight.astype(jnp.float32), project_weight.astype(jnp.float32), attend_gain.astype(jnp.float32), gate_weight.astype(jnp.float32), up_weight.astype(jnp.float32), down_weight.astype(jnp.float32), forward_gain.astype(jnp.float32))
    gradients = pullback(upstream.reshape(seq_count, seq_len, D).astype(jnp.float32))
    return (result.astype(jnp.bfloat16).reshape(inputs.shape), gradients[0].reshape(inputs.shape), gradients[1], gradients[2], gradients[3], gradients[4], gradients[5], gradients[6], gradients[7], gradients[8], gradients[9])
```

```python
import functools
import math

import numpy as np

import jax
import jax.numpy as jnp
from jax import lax
from jax.experimental import pallas as pl
from jax.experimental.pallas import tpu as pltpu
from jax.sharding import Mesh
from jax.sharding import PartitionSpec as P

D = 2048
HEADS = 16
QK = 16
VD = 128
EPS = 1e-05
F32 = jnp.float32
BF16 = jnp.bfloat16
GROUP = ("hi", "core", "col")
FEAT = 1 + QK + QK * (QK + 1) // 2
FPAD = 256
FROWS = 160
PAYLOAD = 384


def feature_constants():
    left = np.zeros((128, FPAD), np.float32)
    right = np.zeros((128, FPAD), np.float32)
    rows = np.zeros((8, 2 * FPAD), np.float32)
    at = 0
    for i in range(QK):
        for j in range(i, QK):
            left[i, at] = 1.0
            right[j, at] = 1.0
            rows[1, at] = (1.0 if i == j else math.sqrt(2.0)) / math.sqrt(2.0 * QK)
            at += 1
    for i in range(QK):
        left[i, at] = 1.0
        rows[0, FPAD + at] = 1.0
        rows[1, at] = QK ** (-0.25)
        at += 1
    rows[0, at] = 1.0
    rows[0, FPAD + at] = 1.0
    rows[1, at] = 1.0
    align = np.zeros((4, 128, 128), np.float32)
    for part in range(4):
        for i in range(QK):
            align[part, part * QK + i, i] = 1.0
    return (
        jnp.asarray(np.concatenate([left, right], 1), BF16),
        jnp.asarray(rows, F32),
        jnp.asarray(align.transpose(1, 0, 2).reshape(128, 512), BF16),
    )


def dot(a, b):
    return jnp.dot(a, b, preferred_element_type=F32)


def dot_t(a, b):
    return lax.dot_general(a, b, (((1,), (1,)), ((), ())), preferred_element_type=F32)


def t_dot(a, b):
    return lax.dot_general(a, b, (((0,), (0,)), ((), ())), preferred_element_type=F32)


def swap(value, axis):
    return lax.ppermute(value, axis, [(0, 1), (1, 0)])


def gather8(own):
    half = own.shape[0] // 2
    over_x = swap(own, "col")
    over_y = swap(own, "hi")
    over_c = swap(own, "core")
    top = swap(over_y[:half], "col")
    low = swap(over_x[half:], "hi")
    over_xc = swap(over_x, "core")
    over_yc = swap(over_y, "core")
    over_xy = jnp.concatenate([top, low], 0)
    over_xyc = swap(over_xy, "core")
    return [own, over_c, over_y, over_yc, over_x, over_xc, over_xy, over_xyc]


def scatter8(parts):
    half = parts[0].shape[0] // 2
    low = [p.astype(BF16) for p in parts]

    def core_sum(j):
        return low[j].astype(F32) + swap(low[j + 1], "core").astype(F32)

    diag = core_sum(6).astype(BF16)
    from_x = swap(diag[:half], "col").astype(F32)
    from_y = swap(diag[half:], "hi").astype(F32)
    sum_x = core_sum(4)
    sum_y = core_sum(2)
    first_x = swap(sum_x[:half].astype(BF16), "col")
    first_y = swap(sum_y[half:].astype(BF16), "hi")
    last_x = swap((sum_x[half:] + from_y).astype(BF16), "col")
    last_y = swap((sum_y[:half] + from_x).astype(BF16), "hi")
    own = core_sum(0)
    got_x = jnp.concatenate([first_x, last_x], 0).astype(F32)
    got_y = jnp.concatenate([last_y, first_y], 0).astype(F32)
    return own + got_x + got_y


def walk(value, mask_of, up):
    rows = lax.axis_size("row")
    pairs = [(i, i + 1) if up else (i + 1, i) for i in range(rows - 1)]
    total = None
    now = value
    for hop in range(1, rows):
        now = lax.ppermute(now, "row", pairs)
        term = mask_of(hop)[:, None, None, None] * now.astype(F32)
        total = term if total is None else total + term
    return total


def ordered(ref, me, lanes=slice(None)):
    return jnp.concatenate([ref[p ^ me, 0, :, lanes] for p in range(8)], 0)


def put_ordered(ref, me, value, lanes=slice(None)):
    sub = value.shape[0] // 8
    for p in range(8):
        ref[p ^ me, 0, :, lanes] = value[p * sub : (p + 1) * sub]


def phi(aligned, feat, rows):
    both = dot(aligned, feat) + rows[0:1, :]
    a, b = both[:, :FPAD], both[:, FPAD:]
    return a, b, a * b * rows[1:2, :FPAD]


def phi_back(a, b, grad, feat, rows):
    scaled = grad * rows[1:2, :FPAD]
    return dot_t((scaled * b).astype(BF16), feat[:, :FPAD]) + dot_t(
        (scaled * a).astype(BF16), feat[:, FPAD:]
    )


def put_state(ref, head, state, norm):
    ref[0, head] = state[:FROWS].astype(BF16)
    high = norm.astype(BF16)
    low = (norm - high.astype(F32)).astype(BF16)
    ref[0, head, FEAT : FEAT + 1, :] = high[:, :128]
    ref[0, head, FEAT + 1 : FEAT + 2, :] = low[:, :128]
    ref[0, head, FEAT + 2 : FEAT + 3, :] = high[:, 128:]
    ref[0, head, FEAT + 3 : FEAT + 4, :] = low[:, 128:]


def get_state(ref, head):
    whole = ref[0, head]
    state = jnp.concatenate([whole, jnp.zeros((FPAD - FROWS, 128), F32)], 0)
    norm = jnp.concatenate(
        [
            whole[FEAT : FEAT + 1] + whole[FEAT + 1 : FEAT + 2],
            whole[FEAT + 2 : FEAT + 3] + whole[FEAT + 3 : FEAT + 4],
        ],
        1,
    )
    return state.astype(BF16), norm


def align4(qk, align_ref):
    out = dot(qk, align_ref[...]).astype(BF16)
    return [out[:, i * 128 : (i + 1) * 128] for i in range(4)]


def visible(cols, seg_row):
    t = cols.shape[0]
    causal = lax.broadcasted_iota(jnp.int32, (t, t), 0) >= lax.broadcasted_iota(jnp.int32, (t, t), 1)
    return causal & (cols[:, 0:1] == seg_row)


def state_kernel(me_ref, qkv_ref, cols_ref, feat_ref, rows_ref, align_ref, out_ref):
    me = me_ref[0]
    qk = ordered(qkv_ref, me, slice(256, 384))
    v = ordered(qkv_ref, me, slice(0, 256))
    last = cols_ref[0][:, 2:3]
    parts = align4(qk, align_ref)
    for head in range(2):
        _, _, feat = phi(parts[2 + head], feat_ref[...], rows_ref[...])
        feat = feat * last
        state = t_dot(feat.astype(BF16), v[:, head * 128 : (head + 1) * 128])
        put_state(out_ref, head, state, jnp.sum(feat, 0, keepdims=True))


def intra_kernel(me_ref, qkv_ref, cols_ref, seg_ref, align_ref, num_ref, den_ref):
    me = me_ref[0]
    qk = ordered(qkv_ref, me, slice(256, 384))
    v = ordered(qkv_ref, me, slice(0, 256))
    see = visible(cols_ref[0], seg_ref[0])
    parts = align4(qk, align_ref)
    den_ref[0] = jnp.zeros(den_ref.shape[1:], F32)
    for head in range(2):
        z = dot_t(parts[head], parts[2 + head])
        w = jnp.where(see, 1.0 + z * (0.25 + 0.03125 * z), 0.0)
        num_ref[0, :, head * 128 : (head + 1) * 128] = dot(
            w.astype(BF16), v[:, head * 128 : (head + 1) * 128]
        )
        den_ref[0, :, head : head + 1] = jnp.sum(w, 1, keepdims=True)


def output_kernel(
    me_ref, qkv_ref, cols_ref, feat_ref, rows_ref, align_ref, num_ref, den_ref, state_ref, o_ref, all_ref
):
    me = me_ref[0]
    qk = ordered(qkv_ref, me, slice(256, 384))
    use = cols_ref[0][:, 1:2]
    parts = align4(qk, align_ref)
    all_ref[0] = jnp.zeros(all_ref.shape[1:], F32)
    for head in range(2):
        lanes = slice(head * 128, (head + 1) * 128)
        _, _, feat = phi(parts[head], feat_ref[...], rows_ref[...])
        state, norm = get_state(state_ref, head)
        num = num_ref[0, :, lanes] + use * dot(feat.astype(BF16), state)
        den = den_ref[0, :, head : head + 1] + use * jnp.sum(feat * norm, 1, keepdims=True)
        all_ref[0, :, head : head + 1] = den
        put_ordered(o_ref, me, (num / den).astype(BF16), lanes)


def back_parts(me, o_ref, do_ref, den_ref, head):
    lanes = slice(head * 128, (head + 1) * 128)
    inv = 1.0 / den_ref[0, :, head : head + 1]
    do = ordered(do_ref, me, lanes).astype(F32)
    o = ordered(o_ref, me, lanes).astype(F32)
    return (do * inv).astype(BF16), -jnp.sum(do * o, 1, keepdims=True) * inv


def back_state_kernel(
    me_ref, qkv_ref, cols_ref, feat_ref, rows_ref, align_ref, o_ref, do_ref, den_ref, out_ref
):
    me = me_ref[0]
    qk = ordered(qkv_ref, me, slice(256, 384))
    use = cols_ref[0][:, 1:2]
    parts = align4(qk, align_ref)
    for head in range(2):
        g, c = back_parts(me, o_ref, do_ref, den_ref, head)
        _, _, feat = phi(parts[head], feat_ref[...], rows_ref[...])
        feat = feat * use
        put_state(out_ref, head, t_dot(feat.astype(BF16), g), jnp.sum(feat * c, 0, keepdims=True))


def back_intra_kernel(
    me_ref, qkv_ref, cols_ref, seg_ref, feat_ref, rows_ref, align_ref, o_ref, do_ref, den_ref, state_ref,
    dq_ref, dk_ref, dv_ref,
):
    me = me_ref[0]
    qk = ordered(qkv_ref, me, slice(256, 384))
    v = ordered(qkv_ref, me, slice(0, 256))
    use = cols_ref[0][:, 1:2]
    see = visible(cols_ref[0], seg_ref[0])
    parts = align4(qk, align_ref)
    for head in range(2):
        lanes = slice(head * 128, (head + 1) * 128)
        g, c = back_parts(me, o_ref, do_ref, den_ref, head)
        z = dot_t(parts[head], parts[2 + head])
        w = jnp.where(see, 1.0 + z * (0.25 + 0.03125 * z), 0.0)
        dv_ref[0, :, lanes] = t_dot(w.astype(BF16), g)
        dw = dot_t(g, v[:, lanes]) + c
        dz = jnp.where(see, dw * (0.25 + 0.0625 * z), 0.0).astype(BF16)
        a, b, _ = phi(parts[head], feat_ref[...], rows_ref[...])
        state, norm = get_state(state_ref, head)
        grad = use * (dot_t(g, state) + c * norm)
        dq_ref[0, :, lanes] = dot(dz, parts[2 + head]) + phi_back(a, b, grad, feat_ref[...], rows_ref[...])
        dk_ref[0, :, lanes] = t_dot(dz, parts[head])


def back_output_kernel(
    me_ref, qkv_ref, cols_ref, feat_ref, rows_ref, align_ref, state_ref, dq_ref, dk_ref, dv_ref, out_ref
):
    me = me_ref[0]
    qk = ordered(qkv_ref, me, slice(256, 384))
    v = ordered(qkv_ref, me, slice(0, 256))
    last = cols_ref[0][:, 2:3]
    parts = align4(qk, align_ref)
    packed = None
    for head in range(2):
        lanes = slice(head * 128, (head + 1) * 128)
        a, b, feat = phi(parts[2 + head], feat_ref[...], rows_ref[...])
        state, norm = get_state(state_ref, head)
        grad = last * (dot_t(v[:, lanes], state) + norm)
        dk = dk_ref[0, :, lanes] + phi_back(a, b, grad, feat_ref[...], rows_ref[...])
        dv = dv_ref[0, :, lanes] + last * dot(feat.astype(BF16), state)
        put_ordered(out_ref, me, dv.astype(BF16), lanes)
        place = align_ref[...]
        term = dot_t(dq_ref[0, :, lanes].astype(BF16), place[:, head * 128 : (head + 1) * 128]) + dot_t(
            dk.astype(BF16), place[:, (2 + head) * 128 : (3 + head) * 128]
        )
        packed = term if packed is None else packed + term
    put_ordered(out_ref, me, packed.astype(BF16), slice(256, 384))


def attention_call(kernel, me, ins, kinds, outs):
    def spec(a, kind):
        if kind == "s":
            return pl.BlockSpec((8, 1) + a.shape[2:], lambda i, m: (0, i, 0, 0))
        rest = len(a.shape) - 1
        if kind == "q":
            return pl.BlockSpec((1,) + a.shape[1:], lambda i, m: (i,) + (0,) * rest)
        return pl.BlockSpec(a.shape, lambda i, m: (0,) * (rest + 1))

    seqs = ins[0].shape[1]
    return pl.pallas_call(
        kernel,
        out_shape=[jax.ShapeDtypeStruct(a.shape, a.dtype) for a, _ in outs],
        grid_spec=pltpu.PrefetchScalarGridSpec(
            num_scalar_prefetch=1,
            grid=(seqs,),
            in_specs=[spec(a, k) for a, k in zip(ins, kinds)],
            out_specs=[spec(a, k) for a, k in outs],
        ),
        compiler_params=pltpu.CompilerParams(
            dimension_semantics=("arbitrary",), vmem_limit_bytes=48 * 1024 * 1024
        ),
        name=kernel.__name__,
    )(me, *ins)


def pick(cond, a, b):
    return jnp.where(cond, a, b)


def half_columns(gate, up, which, n_main, n_mid):
    mid = slice(n_main, n_main + 2 * n_mid)
    main = slice(0, n_main) if which == 0 else slice(n_main + 2 * n_mid, None)
    part = slice(0, n_mid) if which == 0 else slice(n_mid, None)
    return jnp.concatenate([gate[:, main], up[:, main], gate[:, mid][:, part], up[:, mid][:, part]], 1)


def body(inputs, segments, qw, kw, vw, pw, again, gw, uw, dw, fgain, upstream):
    hi, core, row, col = (lax.axis_index(a) for a in ("hi", "core", "row", "col"))
    rows = lax.axis_size("row")
    shards = 2 * rows
    me3 = (4 * col + 2 * hi + core).astype(jnp.int32)
    me = me3[None]
    seqs, sub = inputs.shape[0], inputs.shape[3]
    tokens = seqs * sub
    span = 8 * sub
    n_rows = qw.shape[0]
    is0 = col == 0
    ff = gw.shape[1]
    n_mid = 64
    n_main = ff // 2 - n_mid
    feat_c, rows_c, align_c = feature_constants()

    x = inputs.reshape(tokens, D)
    xs = jnp.stack(gather8(x))
    ups = jnp.stack(gather8(upstream.reshape(tokens, D)))

    gain_one = again.astype(F32)[:, None]
    seg_own = segments.reshape(seqs, 4 * sub)
    seg_other = swap(seg_own, "col")
    seg = jnp.concatenate([pick(is0, seg_own, seg_other), pick(is0, seg_other, seg_own)], 1)
    last_seg = seg[:, -1]

    def by_dest(w, scale):
        return (w.astype(F32) * scale).astype(BF16).reshape(n_rows, 8, -1)

    extra = jnp.zeros((n_rows, PAYLOAD - 320), F32)
    extra = extra.at[:, 0].set(fgain.astype(F32))
    extra = extra.at[:seqs, 1].set((last_seg // 128).astype(F32))
    extra = extra.at[:seqs, 2].set((last_seg % 128).astype(F32))
    payload = jnp.concatenate(
        [
            by_dest(vw, gain_one),
            by_dest(qw, gain_one),
            by_dest(kw, gain_one),
            jnp.broadcast_to(extra.astype(BF16)[:, None], (n_rows, 8, PAYLOAD - 320)),
        ],
        2,
    ).transpose(1, 0, 2)
    payload = lax.all_to_all(payload, GROUP, split_axis=0, concat_axis=0, tiled=True)
    gathered = lax.all_gather(payload, "row", axis=0, tiled=False)
    w_qkv = (
        gathered.reshape(rows, 4, 2, n_rows, PAYLOAD).transpose(1, 0, 2, 3, 4).reshape(D, PAYLOAD)
    )
    gain_two = w_qkv[:, 320].astype(F32)[None, :]
    lasts = gathered[:, 0, :seqs, 321:323].astype(F32)
    lasts = lasts[:, :, 0] * 128.0 + lasts[:, :, 1]

    shard_pairs = [(s, (s % rows) * 2 + s // rows) for s in range(shards)]
    moved = lax.ppermute(pw, ("row", "col"), shard_pairs)
    w_proj = lax.all_gather(moved, "row", axis=0, tiled=True)

    mine = pick(is0, half_columns(gw, uw, 0, n_main, n_mid), half_columns(gw, uw, 1, n_main, n_mid))
    theirs = pick(is0, half_columns(gw, uw, 1, n_main, n_mid), half_columns(gw, uw, 0, n_main, n_mid))
    got = swap(theirs, "col")
    gu_rows = jnp.concatenate([pick(is0, mine, got), pick(is0, got, mine)], 0)
    w_gu = lax.all_gather(gu_rows, "row", axis=0, tiled=True)
    down0 = dw[: n_main + n_mid]
    down1 = jnp.concatenate([dw[n_main + 2 * n_mid :], dw[n_main + n_mid : n_main + 2 * n_mid]], 0)
    d_mine, d_theirs = pick(is0, down0, down1), pick(is0, down1, down0)
    d_got = swap(d_theirs, "col")
    d_cols = jnp.stack([pick(is0, d_mine, d_got), pick(is0, d_got, d_mine)])
    w_down = lax.all_gather(d_cols, "row", axis=0, tiled=True)
    w_down = w_down.transpose(1, 0, 2).reshape(ff // 2, D)

    segf = seg.astype(F32)
    before = jnp.where(row > 0, lasts[jnp.maximum(row - 1, 0)], -1.0)
    here = lasts[row]
    use_in = (segf == before[:, None]).astype(F32)
    is_last = (segf == here[:, None]).astype(F32)
    cols = jnp.stack([segf, use_in, is_last] + [segf] * 5, -1)
    seg_row = segf[:, None, :]

    def mask_up(hop):
        other = lasts[jnp.maximum(row - hop, 0)]
        return ((other == before) & (row >= hop)).astype(F32)

    def mask_down(hop):
        other = lasts[jnp.minimum(row + hop - 1, rows - 1)]
        return ((other == here) & (row + hop < rows)).astype(F32)

    xf = xs.reshape(8 * tokens, D)
    xf32 = xf.astype(F32)
    inv_one = lax.rsqrt(jnp.mean(xf32 * xf32, -1, keepdims=True) + EPS)
    qkv = (dot(xf, w_qkv) * inv_one).astype(BF16).reshape(8, seqs, sub, PAYLOAD)
    sds = jax.ShapeDtypeStruct
    st = sds((seqs, 2, FROWS, 128), BF16)
    (state,) = attention_call(
        state_kernel, me, [qkv, cols, feat_c, rows_c, align_c], "sqccc", [(st, "q")]
    )
    num, den_in = attention_call(
        intra_kernel, me, [qkv, cols, seg_row, align_c], "sqqc",
        [(sds((seqs, span, 256), F32), "q"), (sds((seqs, span, 8), F32), "q")],
    )
    state_in = walk(state, mask_up, True)
    o, den = attention_call(
        output_kernel, me, [qkv, cols, feat_c, rows_c, align_c, num, den_in, state_in], "sqcccqqq",
        [(sds((8, seqs, sub, 256), BF16), "s"), (sds((seqs, span, 8), F32), "q")],
    )
    of = o.reshape(8 * tokens, 256)
    att = dot(of, w_proj).reshape(8, tokens, D)
    residual = x.astype(F32) + scatter8([att[j] for j in range(8)])

    inv_two = lax.rsqrt(jnp.mean(residual * residual, -1, keepdims=True) + EPS)
    normed_two = residual * inv_two
    a2 = jnp.stack(gather8((normed_two * gain_two).astype(BF16))).reshape(8 * tokens, D)
    up_rows = ups.reshape(8 * tokens, D)
    gu = dot(a2, w_gu)
    dh = dot_t(up_rows, w_down)
    g = jnp.concatenate([gu[:, :n_main], gu[:, 2 * n_main : 2 * n_main + n_mid]], 1)
    u = jnp.concatenate([gu[:, n_main : 2 * n_main], gu[:, 2 * n_main + n_mid :]], 1)
    sg = jax.nn.sigmoid(g)
    silu = g * sg
    h = (silu * u).astype(BF16)
    dg = (dh * u * (sg * (1.0 + g * (1.0 - sg)))).astype(BF16)
    du = (dh * silu).astype(BF16)
    dgu = jnp.concatenate([dg[:, :n_main], du[:, :n_main], dg[:, n_main:], du[:, n_main:]], 1)
    da2 = dot_t(dgu, w_gu).reshape(8, tokens, D)
    grad_a2 = scatter8([da2[j] for j in range(8)])
    down_out = dot(h, w_down).reshape(8, tokens, D)
    outputs = (residual + scatter8([down_out[j] for j in range(8)])).astype(BF16)
    down_g = t_dot(h, up_rows)
    gu_g = t_dot(a2, dgu)
    gain_two_part = jnp.sum(gu_g * w_gu.astype(F32), 1)

    down_g = down_g.astype(BF16).reshape(ff // 2, rows, 2, D // shards).transpose(1, 2, 0, 3)
    down_g = lax.psum_scatter(down_g, "row", scatter_dimension=0, tiled=False)
    gu_g = lax.psum_scatter(gu_g.astype(BF16), "row", scatter_dimension=0, tiled=True)

    dy = upstream.reshape(tokens, D).astype(F32)
    e = grad_a2 * gain_two
    grad_r = dy + inv_two * (e - normed_two * jnp.mean(e * normed_two, -1, keepdims=True))
    datt = jnp.stack(gather8(grad_r.astype(BF16))).reshape(8 * tokens, D)
    do = dot_t(datt, w_proj).astype(BF16).reshape(8, seqs, sub, 256)
    proj_g = t_dot(of, datt).astype(BF16)
    proj_g = lax.psum_scatter(proj_g, "row", scatter_dimension=0, tiled=True)
    project_grad = lax.ppermute(proj_g, ("row", "col"), [(b, a) for a, b in shard_pairs]).astype(F32)

    (dstate,) = attention_call(
        back_state_kernel, me, [qkv, cols, feat_c, rows_c, align_c, o, do, den], "sqcccssq", [(st, "q")]
    )
    part = sds((seqs, span, 256), F32)
    dq, dk, dv = attention_call(
        back_intra_kernel, me, [qkv, cols, seg_row, feat_c, rows_c, align_c, o, do, den, state_in],
        "sqqcccssqq", [(part, "q")] * 3,
    )
    dstate_out = walk(dstate, mask_down, False)
    (dqkv,) = attention_call(
        back_output_kernel, me, [qkv, cols, feat_c, rows_c, align_c, dstate_out, dq, dk, dv], "sqcccqqqq",
        [(sds((8, seqs, sub, PAYLOAD), BF16), "s")],
    )
    dqkv = dqkv.reshape(8 * tokens, PAYLOAD)
    f_part = dot_t(dqkv, w_qkv).reshape(8, tokens, D)
    f = scatter8([f_part[j] for j in range(8)])
    inv_own = inv_one[:tokens]
    normed_one = x.astype(F32) * inv_own
    inputs_grad = grad_r + inv_own * (f - normed_one * jnp.mean(f * normed_one, -1, keepdims=True))

    scaled = (dqkv.astype(F32) * inv_one).astype(BF16)
    qkv_g = t_dot(xf, scaled)
    lane = lax.broadcasted_iota(jnp.int32, (1, PAYLOAD), 1)
    qkv_g = jnp.where(lane == 320, gain_two_part[:, None], qkv_g).astype(BF16)
    qkv_g = qkv_g.reshape(4, rows, 2, n_rows, PAYLOAD).transpose(1, 0, 2, 3, 4)
    qkv_g = lax.psum_scatter(qkv_g, "row", scatter_dimension=0, tiled=False)
    qkv_g = lax.all_to_all(
        qkv_g.reshape(8, n_rows, PAYLOAD), GROUP, split_axis=0, concat_axis=0, tiled=True
    ).astype(F32)
    per_row = qkv_g.transpose(1, 0, 2)
    v_g = per_row[:, :, :256].reshape(n_rows, -1)
    q_g = per_row[:, :, 256:288].reshape(n_rows, -1)
    k_g = per_row[:, :, 288:320].reshape(n_rows, -1)
    forward_grad = jnp.sum(per_row[:, :, 320], 1) / fgain.astype(F32)
    attend_grad = (
        jnp.sum(v_g * vw.astype(F32), 1) + jnp.sum(q_g * qw.astype(F32), 1) + jnp.sum(k_g * kw.astype(F32), 1)
    )

    d_keep, d_send = pick(is0, down_g[0], down_g[1]), pick(is0, down_g[1], down_g[0])
    d_got = swap(d_send, "col")
    d0, d1 = pick(is0, d_keep, d_got).astype(F32), pick(is0, d_got, d_keep).astype(F32)
    down_grad = jnp.concatenate([d0, d1[n_main:], d1[:n_main]], 0)
    block = gu_g.shape[0] // 2
    g_keep = pick(is0, gu_g[:block], gu_g[block:])
    g_got = swap(pick(is0, gu_g[block:], gu_g[:block]), "col")
    g0, g1 = pick(is0, g_keep, g_got).astype(F32), pick(is0, g_got, g_keep).astype(F32)
    m = 2 * n_main
    gate_grad = jnp.concatenate(
        [g0[:, :n_main], g0[:, m : m + n_mid], g1[:, m : m + n_mid], g1[:, :n_main]], 1
    )
    up_grad = jnp.concatenate(
        [g0[:, n_main:m], g0[:, m + n_mid :], g1[:, m + n_mid :], g1[:, n_main:m]], 1
    )
    return (
        outputs.reshape(inputs.shape),
        inputs_grad.reshape(inputs.shape),
        q_g * gain_one,
        k_g * gain_one,
        v_g * gain_one,
        project_grad,
        attend_grad,
        gate_grad,
        up_grad,
        down_grad,
        forward_grad,
    )


def solution(mesh):
    heads, shards = mesh.devices.shape
    fine = Mesh(mesh.devices.reshape(heads // 2, 2, shards // 2, 2), ("hi", "core", "row", "col"))
    h, s = ("hi", "core"), ("row", "col")
    every = P(h + s)
    tokens = P(None, s, h)
    return jax.shard_map(
        body,
        mesh=fine,
        in_specs=(
            tokens, P(None, s), every, every, every, every, every, P(s, h), P(s, h), P(h, s), every, tokens,
        ),
        out_specs=(
            tokens, tokens, every, every, every, every, every, P(s, h), P(s, h), P(h, s), every,
        ),
        check_vma=False,
    )
```

```python
import math

import numpy as np

import jax
import jax.numpy as jnp
from jax import lax
from jax.experimental import pallas as pl
from jax.experimental.pallas import tpu as pltpu
from jax.sharding import Mesh
from jax.sharding import PartitionSpec as P

D = 2048
HEADS = 16
QK = 16
VD = 128
EPS = 1e-05
F32 = jnp.float32
BF16 = jnp.bfloat16
GROUP = ("hi", "core", "col")
FEAT = 1 + QK + QK * (QK + 1) // 2
FPAD = 256
FROWS = 160
PAYLOAD = 384


def feature_constants():
    left = np.zeros((128, FPAD), np.float32)
    right = np.zeros((128, FPAD), np.float32)
    rows = np.zeros((8, 2 * FPAD), np.float32)
    at = 0
    for i in range(QK):
        for j in range(i, QK):
            left[i, at] = 1.0
            right[j, at] = 1.0
            rows[1, at] = (1.0 if i == j else math.sqrt(2.0)) / math.sqrt(2.0 * QK)
            at += 1
    for i in range(QK):
        left[i, at] = 1.0
        rows[0, FPAD + at] = 1.0
        rows[1, at] = QK ** (-0.25)
        at += 1
    rows[0, at] = 1.0
    rows[0, FPAD + at] = 1.0
    rows[1, at] = 1.0
    align = np.zeros((4, 128, 128), np.float32)
    for part in range(4):
        for i in range(QK):
            align[part, part * QK + i, i] = 1.0
    return (
        jnp.asarray(np.concatenate([left, right], 1), BF16),
        jnp.asarray(rows, F32),
        jnp.asarray(align.transpose(1, 0, 2).reshape(128, 512), BF16),
    )


def dot(a, b):
    return jnp.dot(a, b, preferred_element_type=F32)


def dot_t(a, b):
    return lax.dot_general(a, b, (((1,), (1,)), ((), ())), preferred_element_type=F32)


def t_dot(a, b):
    return lax.dot_general(a, b, (((0,), (0,)), ((), ())), preferred_element_type=F32)


def swap(value, axis):
    return lax.ppermute(value, axis, [(0, 1), (1, 0)])


def after(value, *others):
    if not others:
        return value

    def gate(*refs):
        pass

    return pl.pallas_call(
        gate,
        in_specs=[pl.BlockSpec(memory_space=pl.ANY)] * (1 + len(others)),
        out_specs=pl.BlockSpec(memory_space=pl.ANY),
        out_shape=jax.ShapeDtypeStruct(value.shape, value.dtype),
        input_output_aliases={0: 0},
        cost_estimate=pl.CostEstimate(flops=0, transcendentals=0, bytes_accessed=0),
        name="gate",
    )(value, *others)


def gather8(own, first=None):
    half = own.shape[0] // 2
    over_x = swap(own, "col")
    over_y = swap(own, "hi")
    over_c = swap(own, "core")
    if first is not None:
        done = first(own)
        over_x, over_y = after(over_x, done), after(over_y, done)
    top = swap(over_y[:half], "col")
    low = swap(over_x[half:], "hi")
    return [
        (own, 0, 0),
        (over_c, 1, 0),
        (over_y, 2, 0),
        (swap(over_y, "core"), 3, 0),
        (over_x, 4, 0),
        (swap(over_x, "core"), 5, 0),
        (top, 6, 0),
        (low, 6, half),
        (swap(top, "core"), 7, 0),
        (swap(low, "core"), 7, half),
    ]


def scatter_steps(parts):
    def both(one, two, start, end):
        return one[start:end].astype(F32) + two[start:end].astype(F32)

    own, other, y, yc, x, xc, xy, xyc = parts
    n = xy.shape[0]
    half = n // 2
    xyc = swap(xyc, "core")
    xc = swap(xc, "core")
    yc = swap(yc, "core")
    other = swap(other, "core")
    to_x = both(xy, xyc, 0, half).astype(BF16)
    to_y = both(xy, xyc, half, n).astype(BF16)
    near_x = both(x, xc, 0, half).astype(BF16)
    near_y = both(y, yc, half, n).astype(BF16)
    from_x, from_y = swap(to_x, "col"), swap(to_y, "hi")
    first_x, first_y = swap(near_x, "col"), swap(near_y, "hi")
    done = yield [to_x, to_y, near_x, near_y]
    from_x, from_y = after(from_x, *done), after(from_y, *done)
    far_x = (both(x, xc, half, n) + from_y.astype(F32)).astype(BF16)
    far_y = (both(y, yc, 0, half) + from_x.astype(F32)).astype(BF16)
    last_x, last_y = swap(far_x, "col"), swap(far_y, "hi")
    done = yield [far_x, far_y]
    last_x, last_y = after(last_x, *done), after(last_y, *done)
    return own, other, first_x, last_y, last_x, first_y


def walk_steps(value, linked, joined, up):
    rows = lax.axis_size("row")
    total = None
    now = value
    step = 1
    while step < rows:
        pairs = [(i, i + step) if up else (i + step, i) for i in range(rows - step)]
        came = lax.ppermute(now, "row", pairs)
        done = yield now, came
        wide = after(came, *done).astype(F32)
        term = joined(step)[:, None, None, None] * wide
        total = term if total is None else total + term
        if 2 * step < rows:
            now = (now.astype(F32) + linked(step)[:, None, None, None] * wide).astype(BF16)
        step = 2 * step
    return total


def finish(steps, done=()):
    try:
        steps.send(done)
        while True:
            steps.send(())
    except StopIteration as end:
        return end.value


def scatter8(parts, *kernels):
    steps = scatter_steps(parts)
    sent = next(steps)
    for i, kernel in enumerate(kernels):
        done = kernel(sent)
        if i == 1:
            return finish(steps, done)
        sent = steps.send(done)
    return finish(steps)


def params(mib=60):
    return pltpu.CompilerParams(dimension_semantics=("arbitrary",), vmem_limit_bytes=mib * 1024 * 1024)


def cost(flops, *arrays):
    return pl.CostEstimate(
        flops=int(flops),
        transcendentals=0,
        bytes_accessed=int(sum(math.prod(a.shape) * a.dtype.itemsize for a in arrays)),
    )


def slot_call(kernel, pieces, ins, outs, flops, deps=(), whole=()):
    n = len(pieces)
    width = pieces[0][0].shape[1]
    per = pieces[0][0].shape[0]

    def wrapped(*refs):
        rows = refs[:n]
        at = n + len(ins)
        rest = refs[n:at] + refs[at + len(deps) : at + len(deps) + len(outs) + len(whole)]
        buf, sem = refs[-2:]
        i = pl.program_id(0)

        @pl.when(i == 0)
        def _():
            for (a, slot, start), ref in zip(pieces, rows):
                pltpu.make_async_copy(ref, buf.at[slot, pl.ds(start, a.shape[0])], sem.at[slot]).start()

        pltpu.make_async_copy(buf.at[i], buf.at[i], sem.at[i]).wait()
        kernel(buf.at[i], *rest)

    def spec(a, by_slot):
        rest = len(a.shape) - 1
        if by_slot:
            return pl.BlockSpec((None,) + a.shape[1:], lambda i: (i,) + (0,) * rest)
        return pl.BlockSpec(a.shape, lambda i: (0,) * (rest + 1))

    return pl.pallas_call(
        wrapped,
        grid=(8,),
        in_specs=[pl.BlockSpec(memory_space=pltpu.HBM)] * n
        + [spec(a, k) for a, k in ins]
        + [pl.BlockSpec(memory_space=pl.ANY)] * len(deps),
        out_specs=[spec(a, True) for a in outs] + [spec(a, False) for a in whole],
        out_shape=list(outs) + list(whole),
        scratch_shapes=[pltpu.VMEM((8, per, width), BF16), pltpu.SemaphoreType.DMA((8,))],
        compiler_params=params(),
        cost_estimate=cost(flops, *[a for a, _, _ in pieces], *[a for a, _ in ins], *outs, *whole),
        name=kernel.__name__,
    )(*[a for a, _, _ in pieces], *[a for a, _ in ins], *deps)


def grad_call(kernel, pieces, tile, whole, ins, outs, flops, index=lambda i: i, steps=None, deps=()):
    n = len(pieces)
    width = pieces[0][0].shape[1]
    places = [(slot, start, a.shape[0]) for a, slot, start in pieces]

    def wrapped(*refs):
        at = n + len(whole) + len(ins)
        kernel(list(zip(refs[:n], places)), *refs[n:at], *refs[at + len(deps) :])

    def fixed(a):
        rest = len(a.shape)
        return pl.BlockSpec(a.shape, lambda i: (0,) * rest)

    return pl.pallas_call(
        wrapped,
        grid=(steps or width // tile,),
        in_specs=[pl.BlockSpec((a.shape[0], tile), lambda i: (0, index(i))) for a, _, _ in pieces]
        + [fixed(a) for a in whole]
        + [pl.BlockSpec(block, where) for _, block, where in ins]
        + [pl.BlockSpec(memory_space=pl.ANY)] * len(deps),
        out_specs=[pl.BlockSpec(block, where) for _, block, where in outs],
        out_shape=[a for a, _, _ in outs],
        compiler_params=params(),
        cost_estimate=cost(
            flops, *[a for a, _, _ in pieces], *whole, *[a for a, _, _ in ins], *[a for a, _, _ in outs]
        ),
        name=kernel.__name__,
    )(*[a for a, _, _ in pieces], *whole, *[a for a, _, _ in ins], *deps)


def summed(rows, right):
    total = None
    for ref, (slot, start, n) in rows:
        term = t_dot(ref[...], right[slot, start : start + n, :])
        total = term if total is None else total + term
    return total


def qkv_kernel(x_ref, given_ref, qkv_ref, inv_ref, w_ref):
    @pl.when(pl.program_id(0) == 0)
    def _():
        rows, groups, n, _ = given_ref.shape
        for g in range(groups):
            for r in range(rows):
                w_ref[pl.ds((g * rows + r) * n, n), :] = given_ref[r, g]

    x = x_ref[...]
    wide = x.astype(F32)
    inv = lax.rsqrt(jnp.sum(wide * wide, 1, keepdims=True) * (1.0 / x.shape[1]) + EPS)
    qkv_ref[...] = (dot(x, w_ref[...]) * inv).astype(BF16)
    inv_ref[...] = jnp.broadcast_to(inv, inv_ref.shape)


def ffn_in_kernel(a_ref, w_ref, gu_ref, h_ref, turned_ref):
    gu = dot(a_ref[...], w_ref[...])
    gu_ref[...] = gu.astype(BF16)
    m = (gu.shape[1] - 128) // 2
    g, u = gu[:, :m], gu[:, m : 2 * m]
    h_ref[:, :m] = (g * jax.nn.sigmoid(g) * u).astype(BF16)
    g = gu[:, 2 * m :]
    u = pltpu.roll(g, 64, 1)
    first = lax.broadcasted_iota(jnp.int32, g.shape, 1) < 64
    h_ref[:, m:] = jnp.where(first, g * jax.nn.sigmoid(g) * u, 0.0).astype(BF16)
    turned_ref[...] = jnp.transpose(h_ref[...])


def ffn_back_kernel(up_ref, w_ref, gu_ref, out_ref):
    up = up_ref[...]
    total = None
    for i in range(8):
        term = dot_t(up[:, i * 256 : (i + 1) * 256], w_ref[i])
        total = term if total is None else total + term
    m = total.shape[1] - 64

    def both(g, u, dh):
        s = jax.nn.sigmoid(g)
        return dh * u * (s * (1.0 + g * (1.0 - s))), dh * (g * s)

    gu = gu_ref[...].astype(F32)
    dg, du = both(gu[:, :m], gu[:, m : 2 * m], total[:, :m])
    out_ref[:, :m] = dg.astype(BF16)
    out_ref[:, m : 2 * m] = du.astype(BF16)
    mid = gu[:, 2 * m :]
    other = pltpu.roll(mid, 64, 1)
    first = lax.broadcasted_iota(jnp.int32, mid.shape, 1) < 64
    dh = jnp.concatenate([total[:, m:], total[:, m:]], 1)
    dg, du = both(jnp.where(first, mid, other), jnp.where(first, other, mid), dh)
    out_ref[:, 2 * m :] = jnp.where(first, dg, du).astype(BF16)


def down_grad_kernel(rows, h_ref, out_ref):
    total = None
    for ref, (slot, start, n) in rows:
        term = dot(h_ref[slot, : out_ref.shape[1], start : start + n], ref[...])
        total = term if total is None else total + term
    out_ref[0] = total.astype(BF16)


def gu_grad_kernel(rows, right_ref, w_ref, out_ref, gain_ref):
    total = summed(rows, right_ref)
    out_ref[...] = total.astype(BF16)
    gain_ref[...] = jnp.broadcast_to(
        jnp.sum(total * w_ref[...].astype(F32), 1, keepdims=True), gain_ref.shape
    )


def do_kernel(d_ref, w_ref, out_ref):
    out_ref[...] = dot_t(d_ref[...], w_ref[...]).astype(BF16)


def proj_grad_kernel(rows, o_ref, out_ref):
    total = None
    for ref, (slot, start, n) in rows:
        term = t_dot(o_ref[slot, start : start + n, :], ref[...])
        total = term if total is None else total + term
    out_ref[...] = total.astype(BF16)


def qkv_grad_kernel(rows, right_ref, gain_ref, out_ref):
    total = summed(rows, right_ref)
    lane = lax.broadcasted_iota(jnp.int32, (1, 128), 1)
    total = jnp.concatenate([total[:, :256], jnp.where(lane == 64, gain_ref[...], total[:, 256:])], 1)
    out_ref[...] = total.astype(BF16).reshape(out_ref.shape)


def row_sum(refs):
    own, other, first_x, last_y, last_x, first_y = [ref[...].astype(F32) for ref in refs]
    return own + other + jnp.concatenate([first_x + last_y, last_x + first_y], 0)


def scaled_rows(rows):
    inv = lax.rsqrt(jnp.sum(rows * rows, 1, keepdims=True) * (1.0 / rows.shape[1]) + EPS)
    return rows * inv, inv


def norm_back(normed, inv, grad):
    return inv * (grad - normed * (jnp.sum(grad * normed, 1, keepdims=True) * (1.0 / grad.shape[1])))


def residual_kernel(refs, x_ref, gain_ref, sum_ref, a_ref):
    rows = x_ref[...].astype(F32) + row_sum(refs)
    sum_ref[...] = rows
    a_ref[...] = (scaled_rows(rows)[0] * gain_ref[...]).astype(BF16)


def output_rows_kernel(refs, sum_ref, out_ref):
    out_ref[...] = (sum_ref[...] + row_sum(refs)).astype(BF16)


def residual_back_kernel(refs, up_ref, sum_ref, gain_ref, grad_ref, low_ref):
    normed, inv = scaled_rows(sum_ref[...])
    grad = up_ref[...].astype(F32) + norm_back(normed, inv, row_sum(refs) * gain_ref[...])
    grad_ref[...] = grad
    low_ref[...] = grad.astype(BF16)


def input_back_kernel(refs, x_ref, grad_ref, out_ref):
    normed, inv = scaled_rows(x_ref[...].astype(F32))
    out_ref[...] = grad_ref[...] + norm_back(normed, inv, row_sum(refs))


def row_call(kernel, pieces, ins, kinds, deps=()):
    shape = pieces[0].shape
    outs = [jax.ShapeDtypeStruct(shape, kind) for kind in kinds]

    def wrapped(*refs):
        at = 6 + len(ins)
        kernel(refs[:6], *refs[6:at], *refs[at + len(deps) :])

    return pl.pallas_call(
        wrapped,
        in_specs=[pl.BlockSpec(memory_space=pltpu.VMEM)] * (6 + len(ins))
        + [pl.BlockSpec(memory_space=pl.ANY)] * len(deps),
        out_specs=[pl.BlockSpec(memory_space=pltpu.VMEM)] * len(outs),
        out_shape=outs,
        compiler_params=pltpu.CompilerParams(vmem_limit_bytes=24 * 1024 * 1024),
        cost_estimate=cost(20 * math.prod(shape), *pieces, *ins, *outs),
        name=kernel.__name__,
    )(*pieces, *ins, *deps)


def parts_call(a, w, kind, deps=(), mib=60):
    slots, per, k = a.shape
    if kind == "blocks":
        tile, depth = w.shape[2], w.shape[1]
        width = w.shape[0] * tile
        w_spec = pl.BlockSpec((1, depth, tile), lambda i: (i, 0, 0))
    elif kind == "nn":
        tile, depth, width = 512, k, w.shape[1]
        w_spec = pl.BlockSpec((k, tile), lambda i: (0, i))
    else:
        tile, depth, width = 512, k, w.shape[0]
        w_spec = pl.BlockSpec((tile, k), lambda i: (i, 0))

    def kernel(a_ref, w_ref, *refs):
        right = w_ref[0] if kind == "blocks" else w_ref[...]
        for slot, out_ref in enumerate(refs[-slots:]):
            left = a_ref[slot, :, :depth]
            out_ref[...] = (dot_t if kind == "nt" else dot)(left, right).astype(BF16)

    out = jax.ShapeDtypeStruct((per, width), BF16)
    return pl.pallas_call(
        kernel,
        grid=(width // tile,),
        in_specs=[pl.BlockSpec(a.shape, lambda i: (0, 0, 0)), w_spec]
        + [pl.BlockSpec(memory_space=pl.ANY)] * len(deps),
        out_specs=[pl.BlockSpec((per, tile), lambda i: (0, i))] * slots,
        out_shape=[out] * slots,
        compiler_params=params(mib),
        cost_estimate=cost(2 * slots * per * depth * width, a, w, *[out] * slots),
        name="parts_" + kind,
    )(a, w, *deps)


def ordered(ref, me, lanes=slice(None)):
    return jnp.concatenate([ref[p ^ me, 0, :, lanes] for p in range(8)], 0)


def put_ordered(ref, me, value, lanes=slice(None)):
    sub = value.shape[0] // 8
    for p in range(8):
        ref[p ^ me, 0, :, lanes] = value[p * sub : (p + 1) * sub]


def phi(aligned, feat, rows):
    both = dot(aligned, feat) + rows[0:1, :]
    a, b = both[:, :FPAD], both[:, FPAD:]
    return a, b, a * b * rows[1:2, :FPAD]


def phi_back(a, b, grad, feat, rows):
    scaled = grad * rows[1:2, :FPAD]
    return dot_t((scaled * b).astype(BF16), feat[:, :FPAD]) + dot_t(
        (scaled * a).astype(BF16), feat[:, FPAD:]
    )


def put_state(ref, head, state, norm):
    ref[0, head] = state[:FROWS].astype(BF16)
    high = norm.astype(BF16)
    low = (norm - high.astype(F32)).astype(BF16)
    ref[0, head, FEAT : FEAT + 1, :] = high[:, :128]
    ref[0, head, FEAT + 1 : FEAT + 2, :] = low[:, :128]
    ref[0, head, FEAT + 2 : FEAT + 3, :] = high[:, 128:]
    ref[0, head, FEAT + 3 : FEAT + 4, :] = low[:, 128:]


def get_state(ref, head):
    whole = ref[0, head]
    state = jnp.concatenate([whole, jnp.zeros((FPAD - FROWS, 128), F32)], 0)
    norm = jnp.concatenate(
        [
            whole[FEAT : FEAT + 1] + whole[FEAT + 1 : FEAT + 2],
            whole[FEAT + 2 : FEAT + 3] + whole[FEAT + 3 : FEAT + 4],
        ],
        1,
    )
    return state.astype(BF16), norm


def align4(qk, align_ref):
    out = dot(qk, align_ref[...]).astype(BF16)
    return [out[:, i * 128 : (i + 1) * 128] for i in range(4)]


def column(seg_ref):
    row = seg_ref[0]
    return jnp.transpose(jnp.broadcast_to(row, (128, row.shape[1])))[:, 0:1]


def mask_of(seg_ref, meta_ref, which):
    at = 1 + which * pl.num_programs(0) + pl.program_id(0)
    return jnp.where(column(seg_ref) == meta_ref[at].astype(F32), 1.0, 0.0)


def visible(seg_ref):
    t = seg_ref.shape[2]
    causal = lax.broadcasted_iota(jnp.int32, (t, t), 0) >= lax.broadcasted_iota(jnp.int32, (t, t), 1)
    return causal & (column(seg_ref) == seg_ref[0])


def state_kernel(me_ref, qkv_ref, seg_ref, feat_ref, rows_ref, align_ref, out_ref):
    me = me_ref[0]
    qk = ordered(qkv_ref, me, slice(256, 384))
    v = ordered(qkv_ref, me, slice(0, 256))
    last = mask_of(seg_ref, me_ref, 1)
    parts = align4(qk, align_ref)
    for head in range(2):
        _, _, feat = phi(parts[2 + head], feat_ref[...], rows_ref[...])
        feat = feat * last
        state = t_dot(feat.astype(BF16), v[:, head * 128 : (head + 1) * 128])
        put_state(out_ref, head, state, jnp.sum(feat, 0, keepdims=True))


def intra_kernel(me_ref, qkv_ref, seg_ref, align_ref, num_ref, den_ref):
    me = me_ref[0]
    qk = ordered(qkv_ref, me, slice(256, 384))
    v = ordered(qkv_ref, me, slice(0, 256))
    see = visible(seg_ref)
    parts = align4(qk, align_ref)
    den_ref[0] = jnp.zeros(den_ref.shape[1:], F32)
    for head in range(2):
        z = dot_t(parts[head], parts[2 + head])
        w = jnp.where(see, 1.0 + z * (0.25 + 0.03125 * z), 0.0)
        num_ref[0, :, head * 128 : (head + 1) * 128] = dot(
            w.astype(BF16), v[:, head * 128 : (head + 1) * 128]
        )
        den_ref[0, :, head : head + 1] = jnp.sum(w, 1, keepdims=True)


def output_kernel(
    me_ref, qkv_ref, seg_ref, feat_ref, rows_ref, align_ref, num_ref, den_ref, state_ref, o_ref, all_ref
):
    me = me_ref[0]
    qk = ordered(qkv_ref, me, slice(256, 384))
    use = mask_of(seg_ref, me_ref, 0)
    parts = align4(qk, align_ref)
    all_ref[0] = jnp.zeros(all_ref.shape[1:], F32)
    for head in range(2):
        lanes = slice(head * 128, (head + 1) * 128)
        _, _, feat = phi(parts[head], feat_ref[...], rows_ref[...])
        state, norm = get_state(state_ref, head)
        num = num_ref[0, :, lanes] + use * dot(feat.astype(BF16), state)
        den = den_ref[0, :, head : head + 1] + use * jnp.sum(feat * norm, 1, keepdims=True)
        all_ref[0, :, head : head + 1] = den
        put_ordered(o_ref, me, (num / den).astype(BF16), lanes)


def back_parts(me, o_ref, do_ref, den_ref, head):
    lanes = slice(head * 128, (head + 1) * 128)
    inv = 1.0 / den_ref[0, :, head : head + 1]
    do = ordered(do_ref, me, lanes).astype(F32)
    o = ordered(o_ref, me, lanes).astype(F32)
    return (do * inv).astype(BF16), -jnp.sum(do * o, 1, keepdims=True) * inv


def back_state_kernel(
    me_ref, qkv_ref, seg_ref, feat_ref, rows_ref, align_ref, o_ref, do_ref, den_ref, out_ref
):
    me = me_ref[0]
    qk = ordered(qkv_ref, me, slice(256, 384))
    use = mask_of(seg_ref, me_ref, 0)
    parts = align4(qk, align_ref)
    for head in range(2):
        g, c = back_parts(me, o_ref, do_ref, den_ref, head)
        _, _, feat = phi(parts[head], feat_ref[...], rows_ref[...])
        feat = feat * use
        put_state(out_ref, head, t_dot(feat.astype(BF16), g), jnp.sum(feat * c, 0, keepdims=True))


def back_intra_kernel(
    me_ref, qkv_ref, seg_ref, feat_ref, rows_ref, align_ref, o_ref, do_ref, den_ref, state_ref,
    dq_ref, dk_ref, dv_ref,
):
    me = me_ref[0]
    qk = ordered(qkv_ref, me, slice(256, 384))
    v = ordered(qkv_ref, me, slice(0, 256))
    use = mask_of(seg_ref, me_ref, 0)
    see = visible(seg_ref)
    parts = align4(qk, align_ref)
    for head in range(2):
        lanes = slice(head * 128, (head + 1) * 128)
        g, c = back_parts(me, o_ref, do_ref, den_ref, head)
        z = dot_t(parts[head], parts[2 + head])
        w = jnp.where(see, 1.0 + z * (0.25 + 0.03125 * z), 0.0)
        dv_ref[0, :, lanes] = t_dot(w.astype(BF16), g)
        dw = dot_t(g, v[:, lanes]) + c
        dz = jnp.where(see, dw * (0.25 + 0.0625 * z), 0.0).astype(BF16)
        a, b, _ = phi(parts[head], feat_ref[...], rows_ref[...])
        state, norm = get_state(state_ref, head)
        grad = use * (dot_t(g, state) + c * norm)
        dq_ref[0, :, lanes] = dot(dz, parts[2 + head]) + phi_back(a, b, grad, feat_ref[...], rows_ref[...])
        dk_ref[0, :, lanes] = t_dot(dz, parts[head])


def back_output_kernel(
    me_ref, qkv_ref, seg_ref, feat_ref, rows_ref, align_ref, state_ref, dq_ref, dk_ref, dv_ref, inv_ref, out_ref, scaled_ref
):
    me = me_ref[0]
    qk = ordered(qkv_ref, me, slice(256, 384))
    v = ordered(qkv_ref, me, slice(0, 256))
    last = mask_of(seg_ref, me_ref, 1)
    parts = align4(qk, align_ref)
    inv = ordered(inv_ref, me)
    packed = None
    for head in range(2):
        lanes = slice(head * 128, (head + 1) * 128)
        a, b, feat = phi(parts[2 + head], feat_ref[...], rows_ref[...])
        state, norm = get_state(state_ref, head)
        grad = last * (dot_t(v[:, lanes], state) + norm)
        dk = dk_ref[0, :, lanes] + phi_back(a, b, grad, feat_ref[...], rows_ref[...])
        dv = dv_ref[0, :, lanes] + last * dot(feat.astype(BF16), state)
        put_ordered(out_ref, me, dv.astype(BF16), lanes)
        put_ordered(scaled_ref, me, (dv * inv).astype(BF16), lanes)
        place = align_ref[...]
        term = dot_t(dq_ref[0, :, lanes].astype(BF16), place[:, head * 128 : (head + 1) * 128]) + dot_t(
            dk.astype(BF16), place[:, (2 + head) * 128 : (3 + head) * 128]
        )
        packed = term if packed is None else packed + term
    put_ordered(out_ref, me, packed.astype(BF16), slice(256, 384))
    put_ordered(scaled_ref, me, (packed * inv).astype(BF16), slice(256, 384))


def attention_call(kernel, me, ins, kinds, outs, flops, deps=()):
    def spec(a, kind):
        if kind == "s":
            return pl.BlockSpec((8, 1) + a.shape[2:], lambda i, m: (0, i, 0, 0))
        rest = len(a.shape) - 1
        if kind == "q":
            return pl.BlockSpec((1,) + a.shape[1:], lambda i, m: (i,) + (0,) * rest)
        return pl.BlockSpec(a.shape, lambda i, m: (0,) * (rest + 1))

    seqs = ins[0].shape[1]
    n = 1 + len(ins)

    def wrapped(*refs):
        kernel(*refs[:n], *refs[n + len(deps) :])

    return pl.pallas_call(
        wrapped,
        out_shape=[jax.ShapeDtypeStruct(a.shape, a.dtype) for a, _ in outs],
        grid_spec=pltpu.PrefetchScalarGridSpec(
            num_scalar_prefetch=1,
            grid=(seqs,),
            in_specs=[spec(a, k) for a, k in zip(ins, kinds)] + [pl.BlockSpec(memory_space=pl.ANY)] * len(deps),
            out_specs=[spec(a, k) for a, k in outs],
        ),
        compiler_params=params(28),
        cost_estimate=cost(flops, *ins, *[a for a, _ in outs]),
        name=kernel.__name__,
    )(me, *ins, *deps)


def pick(cond, a, b):
    return jnp.where(cond, a, b)


def half_columns(gate, up, which, n_main, n_mid):
    mid = slice(n_main, n_main + 2 * n_mid)
    main = slice(0, n_main) if which == 0 else slice(n_main + 2 * n_mid, None)
    part = slice(0, n_mid) if which == 0 else slice(n_mid, None)
    return jnp.concatenate([gate[:, main], up[:, main], gate[:, mid][:, part], up[:, mid][:, part]], 1)


def body(inputs, segments, qw, kw, vw, pw, again, gw, uw, dw, fgain, upstream):
    hi, core, row, col = (lax.axis_index(a) for a in ("hi", "core", "row", "col"))
    rows = lax.axis_size("row")
    shards = 2 * rows
    seqs, sub = inputs.shape[0], inputs.shape[3]
    tokens = seqs * sub
    span = 8 * sub
    n_rows = qw.shape[0]
    is0 = col == 0
    ff = gw.shape[1]
    half_ff = ff // 2
    n_mid = 64
    n_main = half_ff - n_mid
    feat_c, rows_c, align_c = feature_constants()
    sds = jax.ShapeDtypeStruct
    x = inputs.reshape(tokens, D)

    shard_pairs = [(s, (s % rows) * 2 + s // rows) for s in range(shards)]
    moved = lax.ppermute(pw, ("row", "col"), shard_pairs)

    gain_one = again.astype(F32)[:, None]
    seg_own = segments.reshape(seqs, 4 * sub)

    def by_dest(w, scale):
        return (w.astype(F32) * scale).astype(BF16).reshape(n_rows, 8, -1)

    lane = lax.broadcasted_iota(jnp.int32, (n_rows, PAYLOAD - 320), 1)
    ends = jnp.pad(seg_own[:, -1], (0, n_rows - seqs)).astype(F32)[:, None]
    tens = jnp.floor(ends * (1.0 / 128.0))
    extra = jnp.where(
        lane == 0,
        fgain.astype(F32)[:, None],
        jnp.where(lane == 1, tens, jnp.where(lane == 2, ends - 128.0 * tens, 0.0)),
    ).astype(BF16)
    payload = jnp.concatenate(
        [
            by_dest(vw, gain_one),
            by_dest(qw, gain_one),
            by_dest(kw, gain_one),
            jnp.broadcast_to(extra[:, None], (n_rows, 8, PAYLOAD - 320)),
        ],
        2,
    ).transpose(1, 0, 2)
    payload = lax.all_to_all(payload, GROUP, split_axis=0, concat_axis=0, tiled=True)
    x_own = after(x, payload)
    xs = gather8(x_own)
    w_proj = lax.all_gather(moved, "row", axis=0, tiled=True)
    gathered = lax.all_gather(after(payload, moved), "row", axis=0, tiled=False)
    lasts = gathered[:, 1, :seqs, 321:323].astype(F32)
    lasts = (lasts[:, :, 0] * 128.0 + lasts[:, :, 1]).astype(jnp.int32)

    seg_other = swap(seg_own, "col")
    seg = jnp.concatenate([pick(is0, seg_own, seg_other), pick(is0, seg_other, seg_own)], 1)
    seg_row = seg.astype(F32)[:, None, :]
    before = jnp.where(row > 0, lasts[jnp.maximum(row - 1, 0)], -1)
    here = lasts[row]
    me3 = (4 * col + 2 * hi + core).astype(jnp.int32)
    meta = jnp.concatenate([me3[None], before, here])

    ends = jnp.concatenate([lasts, jnp.full((1, seqs), -1, jnp.int32)])

    def end_of(r):
        return ends[jnp.where((r >= 0) & (r < rows), r, rows)]

    def same(r, other):
        return ((end_of(r) == other) & (r >= 0) & (r < rows)).astype(F32)

    every = 8 * tokens
    qkv, inv, w_qkv = slot_call(
        qkv_kernel, xs, [(gathered.reshape(rows, 4, 2 * n_rows, PAYLOAD), False)],
        [sds((8, tokens, PAYLOAD), BF16), sds((8, tokens, 128), F32)], 2 * every * D * PAYLOAD,
        deps=[seg_row], whole=[sds((D, PAYLOAD), BF16)],
    )
    gain_two = w_qkv[:, 320].astype(F32)[None, :]
    inv = inv.reshape(8, seqs, sub, 128)
    ups = gather8(after(upstream.reshape(tokens, D), qkv))
    qkv = qkv.reshape(8, seqs, sub, PAYLOAD)
    st = sds((seqs, 2, FROWS, 128), BF16)
    near = 4 * seqs * span * span * 160
    far = 4 * seqs * span * FPAD * 300
    (state,) = attention_call(
        state_kernel, meta, [qkv, seg_row, feat_c, rows_c, align_c], "sqccc", [(st, "q")], far
    )
    mine = pick(is0, half_columns(gw, uw, 0, n_main, n_mid), half_columns(gw, uw, 1, n_main, n_mid))
    theirs = pick(is0, half_columns(gw, uw, 1, n_main, n_mid), half_columns(gw, uw, 0, n_main, n_mid))
    got = swap(after(theirs, xs[6][0], xs[7][0]), "col")
    got = after(got, state)
    gu_rows = jnp.concatenate([pick(is0, mine, got), pick(is0, got, mine)], 0)
    w_gu = lax.all_gather(gu_rows, "row", axis=0, tiled=True)
    down0 = dw[: n_main + n_mid]
    down1 = jnp.concatenate([dw[n_main + 2 * n_mid :], dw[n_main + n_mid : n_main + 2 * n_mid]], 0)
    d_mine, d_theirs = pick(is0, down0, down1), pick(is0, down1, down0)
    d_got = swap(after(d_theirs, got), "col")
    d_cols = jnp.stack([pick(is0, d_mine, d_got), pick(is0, d_got, d_mine)])
    w_down = lax.all_gather(d_cols, "row", axis=0, tiled=True)
    fold = shards // 8
    w_down = (
        w_down.reshape(8, fold, half_ff, D // shards).transpose(0, 2, 1, 3).reshape(8, half_ff, D // 8)
    )

    num, den_in = attention_call(
        intra_kernel, meta, [qkv, seg_row, align_c], "sqc",
        [(sds((seqs, span, 256), F32), "q"), (sds((seqs, span, 8), F32), "q")], near,
    )
    forth = walk_steps(state, lambda d: same(row - d, here), lambda d: same(row - d, before), True)
    next(forth)
    state_in = finish(forth, [num])
    o, den = attention_call(
        output_kernel, meta, [qkv, seg_row, feat_c, rows_c, align_c, num, den_in, state_in], "sqcccqqq",
        [(sds((8, seqs, sub, 256), BF16), "s"), (sds((seqs, span, 8), F32), "q")], far,
        [ups[6][0], ups[7][0], d_got],
    )
    o_rows = o.reshape(8, tokens, 256)
    residual, a2_own = row_call(
        residual_kernel, scatter8(parts_call(o_rows, w_proj, "nn", mib=28)), [x, gain_two], [F32, BF16]
    )

    a2 = gather8(a2_own)
    ff_flops = 2 * every * D * half_ff
    gu, h, h_turned = slot_call(
        ffn_in_kernel, a2, [(w_gu, False)],
        [
            sds((8, tokens, ff), BF16),
            sds((8, tokens, half_ff + n_mid), BF16),
            sds((8, half_ff + n_mid, tokens), BF16),
        ],
        2 * ff_flops,
    )
    (down_g,) = grad_call(
        down_grad_kernel, ups, 256, [h_turned], [],
        [(sds((8, half_ff, 256), BF16), (1, half_ff, 256), lambda i: (i, 0, 0))], ff_flops,
    )
    (dgu,) = slot_call(
        ffn_back_kernel, ups, [(w_down, False), (gu, True)], [sds((8, tokens, ff), BF16)], ff_flops, [down_g],
    )
    down_g = (
        down_g.reshape(8, half_ff, fold, D // shards).transpose(0, 2, 1, 3).reshape(shards * half_ff, -1)
    )
    down_g = lax.psum_scatter(down_g, "row", scatter_dimension=0, tiled=True)
    block = D // shards
    gu_gs, gains = [], []

    def gu_half(x_bit):
        def run(sent):
            one, gain = grad_call(
                gu_grad_kernel, a2, 256, [dgu], [(w_gu, (256, ff), lambda i: (2 * i + x_bit, 0))],
                [
                    (sds((D // 2, ff), BF16), (256, ff), lambda i: (i, 0)),
                    (sds((D // 2, 128), F32), (256, 128), lambda i: (i, 0)),
                ],
                ff_flops, lambda i: 2 * i + x_bit, 4, sent,
            )
            gu_gs.append(one)
            gains.append(gain)
            return [one]

        return run

    grad_r, datt_own = row_call(
        residual_back_kernel, scatter8(parts_call(dgu, w_gu, "nt"), gu_half(0), gu_half(1)),
        [upstream.reshape(tokens, D), residual, gain_two], [F32, BF16],
    )
    gain_part = jnp.stack([g.reshape(4, 256, 128) for g in gains], 1).reshape(D, 128)
    if fold > 1:
        natural = jnp.stack([g.reshape(4, 256, ff) for g in gu_gs], 1)
        by_col = natural.reshape(rows, 2, block, ff).transpose(1, 0, 2, 3)
        gu_gs = [by_col[0].reshape(D // 2, ff), by_col[1].reshape(D // 2, ff)]
    gu_r = [lax.psum_scatter(g, "row", scatter_dimension=0, tiled=True) for g in gu_gs]

    late = {}

    def down_side(own):
        late["out"] = parts_call(h, w_down, "blocks", [own])
        return late["out"][0]

    datt = gather8(datt_own, down_side)
    (do,) = slot_call(
        do_kernel, datt, [(w_proj, False)], [sds((8, tokens, 256), BF16)], 2 * every * D * 256,
        [down_g, late["out"][0]],
    )
    do = do.reshape(8, seqs, sub, 256)

    (dstate,) = attention_call(
        back_state_kernel, meta, [qkv, seg_row, feat_c, rows_c, align_c, o, do, den], "sqcccssq",
        [(st, "q")], far,
    )
    part = sds((seqs, span, 256), F32)

    back = walk_steps(
        dstate,
        lambda d: same(row + d - 1, before) * (row + d < rows),
        lambda d: same(row + d - 1, here) * (row + d < rows),
        False,
    )
    _, came = next(back)
    down_steps = scatter_steps(late["out"])
    dq, dk, dv = attention_call(
        back_intra_kernel, meta, [qkv, seg_row, feat_c, rows_c, align_c, o, do, den, state_in],
        "sqcccssqq", [(part, "q")] * 3, 3 * near + far, next(down_steps),
    )
    sent = down_steps.send([dq, came])
    now, _ = back.send([dq])
    (proj_g,) = grad_call(
        proj_grad_kernel, datt, 1024, [o_rows], [],
        [(sds((256, D), BF16), (256, 1024), lambda i: (0, i))], 2 * every * D * 256, deps=[*sent, now, gu_r[0]],
    )
    (outputs,) = row_call(output_rows_kernel, finish(down_steps, [proj_g]), [residual], [BF16])
    dstate_out = finish(back, [proj_g])
    proj_r = lax.psum_scatter(proj_g, "row", scatter_dimension=0, tiled=True)
    project_grad = lax.ppermute(proj_r, ("row", "col"), [(b, a) for a, b in shard_pairs]).astype(F32)
    row_out = sds((8, seqs, sub, PAYLOAD), BF16)
    dqkv, scaled = attention_call(
        back_output_kernel, meta, [qkv, seg_row, feat_c, rows_c, align_c, dstate_out, dq, dk, dv, inv],
        "sqcccqqqqs", [(row_out, "s")] * 2, 2 * far, [outputs, gu_r[1]],
    )
    down_g = down_g.reshape(2, half_ff, D // shards)
    d_keep, d_send = pick(is0, down_g[0], down_g[1]), pick(is0, down_g[1], down_g[0])
    d_got = swap(d_send, "col")
    d0, d1 = pick(is0, d_keep, d_got).astype(F32), pick(is0, d_got, d_keep).astype(F32)
    down_grad = jnp.concatenate([d0, d1[n_main:], d1[:n_main]], 0)
    g_keep = pick(is0, gu_r[0], gu_r[1])
    g_got = swap(pick(is0, gu_r[1], gu_r[0]), "col")
    g0, g1 = pick(is0, g_keep, g_got).astype(F32), pick(is0, g_got, g_keep).astype(F32)
    m = 2 * n_main
    gate_grad = jnp.concatenate(
        [g0[:, :n_main], g0[:, m : m + n_mid], g1[:, m : m + n_mid], g1[:, :n_main]], 1
    )
    up_grad = jnp.concatenate(
        [g0[:, n_main:m], g0[:, m + n_mid :], g1[:, m + n_mid :], g1[:, n_main:m]], 1
    )

    def qkv_side(sent):
        (late["qkv"],) = grad_call(
            qkv_grad_kernel, xs, 512, [scaled.reshape(8, tokens, PAYLOAD)],
            [(gain_part, (512, 128), lambda i: (i, 0))],
            [
                (
                    sds((rows, 4, 2 * n_rows, PAYLOAD), BF16),
                    (rows, 1, 2 * n_rows, PAYLOAD),
                    lambda i: (0, i, 0, 0),
                )
            ],
            2 * every * D * PAYLOAD, deps=sent,
        )
        return [late["qkv"]]

    f_parts = parts_call(dqkv.reshape(8, tokens, PAYLOAD), w_qkv, "nt", [gate_grad, up_grad, down_grad], 28)
    f_pieces = scatter8(f_parts, qkv_side)
    qkv_g = late["qkv"]
    (inputs_grad,) = row_call(input_back_kernel, f_pieces, [x, grad_r], [F32])
    qkv_g = lax.psum_scatter(qkv_g.reshape(D, PAYLOAD), "row", scatter_dimension=0, tiled=True)
    qkv_g = lax.all_to_all(
        qkv_g.reshape(8, n_rows, PAYLOAD), GROUP, split_axis=0, concat_axis=0, tiled=True
    ).astype(F32)
    per_row = qkv_g.transpose(1, 0, 2)
    v_g = per_row[:, :, :256].reshape(n_rows, -1)
    q_g = per_row[:, :, 256:288].reshape(n_rows, -1)
    k_g = per_row[:, :, 288:320].reshape(n_rows, -1)
    forward_grad = jnp.sum(per_row[:, :, 320], 1) / fgain.astype(F32)
    attend_grad = (
        jnp.sum(v_g * vw.astype(F32), 1) + jnp.sum(q_g * qw.astype(F32), 1) + jnp.sum(k_g * kw.astype(F32), 1)
    )

    return (
        outputs.reshape(inputs.shape),
        inputs_grad.reshape(inputs.shape),
        q_g * gain_one,
        k_g * gain_one,
        v_g * gain_one,
        project_grad,
        attend_grad,
        gate_grad,
        up_grad,
        down_grad,
        forward_grad,
    )


def solution(mesh):
    heads, shards = mesh.devices.shape
    fine = Mesh(mesh.devices.reshape(heads // 2, 2, shards // 2, 2), ("hi", "core", "row", "col"))
    h, s = ("hi", "core"), ("row", "col")
    every = P(h + s)
    tokens = P(None, s, h)
    return jax.shard_map(
        body,
        mesh=fine,
        in_specs=(
            tokens, P(None, s), every, every, every, every, every, P(s, h), P(s, h), P(h, s), every, tokens,
        ),
        out_specs=(
            tokens, tokens, every, every, every, every, every, P(s, h), P(s, h), P(h, s), every,
        ),
        check_vma=False,
    )
```

```python
import math

import numpy as np

import jax
import jax.numpy as jnp
from jax import lax
from jax.experimental import pallas as pl
from jax.experimental.pallas import tpu as pltpu
from jax.sharding import Mesh
from jax.sharding import PartitionSpec as P

D = 2048
HEADS = 16
QK = 16
VD = 128
EPS = 1e-05
F32 = jnp.float32
BF16 = jnp.bfloat16
GROUP = ("hi", "core", "col")
FEAT = 1 + QK + QK * (QK + 1) // 2
FPAD = 256
FROWS = 160
PAYLOAD = 384


def feature_constants():
    left = np.zeros((128, FPAD), np.float32)
    right = np.zeros((128, FPAD), np.float32)
    rows = np.zeros((8, 2 * FPAD), np.float32)
    at = 0
    for i in range(QK):
        for j in range(i, QK):
            left[i, at] = 1.0
            right[j, at] = 1.0
            rows[1, at] = (1.0 if i == j else math.sqrt(2.0)) / math.sqrt(2.0 * QK)
            at += 1
    for i in range(QK):
        left[i, at] = 1.0
        rows[0, FPAD + at] = 1.0
        rows[1, at] = QK ** (-0.25)
        at += 1
    rows[0, at] = 1.0
    rows[0, FPAD + at] = 1.0
    rows[1, at] = 1.0
    align = np.zeros((4, 128, 128), np.float32)
    for part in range(4):
        for i in range(QK):
            align[part, part * QK + i, i] = 1.0
    return (
        jnp.asarray(np.concatenate([left, right], 1), BF16),
        jnp.asarray(rows, F32),
        jnp.asarray(align.transpose(1, 0, 2).reshape(128, 512), BF16),
    )


def dot(a, b):
    return jnp.dot(a, b, preferred_element_type=F32)


def dot_t(a, b):
    return lax.dot_general(a, b, (((1,), (1,)), ((), ())), preferred_element_type=F32)


def t_dot(a, b):
    return lax.dot_general(a, b, (((0,), (0,)), ((), ())), preferred_element_type=F32)


def swap(value, axis):
    return lax.ppermute(value, axis, [(0, 1), (1, 0)])


def after(value, *others):
    if not others:
        return value

    def gate(*refs):
        pass

    return pl.pallas_call(
        gate,
        in_specs=[pl.BlockSpec(memory_space=pl.ANY)] * (1 + len(others)),
        out_specs=pl.BlockSpec(memory_space=pl.ANY),
        out_shape=jax.ShapeDtypeStruct(value.shape, value.dtype),
        input_output_aliases={0: 0},
        cost_estimate=pl.CostEstimate(flops=0, transcendentals=0, bytes_accessed=0),
        name="gate",
    )(value, *others)


def meet(*values):
    def gate(*refs):
        pass

    return pl.pallas_call(
        gate,
        in_specs=[pl.BlockSpec(memory_space=pl.ANY)] * len(values),
        out_specs=[pl.BlockSpec(memory_space=pl.ANY)] * len(values),
        out_shape=[jax.ShapeDtypeStruct(v.shape, v.dtype) for v in values],
        input_output_aliases={i: i for i in range(len(values))},
        cost_estimate=pl.CostEstimate(flops=0, transcendentals=0, bytes_accessed=0),
        name="meet",
    )(*values)


def gather_steps(own):
    half = own.shape[0] // 2
    over_x = swap(own, "col")
    over_y = swap(own, "hi")
    rows = [(own, 0, 0), (swap(own, "core"), 1, 0)]
    done = yield rows
    over_x, over_y = after(over_x, *done), after(over_y, *done)
    top = swap(over_y[:half], "col")
    low = swap(over_x[half:], "hi")
    near = [(over_y, 2, 0), (swap(over_y, "core"), 3, 0), (over_x, 4, 0), (swap(over_x, "core"), 5, 0)]
    done = yield near
    top, low = after(top, *done), after(low, *done)
    far = [(top, 6, 0), (low, 6, half), (swap(top, "core"), 7, 0), (swap(low, "core"), 7, half)]
    return rows + near + far


def gather8(own):
    steps = gather_steps(own)
    next(steps)
    return finish(steps)


def scatter_steps(parts):
    def both(one, two, start, end):
        return one[start:end].astype(F32) + two[start:end].astype(F32)

    own, other, y, yc, x, xc, xy, xyc = parts
    n = xy.shape[0]
    half = n // 2
    xyc = swap(xyc, "core")
    xc = swap(xc, "core")
    yc = swap(yc, "core")
    other = swap(other, "core")
    to_x = both(xy, xyc, 0, half).astype(BF16)
    to_y = both(xy, xyc, half, n).astype(BF16)
    near_x = both(x, xc, 0, half).astype(BF16)
    near_y = both(y, yc, half, n).astype(BF16)
    from_x, from_y = swap(to_x, "col"), swap(to_y, "hi")
    first_x, first_y = swap(near_x, "col"), swap(near_y, "hi")
    done = yield [to_x, to_y, near_x, near_y]
    from_x, from_y = after(from_x, *done), after(from_y, *done)
    far_x = (both(x, xc, half, n) + from_y.astype(F32)).astype(BF16)
    far_y = (both(y, yc, 0, half) + from_x.astype(F32)).astype(BF16)
    last_x, last_y = swap(far_x, "col"), swap(far_y, "hi")
    done = yield [far_x, far_y]
    last_x, last_y = after(last_x, *done), after(last_y, *done)
    return own, other, first_x, last_y, last_x, first_y


def walk_steps(value, linked, joined, up):
    rows = lax.axis_size("row")
    total = None
    now = value
    step = 1
    while step < rows:
        pairs = [(i, i + step) if up else (i + step, i) for i in range(rows - step)]
        came = lax.ppermute(now, "row", pairs)
        wide = (yield now, came).astype(F32)
        term = joined(step)[:, None, None, None] * wide
        total = term if total is None else total + term
        if 2 * step < rows:
            now = (now.astype(F32) + linked(step)[:, None, None, None] * wide).astype(BF16)
        step = 2 * step
    return total


def finish(steps, done=()):
    try:
        step = steps.send(done)
        while True:
            step = steps.send(step[1] if isinstance(step, tuple) else ())
    except StopIteration as end:
        return end.value


def pair_sum(one, two, start, end):
    return one[start:end].astype(F32) + two[start:end].astype(F32)


def scatter8(parts, *kernels):
    steps = scatter_steps(parts)
    sent = next(steps)
    for i, kernel in enumerate(kernels):
        done = kernel(sent)
        if i == 1:
            return finish(steps, done)
        sent = steps.send(done)
    return finish(steps)


def far_in(values):
    return [pltpu.with_memory_space_constraint(v, pltpu.HBM) if math.prod(v.shape) >= 65536 else v for v in values]


def far_out(shapes):
    return list(shapes)
    return [pltpu.HBM(a.shape, a.dtype) if math.prod(a.shape) >= 65536 else a for a in shapes]


def params(mib=60):
    return pltpu.CompilerParams(dimension_semantics=("arbitrary",), vmem_limit_bytes=mib * 1024 * 1024)


def cost(flops, *arrays):
    return pl.CostEstimate(
        flops=int(flops),
        transcendentals=0,
        bytes_accessed=int(sum(math.prod(a.shape) * a.dtype.itemsize for a in arrays)),
    )


def slot_call(kernel, pieces, ins, outs, flops, deps=(), whole=(), slots=(0, 8), into=(), mib=60):
    first, count = slots[0], slots[1] - slots[0]
    pieces = [p for p in pieces if slots[0] <= p[1] < slots[1]]
    n = len(pieces)
    per, width = outs[0].shape[1], pieces[0][0].shape[1]
    extra = list(deps) + list(into)

    def wrapped(*refs):
        rows = refs[:n]
        at = n + len(ins)
        rest = refs[n:at] + refs[at + len(extra) : at + len(extra) + len(outs) + len(whole)]
        buf, sem = refs[-2:]
        i = pl.program_id(0)

        @pl.when(i == 0)
        def _():
            for (a, slot, start), ref in zip(pieces, rows):
                there = buf.at[slot - first, pl.ds(start, a.shape[0])]
                pltpu.make_async_copy(ref, there, sem.at[slot - first]).start()

        pltpu.make_async_copy(buf.at[i], buf.at[i], sem.at[i]).wait()
        kernel(buf.at[i], *rest)

    def spec(a, by_slot):
        rest = len(a.shape) - 1
        if by_slot:
            return pl.BlockSpec((None,) + a.shape[1:], lambda i: (i + first,) + (0,) * rest)
        return pl.BlockSpec(a.shape, lambda i: (0,) * (rest + 1))

    at = n + len(ins) + len(deps)
    return pl.pallas_call(
        wrapped,
        grid=(count,),
        in_specs=[pl.BlockSpec(memory_space=pltpu.HBM)] * n
        + [spec(a, k) for a, k in ins]
        + [pl.BlockSpec(memory_space=pl.ANY)] * len(extra),
        out_specs=[spec(a, True) for a in outs] + [spec(a, False) for a in whole],
        out_shape=far_out(list(outs) + list(whole)),
        scratch_shapes=[pltpu.VMEM((count, per, width), BF16), pltpu.SemaphoreType.DMA((count,))],
        input_output_aliases={at + i: i for i in range(len(into))},
        compiler_params=params(mib),
        cost_estimate=cost(
            flops * count // 8, *[a for a, _, _ in pieces], *[a for a, k in ins if not k], *outs[:count // 4], *whole
        ),
        name=kernel.__name__,
    )(*[a for a, _, _ in pieces], *far_in([a for a, _ in ins]), *extra)


def grad_call(kernel, pieces, tile, whole, ins, outs, flops, index=lambda i: i, steps=None, deps=(), mib=60):
    n = len(pieces)
    width = pieces[0][0].shape[1]
    places = [(slot, start, a.shape[0]) for a, slot, start in pieces]

    def wrapped(*refs):
        at = n + len(whole) + len(ins)
        kernel(list(zip(refs[:n], places)), *refs[n:at], *refs[at + len(deps) :])

    def fixed(a):
        rest = len(a.shape)
        return pl.BlockSpec(a.shape, lambda i: (0,) * rest)

    return pl.pallas_call(
        wrapped,
        grid=(steps or width // tile,),
        in_specs=[pl.BlockSpec((a.shape[0], tile), lambda i: (0, index(i))) for a, _, _ in pieces]
        + [fixed(a) for a in whole]
        + [pl.BlockSpec(block, where) for _, block, where in ins]
        + [pl.BlockSpec(memory_space=pl.ANY)] * len(deps),
        out_specs=[pl.BlockSpec(block, where) for _, block, where in outs],
        out_shape=far_out([a for a, _, _ in outs]),
        compiler_params=params(mib),
        cost_estimate=cost(
            flops, *[a for a, _, _ in pieces], *whole, *[a for a, _, _ in ins], *[a for a, _, _ in outs]
        ),
        name=kernel.__name__,
    )(*far_in([*[a for a, _, _ in pieces], *whole, *[a for a, _, _ in ins]]), *deps)


def summed(rows, right):
    total = None
    for ref, (slot, start, n) in rows:
        term = t_dot(ref[...], right[slot, start : start + n, :])
        total = term if total is None else total + term
    return total


def qkv_kernel(x_ref, given_ref, qkv_ref, inv_ref, w_ref):
    @pl.when(pl.program_id(0) == 0)
    def _():
        rows, groups, n, _ = given_ref.shape
        for g in range(groups):
            for r in range(rows):
                w_ref[pl.ds((g * rows + r) * n, n), :] = given_ref[r, g]

    x = x_ref[...]
    wide = x.astype(F32)
    inv = lax.rsqrt(jnp.sum(wide * wide, 1, keepdims=True) * (1.0 / x.shape[1]) + EPS)
    qkv_ref[...] = (dot(x, w_ref[...]) * inv).astype(BF16)
    inv_ref[...] = jnp.broadcast_to(inv, inv_ref.shape)


def ffn_in_kernel(a_ref, w_ref, gu_ref, h_ref, turned_ref):
    gu = dot(a_ref[...], w_ref[...])
    gu_ref[...] = gu.astype(BF16)
    m = (gu.shape[1] - 128) // 2
    g, u = gu[:, :m], gu[:, m : 2 * m]
    h_ref[:, :m] = (g * jax.nn.sigmoid(g) * u).astype(BF16)
    g = gu[:, 2 * m :]
    u = pltpu.roll(g, 64, 1)
    first = lax.broadcasted_iota(jnp.int32, g.shape, 1) < 64
    h_ref[:, m:] = jnp.where(first, g * jax.nn.sigmoid(g) * u, 0.0).astype(BF16)
    turned_ref[...] = jnp.transpose(h_ref[...])


def ffn_back_kernel(up_ref, w_ref, gu_ref, out_ref):
    up = up_ref[...]
    total = None
    for i in range(8):
        term = dot_t(up[:, i * 256 : (i + 1) * 256], w_ref[i])
        total = term if total is None else total + term
    m = total.shape[1] - 64

    def both(g, u, dh):
        s = jax.nn.sigmoid(g)
        return dh * u * (s * (1.0 + g * (1.0 - s))), dh * (g * s)

    gu = gu_ref[...].astype(F32)
    dg, du = both(gu[:, :m], gu[:, m : 2 * m], total[:, :m])
    out_ref[:, :m] = dg.astype(BF16)
    out_ref[:, m : 2 * m] = du.astype(BF16)
    mid = gu[:, 2 * m :]
    other = pltpu.roll(mid, 64, 1)
    first = lax.broadcasted_iota(jnp.int32, mid.shape, 1) < 64
    dh = jnp.concatenate([total[:, m:], total[:, m:]], 1)
    dg, du = both(jnp.where(first, mid, other), jnp.where(first, other, mid), dh)
    out_ref[:, 2 * m :] = jnp.where(first, dg, du).astype(BF16)


def down_grad_kernel(rows, h_ref, out_ref):
    total = None
    for ref, (slot, start, n) in rows:
        term = dot(h_ref[slot, : out_ref.shape[1], start : start + n], ref[...])
        total = term if total is None else total + term
    out_ref[0] = total.astype(BF16)


def gu_grad_kernel(rows, right_ref, w_ref, out_ref, gain_ref):
    total = summed(rows, right_ref)
    out_ref[...] = total.astype(BF16)
    gain_ref[...] = jnp.broadcast_to(
        jnp.sum(total * w_ref[...].astype(F32), 1, keepdims=True), gain_ref.shape
    )


def do_kernel(d_ref, w_ref, out_ref):
    out_ref[...] = dot_t(d_ref[...], w_ref[...]).astype(BF16)


def proj_grad_kernel(rows, o_ref, out_ref):
    total = None
    for ref, (slot, start, n) in rows:
        term = t_dot(o_ref[slot, start : start + n, :], ref[...])
        total = term if total is None else total + term
    out_ref[...] = total.astype(BF16)


def qkv_grad_kernel(rows, right_ref, gain_ref, out_ref):
    total = summed(rows, right_ref)
    lane = lax.broadcasted_iota(jnp.int32, (1, 128), 1)
    total = jnp.concatenate([total[:, :256], jnp.where(lane == 64, gain_ref[...], total[:, 256:])], 1)
    out_ref[...] = total.astype(BF16).reshape(out_ref.shape)


def row_sum(refs):
    own, other, first_x, last_y, last_x, first_y = [ref[...].astype(F32) for ref in refs]
    return own + other + jnp.concatenate([first_x + last_y, last_x + first_y], 0)


def scaled_rows(rows):
    inv = lax.rsqrt(jnp.sum(rows * rows, 1, keepdims=True) * (1.0 / rows.shape[1]) + EPS)
    return rows * inv, inv


def norm_back(normed, inv, grad):
    return inv * (grad - normed * (jnp.sum(grad * normed, 1, keepdims=True) * (1.0 / grad.shape[1])))


def residual_kernel(refs, x_ref, gain_ref, sum_ref, a_ref):
    rows = x_ref[...].astype(F32) + row_sum(refs)
    sum_ref[...] = rows
    a_ref[...] = (scaled_rows(rows)[0] * gain_ref[...]).astype(BF16)


def output_rows_kernel(refs, sum_ref, out_ref):
    out_ref[...] = (sum_ref[...] + row_sum(refs)).astype(BF16)


def residual_back_kernel(refs, up_ref, sum_ref, gain_ref, grad_ref, low_ref):
    normed, inv = scaled_rows(sum_ref[...])
    grad = up_ref[...].astype(F32) + norm_back(normed, inv, row_sum(refs) * gain_ref[...])
    grad_ref[...] = grad
    low_ref[...] = grad.astype(BF16)


def input_back_kernel(refs, x_ref, grad_ref, out_ref):
    normed, inv = scaled_rows(x_ref[...].astype(F32))
    out_ref[...] = grad_ref[...] + norm_back(normed, inv, row_sum(refs))


def row_call(kernel, pieces, ins, kinds, deps=()):
    shape = pieces[0].shape
    outs = [jax.ShapeDtypeStruct(shape, kind) for kind in kinds]

    def wrapped(*refs):
        at = 6 + len(ins)
        kernel(refs[:6], *refs[6:at], *refs[at + len(deps) :])

    return pl.pallas_call(
        wrapped,
        in_specs=[pl.BlockSpec(memory_space=pltpu.VMEM)] * (6 + len(ins))
        + [pl.BlockSpec(memory_space=pl.ANY)] * len(deps),
        out_specs=[pl.BlockSpec(memory_space=pltpu.VMEM)] * len(outs),
        out_shape=outs,
        compiler_params=pltpu.CompilerParams(vmem_limit_bytes=24 * 1024 * 1024),
        cost_estimate=cost(20 * math.prod(shape), *pieces, *ins, *outs),
        name=kernel.__name__,
    )(*pieces, *ins, *deps)


def parts_call(a, w, kind, deps=(), mib=60, pairs=(0, 1, 2, 3)):
    _, per, k = a.shape
    n, slots = len(pairs), 2 * len(pairs)
    if kind == "blocks":
        tile, depth = w.shape[2], w.shape[1]
        width = w.shape[0] * tile
        w_spec = pl.BlockSpec((1, depth, tile), lambda i: (i, 0, 0))
    elif kind == "nn":
        tile, depth, width = 512, k, w.shape[1]
        w_spec = pl.BlockSpec((k, tile), lambda i: (0, i))
    else:
        tile, depth, width = 512, k, w.shape[0]
        w_spec = pl.BlockSpec((tile, k), lambda i: (i, 0))

    def kernel(*refs):
        w_ref = refs[n]
        right = w_ref[0] if kind == "blocks" else w_ref[...]
        for slot, out_ref in enumerate(refs[-slots:]):
            left = refs[slot // 2][slot % 2, :, :depth]
            out_ref[...] = (dot_t if kind == "nt" else dot)(left, right).astype(BF16)

    out = jax.ShapeDtypeStruct((per, width), BF16)
    return pl.pallas_call(
        kernel,
        grid=(width // tile,),
        in_specs=[pl.BlockSpec((2, per, k), lambda i, p=p: (p, 0, 0)) for p in pairs]
        + [w_spec]
        + [pl.BlockSpec(memory_space=pl.ANY)] * len(deps),
        out_specs=[pl.BlockSpec((per, tile), lambda i: (0, i))] * slots,
        out_shape=far_out([out] * slots),
        compiler_params=params(mib),
        cost_estimate=cost(2 * slots * per * depth * width, w, *[out] * slots),
        name="parts_" + kind,
    )(*far_in([*[a] * n, w]), *deps)


def ordered(ref, me, lanes=slice(None)):
    return jnp.concatenate([ref[p ^ me, 0, :, lanes] for p in range(8)], 0)


def put_ordered(ref, me, value, lanes=slice(None)):
    sub = value.shape[0] // 8
    for p in range(8):
        ref[p ^ me, 0, :, lanes] = value[p * sub : (p + 1) * sub]


def phi(aligned, feat, rows):
    both = dot(aligned, feat) + rows[0:1, :]
    a, b = both[:, :FPAD], both[:, FPAD:]
    return a, b, a * b * rows[1:2, :FPAD]


def phi_back(a, b, grad, feat, rows):
    scaled = grad * rows[1:2, :FPAD]
    return dot_t((scaled * b).astype(BF16), feat[:, :FPAD]) + dot_t(
        (scaled * a).astype(BF16), feat[:, FPAD:]
    )


def put_state(ref, head, state, norm):
    ref[0, head] = state[:FROWS].astype(BF16)
    high = norm.astype(BF16)
    low = (norm - high.astype(F32)).astype(BF16)
    ref[0, head, FEAT : FEAT + 1, :] = high[:, :128]
    ref[0, head, FEAT + 1 : FEAT + 2, :] = low[:, :128]
    ref[0, head, FEAT + 2 : FEAT + 3, :] = high[:, 128:]
    ref[0, head, FEAT + 3 : FEAT + 4, :] = low[:, 128:]


def get_state(ref, head):
    whole = ref[0, head]
    state = jnp.concatenate([whole, jnp.zeros((FPAD - FROWS, 128), F32)], 0)
    norm = jnp.concatenate(
        [
            whole[FEAT : FEAT + 1] + whole[FEAT + 1 : FEAT + 2],
            whole[FEAT + 2 : FEAT + 3] + whole[FEAT + 3 : FEAT + 4],
        ],
        1,
    )
    return state.astype(BF16), norm


def align4(qk, align_ref):
    out = dot(qk, align_ref[...]).astype(BF16)
    return [out[:, i * 128 : (i + 1) * 128] for i in range(4)]


def column(seg_ref):
    row = seg_ref[0]
    return jnp.transpose(jnp.broadcast_to(row, (128, row.shape[1])))[:, 0:1]


def mask_of(seg_ref, meta_ref, which):
    at = 1 + which * pl.num_programs(0) + pl.program_id(0)
    return jnp.where(column(seg_ref) == meta_ref[at].astype(F32), 1.0, 0.0)


def visible(seg_ref):
    t = seg_ref.shape[2]
    causal = lax.broadcasted_iota(jnp.int32, (t, t), 0) >= lax.broadcasted_iota(jnp.int32, (t, t), 1)
    return causal & (column(seg_ref) == seg_ref[0])


def state_kernel(me_ref, qkv_ref, seg_ref, feat_ref, rows_ref, align_ref, out_ref):
    me = me_ref[0]
    qk = ordered(qkv_ref, me, slice(256, 384))
    v = ordered(qkv_ref, me, slice(0, 256))
    last = mask_of(seg_ref, me_ref, 1)
    parts = align4(qk, align_ref)
    for head in range(2):
        _, _, feat = phi(parts[2 + head], feat_ref[...], rows_ref[...])
        feat = feat * last
        state = t_dot(feat.astype(BF16), v[:, head * 128 : (head + 1) * 128])
        put_state(out_ref, head, state, jnp.sum(feat, 0, keepdims=True))


def intra_kernel(me_ref, qkv_ref, seg_ref, align_ref, num_ref, den_ref):
    me = me_ref[0]
    qk = ordered(qkv_ref, me, slice(256, 384))
    v = ordered(qkv_ref, me, slice(0, 256))
    see = visible(seg_ref)
    parts = align4(qk, align_ref)
    den_ref[0] = jnp.zeros(den_ref.shape[1:], F32)
    for head in range(2):
        z = dot_t(parts[head], parts[2 + head])
        w = jnp.where(see, 1.0 + z * (0.25 + 0.03125 * z), 0.0)
        num_ref[0, :, head * 128 : (head + 1) * 128] = dot(
            w.astype(BF16), v[:, head * 128 : (head + 1) * 128]
        )
        den_ref[0, :, head : head + 1] = jnp.sum(w, 1, keepdims=True)


def output_kernel(
    me_ref, qkv_ref, seg_ref, feat_ref, rows_ref, align_ref, num_ref, den_ref, state_ref, o_ref, all_ref
):
    me = me_ref[0]
    qk = ordered(qkv_ref, me, slice(256, 384))
    use = mask_of(seg_ref, me_ref, 0)
    parts = align4(qk, align_ref)
    all_ref[0] = jnp.zeros(all_ref.shape[1:], F32)
    for head in range(2):
        lanes = slice(head * 128, (head + 1) * 128)
        _, _, feat = phi(parts[head], feat_ref[...], rows_ref[...])
        state, norm = get_state(state_ref, head)
        num = num_ref[0, :, lanes] + use * dot(feat.astype(BF16), state)
        den = den_ref[0, :, head : head + 1] + use * jnp.sum(feat * norm, 1, keepdims=True)
        all_ref[0, :, head : head + 1] = den
        put_ordered(o_ref, me, (num / den).astype(BF16), lanes)


def back_parts(me, o_ref, do_ref, den_ref, head):
    lanes = slice(head * 128, (head + 1) * 128)
    inv = 1.0 / den_ref[0, :, head : head + 1]
    do = ordered(do_ref, me, lanes).astype(F32)
    o = ordered(o_ref, me, lanes).astype(F32)
    return (do * inv).astype(BF16), -jnp.sum(do * o, 1, keepdims=True) * inv


def back_state_kernel(
    me_ref, qkv_ref, seg_ref, feat_ref, rows_ref, align_ref, o_ref, do_ref, den_ref, out_ref
):
    me = me_ref[0]
    qk = ordered(qkv_ref, me, slice(256, 384))
    use = mask_of(seg_ref, me_ref, 0)
    parts = align4(qk, align_ref)
    for head in range(2):
        g, c = back_parts(me, o_ref, do_ref, den_ref, head)
        _, _, feat = phi(parts[head], feat_ref[...], rows_ref[...])
        feat = feat * use
        put_state(out_ref, head, t_dot(feat.astype(BF16), g), jnp.sum(feat * c, 0, keepdims=True))


def back_intra_kernel(
    me_ref, qkv_ref, seg_ref, feat_ref, rows_ref, align_ref, o_ref, do_ref, den_ref, state_ref,
    dq_ref, dk_ref, dv_ref,
):
    me = me_ref[0]
    qk = ordered(qkv_ref, me, slice(256, 384))
    v = ordered(qkv_ref, me, slice(0, 256))
    use = mask_of(seg_ref, me_ref, 0)
    see = visible(seg_ref)
    parts = align4(qk, align_ref)
    for head in range(2):
        lanes = slice(head * 128, (head + 1) * 128)
        g, c = back_parts(me, o_ref, do_ref, den_ref, head)
        z = dot_t(parts[head], parts[2 + head])
        w = jnp.where(see, 1.0 + z * (0.25 + 0.03125 * z), 0.0)
        dv_ref[0, :, lanes] = t_dot(w.astype(BF16), g)
        dw = dot_t(g, v[:, lanes]) + c
        dz = jnp.where(see, dw * (0.25 + 0.0625 * z), 0.0).astype(BF16)
        a, b, _ = phi(parts[head], feat_ref[...], rows_ref[...])
        state, norm = get_state(state_ref, head)
        grad = use * (dot_t(g, state) + c * norm)
        dq_ref[0, :, lanes] = dot(dz, parts[2 + head]) + phi_back(a, b, grad, feat_ref[...], rows_ref[...])
        dk_ref[0, :, lanes] = t_dot(dz, parts[head])


def back_output_kernel(
    me_ref, qkv_ref, seg_ref, feat_ref, rows_ref, align_ref, state_ref, dq_ref, dk_ref, dv_ref, inv_ref, out_ref, scaled_ref
):
    me = me_ref[0]
    qk = ordered(qkv_ref, me, slice(256, 384))
    v = ordered(qkv_ref, me, slice(0, 256))
    last = mask_of(seg_ref, me_ref, 1)
    parts = align4(qk, align_ref)
    inv = ordered(inv_ref, me)
    packed = None
    for head in range(2):
        lanes = slice(head * 128, (head + 1) * 128)
        a, b, feat = phi(parts[2 + head], feat_ref[...], rows_ref[...])
        state, norm = get_state(state_ref, head)
        grad = last * (dot_t(v[:, lanes], state) + norm)
        dk = dk_ref[0, :, lanes] + phi_back(a, b, grad, feat_ref[...], rows_ref[...])
        dv = dv_ref[0, :, lanes] + last * dot(feat.astype(BF16), state)
        put_ordered(out_ref, me, dv.astype(BF16), lanes)
        put_ordered(scaled_ref, me, (dv * inv).astype(BF16), lanes)
        place = align_ref[...]
        term = dot_t(dq_ref[0, :, lanes].astype(BF16), place[:, head * 128 : (head + 1) * 128]) + dot_t(
            dk.astype(BF16), place[:, (2 + head) * 128 : (3 + head) * 128]
        )
        packed = term if packed is None else packed + term
    put_ordered(out_ref, me, packed.astype(BF16), slice(256, 384))
    put_ordered(scaled_ref, me, (packed * inv).astype(BF16), slice(256, 384))


def attention_call(kernel, me, ins, kinds, outs, flops, deps=()):
    def spec(a, kind):
        if kind == "s":
            return pl.BlockSpec((8, 1) + a.shape[2:], lambda i, m: (0, i, 0, 0))
        rest = len(a.shape) - 1
        if kind == "q":
            return pl.BlockSpec((1,) + a.shape[1:], lambda i, m: (i,) + (0,) * rest)
        return pl.BlockSpec(a.shape, lambda i, m: (0,) * (rest + 1))

    seqs = ins[0].shape[1]
    n = 1 + len(ins)

    def wrapped(*refs):
        kernel(*refs[:n], *refs[n + len(deps) :])

    return pl.pallas_call(
        wrapped,
        out_shape=far_out([a for a, _ in outs]),
        grid_spec=pltpu.PrefetchScalarGridSpec(
            num_scalar_prefetch=1,
            grid=(seqs,),
            in_specs=[spec(a, k) for a, k in zip(ins, kinds)] + [pl.BlockSpec(memory_space=pl.ANY)] * len(deps),
            out_specs=[spec(a, k) for a, k in outs],
        ),
        compiler_params=params(28),
        cost_estimate=cost(flops, *ins, *[a for a, _ in outs]),
        name=kernel.__name__,
    )(me, *far_in(ins), *deps)


def pick(cond, a, b):
    return jnp.where(cond, a, b)


def half_columns(gate, up, which, n_main, n_mid):
    mid = slice(n_main, n_main + 2 * n_mid)
    main = slice(0, n_main) if which == 0 else slice(n_main + 2 * n_mid, None)
    part = slice(0, n_mid) if which == 0 else slice(n_mid, None)
    return jnp.concatenate([gate[:, main], up[:, main], gate[:, mid][:, part], up[:, mid][:, part]], 1)


def body(inputs, segments, qw, kw, vw, pw, again, gw, uw, dw, fgain, upstream):
    hi, core, row, col = (lax.axis_index(a) for a in ("hi", "core", "row", "col"))
    rows = lax.axis_size("row")
    shards = 2 * rows
    seqs, sub = inputs.shape[0], inputs.shape[3]
    tokens = seqs * sub
    span = 8 * sub
    n_rows = qw.shape[0]
    is0 = col == 0
    ff = gw.shape[1]
    half_ff = ff // 2
    n_mid = 64
    n_main = half_ff - n_mid
    feat_c, rows_c, align_c = feature_constants()
    sds = jax.ShapeDtypeStruct
    x = inputs.reshape(tokens, D)

    shard_pairs = [(s, (s % rows) * 2 + s // rows) for s in range(shards)]
    moved = lax.ppermute(pw, ("row", "col"), shard_pairs)

    gain_one = again.astype(F32)[:, None]
    seg_own = segments.reshape(seqs, 4 * sub)

    def by_dest(w, scale):
        return (w.astype(F32) * scale).astype(BF16).reshape(n_rows, 8, -1)

    lane = lax.broadcasted_iota(jnp.int32, (n_rows, PAYLOAD - 320), 1)
    ends = jnp.pad(seg_own[:, -1], (0, n_rows - seqs)).astype(F32)[:, None]
    tens = jnp.floor(ends * (1.0 / 128.0))
    extra = jnp.where(
        lane == 0,
        fgain.astype(F32)[:, None],
        jnp.where(lane == 1, tens, jnp.where(lane == 2, ends - 128.0 * tens, 0.0)),
    ).astype(BF16)
    payload = jnp.concatenate(
        [
            by_dest(vw, gain_one),
            by_dest(qw, gain_one),
            by_dest(kw, gain_one),
            jnp.broadcast_to(extra[:, None], (n_rows, 8, PAYLOAD - 320)),
        ],
        2,
    ).transpose(1, 0, 2)
    payload = lax.all_to_all(payload, GROUP, split_axis=0, concat_axis=0, tiled=True)
    x_own = after(x, payload)
    xs = gather8(x_own)
    w_proj = lax.all_gather(moved, "row", axis=0, tiled=True)
    gathered = lax.all_gather(after(payload, moved), "row", axis=0, tiled=False)
    lasts = gathered[:, 1, :seqs, 321:323].astype(F32)
    lasts = (lasts[:, :, 0] * 128.0 + lasts[:, :, 1]).astype(jnp.int32)

    seg_other = swap(seg_own, "col")
    seg = jnp.concatenate([pick(is0, seg_own, seg_other), pick(is0, seg_other, seg_own)], 1)
    seg_row = seg.astype(F32)[:, None, :]
    before = jnp.where(row > 0, lasts[jnp.maximum(row - 1, 0)], -1)
    here = lasts[row]
    me3 = (4 * col + 2 * hi + core).astype(jnp.int32)
    meta = jnp.concatenate([me3[None], before, here])

    ends = jnp.concatenate([lasts, jnp.full((1, seqs), -1, jnp.int32)])

    def end_of(r):
        return ends[jnp.where((r >= 0) & (r < rows), r, rows)]

    def same(r, other):
        return ((end_of(r) == other) & (r >= 0) & (r < rows)).astype(F32)

    every = 8 * tokens
    qkv, inv, w_qkv = slot_call(
        qkv_kernel, xs, [(gathered.reshape(rows, 4, 2 * n_rows, PAYLOAD), False)],
        [sds((8, tokens, PAYLOAD), BF16), sds((8, tokens, 128), F32)], 2 * every * D * PAYLOAD,
        deps=[seg_row], whole=[sds((D, PAYLOAD), BF16)],
    )
    gain_two = w_qkv[:, 320].astype(F32)[None, :]
    inv = inv.reshape(8, seqs, sub, 128)
    ups = gather8(after(upstream.reshape(tokens, D), qkv))
    qkv = qkv.reshape(8, seqs, sub, PAYLOAD)
    st = sds((seqs, 2, FROWS, 128), BF16)
    near = 4 * seqs * span * span * 160
    far = 4 * seqs * span * FPAD * 300
    (state,) = attention_call(
        state_kernel, meta, [qkv, seg_row, feat_c, rows_c, align_c], "sqccc", [(st, "q")], far
    )
    mine = pick(is0, half_columns(gw, uw, 0, n_main, n_mid), half_columns(gw, uw, 1, n_main, n_mid))
    theirs = pick(is0, half_columns(gw, uw, 1, n_main, n_mid), half_columns(gw, uw, 0, n_main, n_mid))
    got = swap(after(theirs, xs[6][0], xs[7][0]), "col")
    got = after(got, state)
    gu_rows = jnp.concatenate([pick(is0, mine, got), pick(is0, got, mine)], 0)
    w_gu = lax.all_gather(gu_rows, "row", axis=0, tiled=True)
    down0 = dw[: n_main + n_mid]
    down1 = jnp.concatenate([dw[n_main + 2 * n_mid :], dw[n_main + n_mid : n_main + 2 * n_mid]], 0)
    d_mine, d_theirs = pick(is0, down0, down1), pick(is0, down1, down0)
    d_got = swap(after(d_theirs, got), "col")
    d_cols = jnp.stack([pick(is0, d_mine, d_got), pick(is0, d_got, d_mine)])
    w_down = lax.all_gather(d_cols, "row", axis=0, tiled=True)
    fold = shards // 8
    w_down = (
        w_down.reshape(8, fold, half_ff, D // shards).transpose(0, 2, 1, 3).reshape(8, half_ff, D // 8)
    )

    num, den_in = attention_call(
        intra_kernel, meta, [qkv, seg_row, align_c], "sqc",
        [(sds((seqs, span, 256), F32), "q"), (sds((seqs, span, 8), F32), "q")], near,
    )
    forth = walk_steps(state, lambda d: same(row - d, here), lambda d: same(row - d, before), True)
    _, came = next(forth)
    came, num, den_in = meet(came, num, den_in)
    state_in = finish(forth, came)
    o, den = attention_call(
        output_kernel, meta, [qkv, seg_row, feat_c, rows_c, align_c, num, den_in, state_in], "sqcccqqq",
        [(sds((8, seqs, sub, 256), BF16), "s"), (sds((seqs, span, 8), F32), "q")], far,
        [ups[6][0], ups[7][0], d_got],
    )
    o_rows = o.reshape(8, tokens, 256)
    residual, a2_own = row_call(
        residual_kernel, scatter8(parts_call(o_rows, w_proj, "nn", mib=28)), [x, gain_two], [F32, BF16]
    )

    ff_flops = 2 * every * D * half_ff
    steps = gather_steps(a2_own)
    wide = [
        sds((8, tokens, ff), BF16),
        sds((8, tokens, half_ff + n_mid), BF16),
        sds((8, half_ff + n_mid, tokens), BF16),
    ]
    hidden = slot_call(ffn_in_kernel, next(steps), [(w_gu, False)], wide, 2 * ff_flops, slots=(0, 2))
    hidden = slot_call(
        ffn_in_kernel, steps.send(hidden[:1]), [(w_gu, False)], wide, 2 * ff_flops, slots=(2, 6), into=hidden
    )
    a2 = finish(steps, hidden[:1])
    gu, h, h_turned = slot_call(
        ffn_in_kernel, a2, [(w_gu, False)], wide, 2 * ff_flops, slots=(6, 8), into=hidden
    )
    (down_g,) = grad_call(
        down_grad_kernel, ups, 256, [h_turned], [],
        [(sds((8, half_ff, 256), BF16), (1, half_ff, 256), lambda i: (i, 0, 0))], ff_flops,
    )
    late = {}

    def ffn_back(slots, into, deps=()):
        return slot_call(
            ffn_back_kernel, ups, [(w_down, False), (gu, True)], [sds((8, tokens, ff), BF16)], ff_flops, deps,
            slots=slots, into=into,
        )[0]

    half = tokens // 2
    dgu = ffn_back((6, 8), (), [down_g])
    xy, xyc = parts_call(dgu, w_gu, "nt", pairs=(3,))
    xyc, dgu = meet(swap(xyc, "core"), ffn_back((2, 6), [dgu], [xy]))
    to_x = pair_sum(xy, xyc, 0, half).astype(BF16)
    to_y = pair_sum(xy, xyc, half, tokens).astype(BF16)
    from_x, from_y, y, yc, x_, xc = meet(
        swap(to_x, "col"), swap(to_y, "hi"), *parts_call(dgu, w_gu, "nt", [to_x, to_y], pairs=(1, 2))
    )
    xc, yc, dgu = meet(swap(xc, "core"), swap(yc, "core"), ffn_back((0, 2), [dgu], [x_]))
    near_x = pair_sum(x_, xc, 0, half).astype(BF16)
    near_y = pair_sum(y, yc, half, tokens).astype(BF16)
    far_x = (pair_sum(x_, xc, half, tokens) + from_y.astype(F32)).astype(BF16)
    far_y = (pair_sum(y, yc, 0, half) + from_x.astype(F32)).astype(BF16)
    own, other = parts_call(dgu, w_gu, "nt", [near_x, near_y, far_x, far_y], pairs=(0,))
    down_g = (
        down_g.reshape(8, half_ff, fold, D // shards).transpose(0, 2, 1, 3).reshape(shards * half_ff, -1)
    )
    down_g = lax.psum_scatter(down_g, "row", scatter_dimension=0, tiled=True)
    block = D // shards
    gu_gs, gains = [], []

    def gu_half(x_bit):
        def run(sent):
            one, gain = grad_call(
                gu_grad_kernel, a2, 256, [dgu], [(w_gu, (256, ff), lambda i: (2 * i + x_bit, 0))],
                [
                    (sds((D // 2, ff), BF16), (256, ff), lambda i: (i, 0)),
                    (sds((D // 2, 128), F32), (256, 128), lambda i: (i, 0)),
                ],
                ff_flops, lambda i: 2 * i + x_bit, 4, sent,
            )
            gu_gs.append(one)
            gains.append(gain)
            return [one]

        return run

    gu_half(0)([own])
    first_x, first_y, last_x, last_y, other, gu_gs[0] = meet(
        swap(near_x, "col"), swap(near_y, "hi"), swap(far_x, "col"), swap(far_y, "hi"), swap(other, "core"), gu_gs[0]
    )
    grad_r, datt_own = row_call(
        residual_back_kernel, [own, other, first_x, last_y, last_x, first_y],
        [upstream.reshape(tokens, D), residual, gain_two], [F32, BF16],
    )
    gu_half(1)([datt_own])
    over_x, over_y, over_c, gu_gs[1] = meet(
        swap(datt_own, "col"), swap(datt_own, "hi"), swap(datt_own, "core"), gu_gs[1]
    )
    to_x, to_y = over_y[:half], over_x[half:]
    down_parts = parts_call(h, w_down, "blocks", [to_x, to_y])
    top, low, over_yc, over_xc, *down_parts = meet(
        swap(to_x, "col"), swap(to_y, "hi"), swap(over_y, "core"), swap(over_x, "core"), *down_parts
    )
    datt = [
        (datt_own, 0, 0), (over_c, 1, 0), (over_y, 2, 0), (over_yc, 3, 0), (over_x, 4, 0), (over_xc, 5, 0),
        (top, 6, 0), (low, 6, half), (swap(top, "core"), 7, 0), (swap(low, "core"), 7, half),
    ]
    (do,) = slot_call(
        do_kernel, datt, [(w_proj, False)], [sds((8, tokens, 256), BF16)], 2 * every * D * 256, [down_g]
    )
    gain_part = jnp.stack([g.reshape(4, 256, 128) for g in gains], 1).reshape(D, 128)
    if fold > 1:
        natural = jnp.stack([g.reshape(4, 256, ff) for g in gu_gs], 1)
        by_col = natural.reshape(rows, 2, block, ff).transpose(1, 0, 2, 3)
        gu_gs = [by_col[0].reshape(D // 2, ff), by_col[1].reshape(D // 2, ff)]
    gu_r = [lax.psum_scatter(g, "row", scatter_dimension=0, tiled=True) for g in gu_gs]

    do = do.reshape(8, seqs, sub, 256)

    (dstate,) = attention_call(
        back_state_kernel, meta, [qkv, seg_row, feat_c, rows_c, align_c, o, do, den], "sqcccssq",
        [(st, "q")], far,
    )
    part = sds((seqs, span, 256), F32)

    back = walk_steps(
        dstate,
        lambda d: same(row + d - 1, before) * (row + d < rows),
        lambda d: same(row + d - 1, here) * (row + d < rows),
        False,
    )
    _, came = next(back)
    own, other, y, yc, x_, xc, xy, xyc = down_parts
    other, yc, xc, xyc = (swap(part, "core") for part in (other, yc, xc, xyc))
    to_x = pair_sum(xy, xyc, 0, half).astype(BF16)
    to_y = pair_sum(xy, xyc, half, tokens).astype(BF16)
    near_x = pair_sum(x_, xc, 0, half).astype(BF16)
    near_y = pair_sum(y, yc, half, tokens).astype(BF16)
    intra = attention_call(
        back_intra_kernel, meta, [qkv, seg_row, feat_c, rows_c, align_c, o, do, den, state_in],
        "sqcccssqq", [(part, "q")] * 3, 3 * near + far, [dstate, to_x, to_y, near_x, near_y, gu_r[0]],
    )
    dq, dk, dv = intra
    came, from_x, from_y, first_x, first_y, dq = meet(
        came, swap(to_x, "col"), swap(to_y, "hi"), swap(near_x, "col"), swap(near_y, "hi"), dq
    )
    far_x = (pair_sum(x_, xc, half, tokens) + from_y.astype(F32)).astype(BF16)
    far_y = (pair_sum(y, yc, 0, half) + from_x.astype(F32)).astype(BF16)
    step = back.send(came)
    now = None
    if step is not None:
        now, came = step
    (proj_g,) = grad_call(
        proj_grad_kernel, datt, 1024, [o_rows], [],
        [(sds((256, D), BF16), (256, 1024), lambda i: (0, i))], 2 * every * D * 256, deps=[far_x, far_y, now], mib=24,
    )
    down_r = down_g.reshape(2, half_ff, D // shards)
    d_keep, d_send = pick(is0, down_r[0], down_r[1]), pick(is0, down_r[1], down_r[0])
    g_keep = pick(is0, gu_r[0], gu_r[1])
    g_send = pick(is0, gu_r[1], gu_r[0])
    came, last_x, last_y, d_got, proj_g = meet(
        came, swap(far_x, "col"), swap(far_y, "hi"), swap(d_send, "col"), proj_g
    )
    (outputs,) = row_call(
        output_rows_kernel, [own, other, first_x, last_y, last_x, first_y], [residual], [BF16]
    )
    dstate_out = finish(back, came)
    proj_r = lax.psum_scatter(proj_g, "row", scatter_dimension=0, tiled=True)
    row_out = sds((8, seqs, sub, PAYLOAD), BF16)
    dqkv, scaled = attention_call(
        back_output_kernel, meta, [qkv, seg_row, feat_c, rows_c, align_c, dstate_out, dq, dk, dv, inv],
        "sqcccqqqqs", [(row_out, "s")] * 2, 2 * far, [outputs, gu_r[1]],
    )

    def qkv_side(sent):
        (late["qkv"],) = grad_call(
            qkv_grad_kernel, xs, 512, [scaled.reshape(8, tokens, PAYLOAD)],
            [(gain_part, (512, 128), lambda i: (i, 0))],
            [
                (
                    sds((rows, 4, 2 * n_rows, PAYLOAD), BF16),
                    (rows, 1, 2 * n_rows, PAYLOAD),
                    lambda i: (0, i, 0, 0),
                )
            ],
            2 * every * D * PAYLOAD, deps=sent, mib=24,
        )
        return [late["qkv"]]

    own, other, y, yc, x_, xc, xy, xyc = parts_call(
        dqkv.reshape(8, tokens, PAYLOAD), w_qkv, "nt", [proj_r], 28
    )
    qkv_side([own])
    other, yc, xc, xyc, qkv_g = meet(*(swap(part, "core") for part in (other, yc, xc, xyc)), late["qkv"])
    to_x = pair_sum(xy, xyc, 0, half).astype(BF16)
    to_y = pair_sum(xy, xyc, half, tokens).astype(BF16)
    near_x = pair_sum(x_, xc, 0, half).astype(BF16)
    near_y = pair_sum(y, yc, half, tokens).astype(BF16)
    from_x, from_y, first_x, first_y = (
        swap(to_x, "col"), swap(to_y, "hi"), swap(near_x, "col"), swap(near_y, "hi")
    )
    far_x = (pair_sum(x_, xc, half, tokens) + from_y.astype(F32)).astype(BF16)
    far_y = (pair_sum(y, yc, 0, half) + from_x.astype(F32)).astype(BF16)
    g_got = swap(after(g_send, far_x), "col")
    f_pieces = [own, other, first_x, swap(far_y, "hi"), swap(far_x, "col"), first_y]
    (inputs_grad,) = row_call(input_back_kernel, f_pieces, [x, grad_r], [F32])
    qkv_g = lax.psum_scatter(qkv_g.reshape(D, PAYLOAD), "row", scatter_dimension=0, tiled=True)
    project_grad = lax.ppermute(
        after(proj_r, qkv_g), ("row", "col"), [(b, a) for a, b in shard_pairs]
    ).astype(F32)
    qkv_g = lax.all_to_all(
        qkv_g.reshape(8, n_rows, PAYLOAD), GROUP, split_axis=0, concat_axis=0, tiled=True
    ).astype(F32)
    per_row = qkv_g.transpose(1, 0, 2)
    v_g = per_row[:, :, :256].reshape(n_rows, -1)
    q_g = per_row[:, :, 256:288].reshape(n_rows, -1)
    k_g = per_row[:, :, 288:320].reshape(n_rows, -1)
    d0, d1 = pick(is0, d_keep, d_got).astype(F32), pick(is0, d_got, d_keep).astype(F32)
    down_grad = jnp.concatenate([d0, d1[n_main:], d1[:n_main]], 0)
    g0, g1 = pick(is0, g_keep, g_got).astype(F32), pick(is0, g_got, g_keep).astype(F32)
    m = 2 * n_main
    gate_grad = jnp.concatenate(
        [g0[:, :n_main], g0[:, m : m + n_mid], g1[:, m : m + n_mid], g1[:, :n_main]], 1
    )
    up_grad = jnp.concatenate(
        [g0[:, n_main:m], g0[:, m + n_mid :], g1[:, m + n_mid :], g1[:, n_main:m]], 1
    )
    forward_grad = jnp.sum(per_row[:, :, 320], 1) / fgain.astype(F32)
    attend_grad = (
        jnp.sum(v_g * vw.astype(F32), 1) + jnp.sum(q_g * qw.astype(F32), 1) + jnp.sum(k_g * kw.astype(F32), 1)
    )

    return (
        outputs.reshape(inputs.shape),
        inputs_grad.reshape(inputs.shape),
        q_g * gain_one,
        k_g * gain_one,
        v_g * gain_one,
        project_grad,
        attend_grad,
        gate_grad,
        up_grad,
        down_grad,
        forward_grad,
    )


def solution(mesh):
    heads, shards = mesh.devices.shape
    fine = Mesh(mesh.devices.reshape(heads // 2, 2, shards // 2, 2), ("hi", "core", "row", "col"))
    h, s = ("hi", "core"), ("row", "col")
    every = P(h + s)
    tokens = P(None, s, h)
    return jax.shard_map(
        body,
        mesh=fine,
        in_specs=(
            tokens, P(None, s), every, every, every, every, every, P(s, h), P(s, h), P(h, s), every, tokens,
        ),
        out_specs=(
            tokens, tokens, every, every, every, every, every, P(s, h), P(s, h), P(h, s), every,
        ),
        check_vma=False,
    )
```

```python
import math

import numpy as np

import jax
import jax.numpy as jnp
from jax import lax
from jax.experimental import pallas as pl
from jax.experimental.pallas import tpu as pltpu
from jax.sharding import Mesh
from jax.sharding import PartitionSpec as P

D = 2048
HEADS = 16
QK = 16
VD = 128
EPS = 1e-05
F32 = jnp.float32
BF16 = jnp.bfloat16
GROUP = ("hi", "core", "col")
FEAT = 1 + QK + QK * (QK + 1) // 2
FPAD = 256
FROWS = 160
PAYLOAD = 384


def feature_constants():
    left = np.zeros((128, FPAD), np.float32)
    right = np.zeros((128, FPAD), np.float32)
    rows = np.zeros((8, 2 * FPAD), np.float32)
    at = 0
    for i in range(QK):
        for j in range(i, QK):
            left[i, at] = 1.0
            right[j, at] = 1.0
            rows[1, at] = (1.0 if i == j else math.sqrt(2.0)) / math.sqrt(2.0 * QK)
            at += 1
    for i in range(QK):
        left[i, at] = 1.0
        rows[0, FPAD + at] = 1.0
        rows[1, at] = QK ** (-0.25)
        at += 1
    rows[0, at] = 1.0
    rows[0, FPAD + at] = 1.0
    rows[1, at] = 1.0
    align = np.zeros((4, 128, 128), np.float32)
    for part in range(4):
        for i in range(QK):
            align[part, part * QK + i, i] = 1.0
    return (
        jnp.asarray(np.concatenate([left, right], 1), BF16),
        jnp.asarray(rows, F32),
        jnp.asarray(align.transpose(1, 0, 2).reshape(128, 512), BF16),
    )


def dot(a, b):
    return jnp.dot(a, b, preferred_element_type=F32)


def dot_t(a, b):
    return lax.dot_general(a, b, (((1,), (1,)), ((), ())), preferred_element_type=F32)


def t_dot(a, b):
    return lax.dot_general(a, b, (((0,), (0,)), ((), ())), preferred_element_type=F32)


def swap(value, axis):
    return lax.ppermute(value, axis, [(0, 1), (1, 0)])


def after(value, *others):
    if not others:
        return value

    def gate(*refs):
        pass

    return pl.pallas_call(
        gate,
        in_specs=[pl.BlockSpec(memory_space=pl.ANY)] * (1 + len(others)),
        out_specs=pl.BlockSpec(memory_space=pl.ANY),
        out_shape=jax.ShapeDtypeStruct(value.shape, value.dtype),
        input_output_aliases={0: 0},
        cost_estimate=pl.CostEstimate(flops=0, transcendentals=0, bytes_accessed=0),
        name="gate",
    )(value, *others)


def meet(*values):
    def gate(*refs):
        pass

    return pl.pallas_call(
        gate,
        in_specs=[pl.BlockSpec(memory_space=pl.ANY)] * len(values),
        out_specs=[pl.BlockSpec(memory_space=pl.ANY)] * len(values),
        out_shape=[jax.ShapeDtypeStruct(v.shape, v.dtype) for v in values],
        input_output_aliases={i: i for i in range(len(values))},
        cost_estimate=pl.CostEstimate(flops=0, transcendentals=0, bytes_accessed=0),
        name="meet",
    )(*values)


def gather_steps(own):
    half = own.shape[0] // 2
    over_x = swap(own, "col")
    over_y = swap(own, "hi")
    rows = [(own, 0, 0), (swap(own, "core"), 1, 0)]
    done = yield rows
    over_x, over_y = after(over_x, *done), after(over_y, *done)
    top = swap(over_y[:half], "col")
    low = swap(over_x[half:], "hi")
    near = [(over_y, 2, 0), (swap(over_y, "core"), 3, 0), (over_x, 4, 0), (swap(over_x, "core"), 5, 0)]
    done = yield near
    top, low = after(top, *done), after(low, *done)
    far = [(top, 6, 0), (low, 6, half), (swap(top, "core"), 7, 0), (swap(low, "core"), 7, half)]
    return rows + near + far


def gather8(own):
    steps = gather_steps(own)
    next(steps)
    return finish(steps)


def scatter_steps(parts):
    def both(one, two, start, end):
        return one[start:end].astype(F32) + two[start:end].astype(F32)

    own, other, y, yc, x, xc, xy, xyc = parts
    n = xy.shape[0]
    half = n // 2
    xyc = swap(xyc, "core")
    xc = swap(xc, "core")
    yc = swap(yc, "core")
    other = swap(other, "core")
    to_x = both(xy, xyc, 0, half).astype(BF16)
    to_y = both(xy, xyc, half, n).astype(BF16)
    near_x = both(x, xc, 0, half).astype(BF16)
    near_y = both(y, yc, half, n).astype(BF16)
    from_x, from_y = swap(to_x, "col"), swap(to_y, "hi")
    first_x, first_y = swap(near_x, "col"), swap(near_y, "hi")
    done = yield [to_x, to_y, near_x, near_y]
    from_x, from_y = after(from_x, *done), after(from_y, *done)
    far_x = (both(x, xc, half, n) + from_y.astype(F32)).astype(BF16)
    far_y = (both(y, yc, 0, half) + from_x.astype(F32)).astype(BF16)
    last_x, last_y = swap(far_x, "col"), swap(far_y, "hi")
    done = yield [far_x, far_y]
    last_x, last_y = after(last_x, *done), after(last_y, *done)
    return own, other, first_x, last_y, last_x, first_y


def walk_steps(value, linked, joined, up):
    rows = lax.axis_size("row")
    total = None
    now = value
    step = 1
    while step < rows:
        pairs = [(i, i + step) if up else (i + step, i) for i in range(rows - step)]
        came = lax.ppermute(now, "row", pairs)
        wide = (yield now, came).astype(F32)
        term = joined(step)[:, None, None, None] * wide
        total = term if total is None else total + term
        if 2 * step < rows:
            now = (now.astype(F32) + linked(step)[:, None, None, None] * wide).astype(BF16)
        step = 2 * step
    return total


def finish(steps, done=()):
    try:
        step = steps.send(done)
        while True:
            step = steps.send(step[1] if isinstance(step, tuple) else ())
    except StopIteration as end:
        return end.value


def pair_sum(one, two, start, end):
    return one[start:end].astype(F32) + two[start:end].astype(F32)


def scatter8(parts, *kernels):
    steps = scatter_steps(parts)
    sent = next(steps)
    for i, kernel in enumerate(kernels):
        done = kernel(sent)
        if i == 1:
            return finish(steps, done)
        sent = steps.send(done)
    return finish(steps)


def far_in(values):
    return [pltpu.with_memory_space_constraint(v, pltpu.HBM) if math.prod(v.shape) >= 65536 else v for v in values]


def far_out(shapes, far=False):
    if not far:
        return list(shapes)
    return [pltpu.HBM(a.shape, a.dtype) if math.prod(a.shape) >= 65536 else a for a in shapes]


def params(mib=60):
    return pltpu.CompilerParams(dimension_semantics=("arbitrary",), vmem_limit_bytes=mib * 1024 * 1024)


def cost(flops, *arrays):
    return pl.CostEstimate(
        flops=int(flops),
        transcendentals=0,
        bytes_accessed=int(sum(math.prod(a.shape) * a.dtype.itemsize for a in arrays)),
    )


def slot_call(kernel, pieces, ins, outs, flops, deps=(), whole=(), slots=(0, 8), into=(), mib=60):
    first, count = slots[0], slots[1] - slots[0]
    pieces = [p for p in pieces if slots[0] <= p[1] < slots[1]]
    n = len(pieces)
    per, width = outs[0].shape[1], pieces[0][0].shape[1]
    extra = list(deps) + list(into)

    def wrapped(*refs):
        rows = refs[:n]
        at = n + len(ins)
        rest = refs[n:at] + refs[at + len(extra) : at + len(extra) + len(outs) + len(whole)]
        buf, sem = refs[-2:]
        i = pl.program_id(0)

        @pl.when(i == 0)
        def _():
            for (a, slot, start), ref in zip(pieces, rows):
                there = buf.at[slot - first, pl.ds(start, a.shape[0])]
                pltpu.make_async_copy(ref, there, sem.at[slot - first]).start()

        pltpu.make_async_copy(buf.at[i], buf.at[i], sem.at[i]).wait()
        kernel(buf.at[i], *rest)

    def spec(a, by_slot):
        rest = len(a.shape) - 1
        if by_slot:
            return pl.BlockSpec((None,) + a.shape[1:], lambda i: (i + first,) + (0,) * rest)
        return pl.BlockSpec(a.shape, lambda i: (0,) * (rest + 1))

    at = n + len(ins) + len(deps)
    return pl.pallas_call(
        wrapped,
        grid=(count,),
        in_specs=[pl.BlockSpec(memory_space=pltpu.HBM)] * n
        + [spec(a, k) for a, k in ins]
        + [pl.BlockSpec(memory_space=pl.ANY)] * len(extra),
        out_specs=[spec(a, True) for a in outs] + [spec(a, False) for a in whole],
        out_shape=far_out(list(outs) + list(whole)),
        scratch_shapes=[pltpu.VMEM((count, per, width), BF16), pltpu.SemaphoreType.DMA((count,))],
        input_output_aliases={at + i: i for i in range(len(into))},
        compiler_params=params(mib),
        cost_estimate=cost(
            flops * count // 8, *[a for a, _, _ in pieces], *[a for a, k in ins if not k], *outs[:count // 4], *whole
        ),
        name=kernel.__name__,
    )(*[a for a, _, _ in pieces], *far_in([a for a, _ in ins]), *extra)


def grad_call(kernel, pieces, tile, whole, ins, outs, flops, index=lambda i: i, steps=None, deps=(), mib=60):
    n = len(pieces)
    width = pieces[0][0].shape[1]
    places = [(slot, start, a.shape[0]) for a, slot, start in pieces]

    def wrapped(*refs):
        at = n + len(whole) + len(ins)
        kernel(list(zip(refs[:n], places)), *refs[n:at], *refs[at + len(deps) :])

    def fixed(a):
        rest = len(a.shape)
        return pl.BlockSpec(a.shape, lambda i: (0,) * rest)

    return pl.pallas_call(
        wrapped,
        grid=(steps or width // tile,),
        in_specs=[pl.BlockSpec((a.shape[0], tile), lambda i: (0, index(i))) for a, _, _ in pieces]
        + [fixed(a) for a in whole]
        + [pl.BlockSpec(block, where) for _, block, where in ins]
        + [pl.BlockSpec(memory_space=pl.ANY)] * len(deps),
        out_specs=[pl.BlockSpec(block, where) for _, block, where in outs],
        out_shape=far_out([a for a, _, _ in outs]),
        compiler_params=params(mib),
        cost_estimate=cost(
            flops, *[a for a, _, _ in pieces], *whole, *[a for a, _, _ in ins], *[a for a, _, _ in outs]
        ),
        name=kernel.__name__,
    )(*far_in([*[a for a, _, _ in pieces], *whole, *[a for a, _, _ in ins]]), *deps)


def summed(rows, right):
    total = None
    for ref, (slot, start, n) in rows:
        term = t_dot(ref[...], right[slot, start : start + n, :])
        total = term if total is None else total + term
    return total


def qkv_kernel(x_ref, given_ref, qkv_ref, inv_ref, w_ref):
    @pl.when(pl.program_id(0) == 0)
    def _():
        rows, groups, n, _ = given_ref.shape
        for g in range(groups):
            for r in range(rows):
                w_ref[pl.ds((g * rows + r) * n, n), :] = given_ref[r, g]

    x = x_ref[...]
    wide = x.astype(F32)
    inv = lax.rsqrt(jnp.sum(wide * wide, 1, keepdims=True) * (1.0 / x.shape[1]) + EPS)
    qkv_ref[...] = (dot(x, w_ref[...]) * inv).astype(BF16)
    inv_ref[...] = jnp.broadcast_to(inv, inv_ref.shape)


def ffn_in_kernel(a_ref, w_ref, gu_ref, h_ref, turned_ref):
    gu = dot(a_ref[...], w_ref[...])
    gu_ref[...] = gu.astype(BF16)
    m = (gu.shape[1] - 128) // 2
    g, u = gu[:, :m], gu[:, m : 2 * m]
    h_ref[:, :m] = (g * jax.nn.sigmoid(g) * u).astype(BF16)
    g = gu[:, 2 * m :]
    u = pltpu.roll(g, 64, 1)
    first = lax.broadcasted_iota(jnp.int32, g.shape, 1) < 64
    h_ref[:, m:] = jnp.where(first, g * jax.nn.sigmoid(g) * u, 0.0).astype(BF16)
    turned_ref[...] = jnp.transpose(h_ref[...])


def ffn_back_kernel(up_ref, w_ref, gu_ref, out_ref):
    up = up_ref[...]
    total = None
    for i in range(8):
        term = dot_t(up[:, i * 256 : (i + 1) * 256], w_ref[i])
        total = term if total is None else total + term
    m = total.shape[1] - 64

    def both(g, u, dh):
        s = jax.nn.sigmoid(g)
        return dh * u * (s * (1.0 + g * (1.0 - s))), dh * (g * s)

    gu = gu_ref[...].astype(F32)
    dg, du = both(gu[:, :m], gu[:, m : 2 * m], total[:, :m])
    out_ref[:, :m] = dg.astype(BF16)
    out_ref[:, m : 2 * m] = du.astype(BF16)
    mid = gu[:, 2 * m :]
    other = pltpu.roll(mid, 64, 1)
    first = lax.broadcasted_iota(jnp.int32, mid.shape, 1) < 64
    dh = jnp.concatenate([total[:, m:], total[:, m:]], 1)
    dg, du = both(jnp.where(first, mid, other), jnp.where(first, other, mid), dh)
    out_ref[:, 2 * m :] = jnp.where(first, dg, du).astype(BF16)


def down_grad_kernel(rows, h_ref, out_ref):
    total = None
    for ref, (slot, start, n) in rows:
        term = dot(h_ref[slot, : out_ref.shape[1], start : start + n], ref[...])
        total = term if total is None else total + term
    out_ref[0] = total.astype(BF16)


def gu_grad_kernel(rows, right_ref, w_ref, out_ref, gain_ref):
    total = summed(rows, right_ref)
    out_ref[...] = total.astype(BF16)
    gain_ref[...] = jnp.broadcast_to(
        jnp.sum(total * w_ref[...].astype(F32), 1, keepdims=True), gain_ref.shape
    )


def do_kernel(d_ref, w_ref, out_ref):
    out_ref[...] = dot_t(d_ref[...], w_ref[...]).astype(BF16)


def proj_grad_kernel(rows, o_ref, out_ref):
    total = None
    for ref, (slot, start, n) in rows:
        term = t_dot(o_ref[slot, start : start + n, :], ref[...])
        total = term if total is None else total + term
    out_ref[...] = total.astype(BF16)


def qkv_grad_kernel(rows, right_ref, gain_ref, out_ref):
    total = summed(rows, right_ref)
    lane = lax.broadcasted_iota(jnp.int32, (1, 128), 1)
    total = jnp.concatenate([total[:, :256], jnp.where(lane == 64, gain_ref[...], total[:, 256:])], 1)
    out_ref[...] = total.astype(BF16).reshape(out_ref.shape)


def row_sum(refs):
    own, other, first_x, last_y, last_x, first_y = [ref[...].astype(F32) for ref in refs]
    return own + other + jnp.concatenate([first_x + last_y, last_x + first_y], 0)


def scaled_rows(rows):
    inv = lax.rsqrt(jnp.sum(rows * rows, 1, keepdims=True) * (1.0 / rows.shape[1]) + EPS)
    return rows * inv, inv


def norm_back(normed, inv, grad):
    return inv * (grad - normed * (jnp.sum(grad * normed, 1, keepdims=True) * (1.0 / grad.shape[1])))


def residual_kernel(refs, x_ref, gain_ref, sum_ref, a_ref):
    rows = x_ref[...].astype(F32) + row_sum(refs)
    sum_ref[...] = rows
    a_ref[...] = (scaled_rows(rows)[0] * gain_ref[...]).astype(BF16)


def output_rows_kernel(refs, sum_ref, out_ref):
    out_ref[...] = (sum_ref[...] + row_sum(refs)).astype(BF16)


def residual_back_kernel(refs, up_ref, sum_ref, gain_ref, grad_ref, low_ref):
    normed, inv = scaled_rows(sum_ref[...])
    grad = up_ref[...].astype(F32) + norm_back(normed, inv, row_sum(refs) * gain_ref[...])
    grad_ref[...] = grad
    low_ref[...] = grad.astype(BF16)


def input_back_kernel(refs, x_ref, grad_ref, out_ref):
    normed, inv = scaled_rows(x_ref[...].astype(F32))
    out_ref[...] = grad_ref[...] + norm_back(normed, inv, row_sum(refs))


def weights_kernel(got_ref, place_ref, vw_ref, qw_ref, kw_ref, gain_ref, v_ref, q_ref, k_ref, gains_ref):
    gain = gain_ref[:, 0:1]
    attend = jnp.zeros(gain.shape, F32)
    forward = jnp.zeros(gain.shape, F32)
    heads = None
    lane = lax.broadcasted_iota(jnp.int32, (1, 128), 1)
    for d in range(8):
        lanes = slice(256 * d, 256 * (d + 1))
        part = got_ref[d, :, :256].astype(F32)
        attend = attend + jnp.sum(part * vw_ref[:, lanes].astype(F32), 1, keepdims=True)
        v_ref[:, lanes] = part * gain
        tail = got_ref[d, :, 256:]
        forward = forward + jnp.sum(jnp.where(lane == 64, tail.astype(F32), 0.0), 1, keepdims=True)
        term = dot(tail, place_ref[d])
        heads = term if heads is None else heads + term
    q, k = heads[:, :256], heads[:, 256:]
    attend = attend + jnp.sum(q * qw_ref[...].astype(F32) + k * kw_ref[...].astype(F32), 1, keepdims=True)
    q_ref[...] = q * gain
    k_ref[...] = k * gain
    gains_ref[...] = jnp.where(lane == 0, attend, forward / gain_ref[:, 1:2])


def weights_call(got, vw, qw, kw, gains):
    place = np.zeros((8, 128, 512), np.float32)
    for d in range(8):
        for i in range(32):
            place[d, i, 32 * d + i] = 1.0
            place[d, 32 + i, 256 + 32 * d + i] = 1.0
    n = got.shape[1]
    outs = [jax.ShapeDtypeStruct((n, c), F32) for c in (vw.shape[1], qw.shape[1], kw.shape[1], 128)]
    return pl.pallas_call(
        weights_kernel, out_shape=outs, compiler_params=pltpu.CompilerParams(vmem_limit_bytes=16 * 1024 * 1024),
        name="weights_kernel",
    )(got, jnp.asarray(place, BF16), vw, qw, kw, gains)


def row_call(kernel, pieces, ins, kinds, deps=()):
    shape = pieces[0].shape
    outs = [jax.ShapeDtypeStruct(shape, kind) for kind in kinds]

    def wrapped(*refs):
        at = 6 + len(ins)
        kernel(refs[:6], *refs[6:at], *refs[at + len(deps) :])

    return pl.pallas_call(
        wrapped,
        in_specs=[pl.BlockSpec(memory_space=pltpu.VMEM)] * (6 + len(ins))
        + [pl.BlockSpec(memory_space=pl.ANY)] * len(deps),
        out_specs=[pl.BlockSpec(memory_space=pltpu.VMEM)] * len(outs),
        out_shape=outs,
        compiler_params=pltpu.CompilerParams(vmem_limit_bytes=24 * 1024 * 1024),
        cost_estimate=cost(20 * math.prod(shape), *pieces, *ins, *outs),
        name=kernel.__name__,
    )(*pieces, *ins, *deps)


def parts_call(a, w, kind, deps=(), mib=60, pairs=(0, 1, 2, 3)):
    _, per, k = a.shape
    n, slots = len(pairs), 2 * len(pairs)
    if kind == "blocks":
        tile, depth = w.shape[2], w.shape[1]
        width = w.shape[0] * tile
        w_spec = pl.BlockSpec((1, depth, tile), lambda i: (i, 0, 0))
    elif kind == "nn":
        tile, depth, width = 512, k, w.shape[1]
        w_spec = pl.BlockSpec((k, tile), lambda i: (0, i))
    else:
        tile, depth, width = 512, k, w.shape[0]
        w_spec = pl.BlockSpec((tile, k), lambda i: (i, 0))

    def kernel(*refs):
        w_ref = refs[n]
        right = w_ref[0] if kind == "blocks" else w_ref[...]
        for slot, out_ref in enumerate(refs[-slots:]):
            left = refs[slot // 2][slot % 2, :, :depth]
            out_ref[...] = (dot_t if kind == "nt" else dot)(left, right).astype(BF16)

    out = jax.ShapeDtypeStruct((per, width), BF16)
    return pl.pallas_call(
        kernel,
        grid=(width // tile,),
        in_specs=[pl.BlockSpec((2, per, k), lambda i, p=p: (p, 0, 0)) for p in pairs]
        + [w_spec]
        + [pl.BlockSpec(memory_space=pl.ANY)] * len(deps),
        out_specs=[pl.BlockSpec((per, tile), lambda i: (0, i))] * slots,
        out_shape=far_out([out] * slots),
        compiler_params=params(mib),
        cost_estimate=cost(2 * slots * per * depth * width, w, *[out] * slots),
        name="parts_" + kind,
    )(*far_in([*[a] * n, w]), *deps)


def ordered(ref, me, lanes=slice(None)):
    return jnp.concatenate([ref[p ^ me, 0, :, lanes] for p in range(8)], 0)


def put_ordered(ref, me, value, lanes=slice(None)):
    sub = value.shape[0] // 8
    for p in range(8):
        ref[p ^ me, 0, :, lanes] = value[p * sub : (p + 1) * sub]


def phi(aligned, feat, rows):
    both = dot(aligned, feat) + rows[0:1, :]
    a, b = both[:, :FPAD], both[:, FPAD:]
    return a, b, a * b * rows[1:2, :FPAD]


def phi_back(a, b, grad, feat, rows):
    scaled = grad * rows[1:2, :FPAD]
    return dot_t((scaled * b).astype(BF16), feat[:, :FPAD]) + dot_t(
        (scaled * a).astype(BF16), feat[:, FPAD:]
    )


def put_state(ref, head, state, norm):
    ref[0, head] = state[:FROWS].astype(BF16)
    high = norm.astype(BF16)
    low = (norm - high.astype(F32)).astype(BF16)
    ref[0, head, FEAT : FEAT + 1, :] = high[:, :128]
    ref[0, head, FEAT + 1 : FEAT + 2, :] = low[:, :128]
    ref[0, head, FEAT + 2 : FEAT + 3, :] = high[:, 128:]
    ref[0, head, FEAT + 3 : FEAT + 4, :] = low[:, 128:]


def get_state(ref, head):
    whole = ref[0, head]
    state = jnp.concatenate([whole, jnp.zeros((FPAD - FROWS, 128), F32)], 0)
    norm = jnp.concatenate(
        [
            whole[FEAT : FEAT + 1] + whole[FEAT + 1 : FEAT + 2],
            whole[FEAT + 2 : FEAT + 3] + whole[FEAT + 3 : FEAT + 4],
        ],
        1,
    )
    return state.astype(BF16), norm


def align4(qk, align_ref):
    out = dot(qk, align_ref[...]).astype(BF16)
    return [out[:, i * 128 : (i + 1) * 128] for i in range(4)]


def column(seg_ref):
    row = seg_ref[0]
    return jnp.transpose(jnp.broadcast_to(row, (128, row.shape[1])))[:, 0:1]


def mask_of(seg_ref, meta_ref, which):
    at = 1 + which * pl.num_programs(0) + pl.program_id(0)
    return jnp.where(column(seg_ref) == meta_ref[at].astype(F32), 1.0, 0.0)


def visible(seg_ref):
    t = seg_ref.shape[2]
    causal = lax.broadcasted_iota(jnp.int32, (t, t), 0) >= lax.broadcasted_iota(jnp.int32, (t, t), 1)
    return causal & (column(seg_ref) == seg_ref[0])


def state_kernel(me_ref, qkv_ref, seg_ref, feat_ref, rows_ref, align_ref, out_ref):
    me = me_ref[0]
    qk = ordered(qkv_ref, me, slice(256, 384))
    v = ordered(qkv_ref, me, slice(0, 256))
    last = mask_of(seg_ref, me_ref, 1)
    parts = align4(qk, align_ref)
    for head in range(2):
        _, _, feat = phi(parts[2 + head], feat_ref[...], rows_ref[...])
        feat = feat * last
        state = t_dot(feat.astype(BF16), v[:, head * 128 : (head + 1) * 128])
        put_state(out_ref, head, state, jnp.sum(feat, 0, keepdims=True))


def intra_kernel(me_ref, qkv_ref, seg_ref, align_ref, num_ref, den_ref):
    me = me_ref[0]
    qk = ordered(qkv_ref, me, slice(256, 384))
    v = ordered(qkv_ref, me, slice(0, 256))
    see = visible(seg_ref)
    parts = align4(qk, align_ref)
    den_ref[0] = jnp.zeros(den_ref.shape[1:], F32)
    for head in range(2):
        z = dot_t(parts[head], parts[2 + head])
        w = jnp.where(see, 1.0 + z * (0.25 + 0.03125 * z), 0.0)
        num_ref[0, :, head * 128 : (head + 1) * 128] = dot(
            w.astype(BF16), v[:, head * 128 : (head + 1) * 128]
        )
        den_ref[0, :, head : head + 1] = jnp.sum(w, 1, keepdims=True)


def output_kernel(
    me_ref, qkv_ref, seg_ref, feat_ref, rows_ref, align_ref, num_ref, den_ref, state_ref, o_ref, all_ref
):
    me = me_ref[0]
    qk = ordered(qkv_ref, me, slice(256, 384))
    use = mask_of(seg_ref, me_ref, 0)
    parts = align4(qk, align_ref)
    all_ref[0] = jnp.zeros(all_ref.shape[1:], F32)
    for head in range(2):
        lanes = slice(head * 128, (head + 1) * 128)
        _, _, feat = phi(parts[head], feat_ref[...], rows_ref[...])
        state, norm = get_state(state_ref, head)
        num = num_ref[0, :, lanes] + use * dot(feat.astype(BF16), state)
        den = den_ref[0, :, head : head + 1] + use * jnp.sum(feat * norm, 1, keepdims=True)
        all_ref[0, :, head : head + 1] = den
        put_ordered(o_ref, me, (num / den).astype(BF16), lanes)


def back_parts(me, o_ref, do_ref, den_ref, head):
    lanes = slice(head * 128, (head + 1) * 128)
    inv = 1.0 / den_ref[0, :, head : head + 1]
    do = ordered(do_ref, me, lanes).astype(F32)
    o = ordered(o_ref, me, lanes).astype(F32)
    return (do * inv).astype(BF16), -jnp.sum(do * o, 1, keepdims=True) * inv


def back_state_kernel(
    me_ref, qkv_ref, seg_ref, feat_ref, rows_ref, align_ref, o_ref, do_ref, den_ref, out_ref
):
    me = me_ref[0]
    qk = ordered(qkv_ref, me, slice(256, 384))
    use = mask_of(seg_ref, me_ref, 0)
    parts = align4(qk, align_ref)
    for head in range(2):
        g, c = back_parts(me, o_ref, do_ref, den_ref, head)
        _, _, feat = phi(parts[head], feat_ref[...], rows_ref[...])
        feat = feat * use
        put_state(out_ref, head, t_dot(feat.astype(BF16), g), jnp.sum(feat * c, 0, keepdims=True))


def back_intra_kernel(
    me_ref, qkv_ref, seg_ref, feat_ref, rows_ref, align_ref, o_ref, do_ref, den_ref, state_ref,
    dq_ref, dk_ref, dv_ref,
):
    me = me_ref[0]
    qk = ordered(qkv_ref, me, slice(256, 384))
    v = ordered(qkv_ref, me, slice(0, 256))
    use = mask_of(seg_ref, me_ref, 0)
    see = visible(seg_ref)
    parts = align4(qk, align_ref)
    for head in range(2):
        lanes = slice(head * 128, (head + 1) * 128)
        g, c = back_parts(me, o_ref, do_ref, den_ref, head)
        z = dot_t(parts[head], parts[2 + head])
        w = jnp.where(see, 1.0 + z * (0.25 + 0.03125 * z), 0.0)
        dv_ref[0, :, lanes] = t_dot(w.astype(BF16), g)
        dw = dot_t(g, v[:, lanes]) + c
        dz = jnp.where(see, dw * (0.25 + 0.0625 * z), 0.0).astype(BF16)
        a, b, _ = phi(parts[head], feat_ref[...], rows_ref[...])
        state, norm = get_state(state_ref, head)
        grad = use * (dot_t(g, state) + c * norm)
        dq_ref[0, :, lanes] = dot(dz, parts[2 + head]) + phi_back(a, b, grad, feat_ref[...], rows_ref[...])
        dk_ref[0, :, lanes] = t_dot(dz, parts[head])


def back_output_kernel(
    me_ref, qkv_ref, seg_ref, feat_ref, rows_ref, align_ref, state_ref, dq_ref, dk_ref, dv_ref, inv_ref, out_ref, scaled_ref
):
    me = me_ref[0]
    qk = ordered(qkv_ref, me, slice(256, 384))
    v = ordered(qkv_ref, me, slice(0, 256))
    last = mask_of(seg_ref, me_ref, 1)
    parts = align4(qk, align_ref)
    inv = ordered(inv_ref, me)
    packed = None
    for head in range(2):
        lanes = slice(head * 128, (head + 1) * 128)
        a, b, feat = phi(parts[2 + head], feat_ref[...], rows_ref[...])
        state, norm = get_state(state_ref, head)
        grad = last * (dot_t(v[:, lanes], state) + norm)
        dk = dk_ref[0, :, lanes] + phi_back(a, b, grad, feat_ref[...], rows_ref[...])
        dv = dv_ref[0, :, lanes] + last * dot(feat.astype(BF16), state)
        put_ordered(out_ref, me, dv.astype(BF16), lanes)
        put_ordered(scaled_ref, me, (dv * inv).astype(BF16), lanes)
        place = align_ref[...]
        term = dot_t(dq_ref[0, :, lanes].astype(BF16), place[:, head * 128 : (head + 1) * 128]) + dot_t(
            dk.astype(BF16), place[:, (2 + head) * 128 : (3 + head) * 128]
        )
        packed = term if packed is None else packed + term
    put_ordered(out_ref, me, packed.astype(BF16), slice(256, 384))
    put_ordered(scaled_ref, me, (packed * inv).astype(BF16), slice(256, 384))


def attention_call(kernel, me, ins, kinds, outs, flops, deps=()):
    def spec(a, kind):
        if kind == "s":
            return pl.BlockSpec((8, 1) + a.shape[2:], lambda i, m: (0, i, 0, 0))
        rest = len(a.shape) - 1
        if kind == "q":
            return pl.BlockSpec((1,) + a.shape[1:], lambda i, m: (i,) + (0,) * rest)
        return pl.BlockSpec(a.shape, lambda i, m: (0,) * (rest + 1))

    seqs = ins[0].shape[1]
    n = 1 + len(ins)

    def wrapped(*refs):
        kernel(*refs[:n], *refs[n + len(deps) :])

    return pl.pallas_call(
        wrapped,
        out_shape=far_out([a for a, _ in outs], kernel is back_intra_kernel),
        grid_spec=pltpu.PrefetchScalarGridSpec(
            num_scalar_prefetch=1,
            grid=(seqs,),
            in_specs=[spec(a, k) for a, k in zip(ins, kinds)] + [pl.BlockSpec(memory_space=pl.ANY)] * len(deps),
            out_specs=[spec(a, k) for a, k in outs],
        ),
        compiler_params=params(28),
        cost_estimate=cost(flops, *ins, *[a for a, _ in outs]),
        name=kernel.__name__,
    )(me, *far_in(ins), *deps)


def pick(cond, a, b):
    return jnp.where(cond, a, b)


def half_columns(gate, up, which, n_main, n_mid):
    mid = slice(n_main, n_main + 2 * n_mid)
    main = slice(0, n_main) if which == 0 else slice(n_main + 2 * n_mid, None)
    part = slice(0, n_mid) if which == 0 else slice(n_mid, None)
    return jnp.concatenate([gate[:, main], up[:, main], gate[:, mid][:, part], up[:, mid][:, part]], 1)


def body(inputs, segments, qw, kw, vw, pw, again, gw, uw, dw, fgain, upstream):
    hi, core, row, col = (lax.axis_index(a) for a in ("hi", "core", "row", "col"))
    rows = lax.axis_size("row")
    shards = 2 * rows
    seqs, sub = inputs.shape[0], inputs.shape[3]
    tokens = seqs * sub
    span = 8 * sub
    n_rows = qw.shape[0]
    is0 = col == 0
    ff = gw.shape[1]
    half_ff = ff // 2
    n_mid = 64
    n_main = half_ff - n_mid
    feat_c, rows_c, align_c = feature_constants()
    sds = jax.ShapeDtypeStruct
    x = inputs.reshape(tokens, D)

    shard_pairs = [(s, (s % rows) * 2 + s // rows) for s in range(shards)]
    moved = lax.ppermute(pw, ("row", "col"), shard_pairs)

    gain_one = again.astype(F32)[:, None]
    seg_own = segments.reshape(seqs, 4 * sub)

    def by_dest(w, scale):
        return (w.astype(F32) * scale).astype(BF16).reshape(n_rows, 8, -1)

    lane = lax.broadcasted_iota(jnp.int32, (n_rows, PAYLOAD - 320), 1)
    ends = jnp.pad(seg_own[:, -1], (0, n_rows - seqs)).astype(F32)[:, None]
    tens = jnp.floor(ends * (1.0 / 128.0))
    extra = jnp.where(
        lane == 0,
        fgain.astype(F32)[:, None],
        jnp.where(lane == 1, tens, jnp.where(lane == 2, ends - 128.0 * tens, 0.0)),
    ).astype(BF16)
    payload = jnp.concatenate(
        [
            by_dest(vw, gain_one),
            by_dest(qw, gain_one),
            by_dest(kw, gain_one),
            jnp.broadcast_to(extra[:, None], (n_rows, 8, PAYLOAD - 320)),
        ],
        2,
    ).transpose(1, 0, 2)
    payload = lax.all_to_all(payload, GROUP, split_axis=0, concat_axis=0, tiled=True)
    x_own = after(x, payload)
    xs = gather8(x_own)
    w_proj = lax.all_gather(moved, "row", axis=0, tiled=True)
    gathered = lax.all_gather(after(payload, moved), "row", axis=0, tiled=False)
    lasts = gathered[:, 1, :seqs, 321:323].astype(F32)
    lasts = (lasts[:, :, 0] * 128.0 + lasts[:, :, 1]).astype(jnp.int32)

    seg_other = swap(seg_own, "col")
    seg = jnp.concatenate([pick(is0, seg_own, seg_other), pick(is0, seg_other, seg_own)], 1)
    seg_row = seg.astype(F32)[:, None, :]
    before = jnp.where(row > 0, lasts[jnp.maximum(row - 1, 0)], -1)
    here = lasts[row]
    me3 = (4 * col + 2 * hi + core).astype(jnp.int32)
    meta = jnp.concatenate([me3[None], before, here])

    ends = jnp.concatenate([lasts, jnp.full((1, seqs), -1, jnp.int32)])

    def end_of(r):
        return ends[jnp.where((r >= 0) & (r < rows), r, rows)]

    def same(r, other):
        return ((end_of(r) == other) & (r >= 0) & (r < rows)).astype(F32)

    every = 8 * tokens
    qkv, inv, w_qkv = slot_call(
        qkv_kernel, xs, [(gathered.reshape(rows, 4, 2 * n_rows, PAYLOAD), False)],
        [sds((8, tokens, PAYLOAD), BF16), sds((8, tokens, 128), F32)], 2 * every * D * PAYLOAD,
        deps=[seg_row], whole=[sds((D, PAYLOAD), BF16)],
    )
    gain_two = w_qkv[:, 320].astype(F32)[None, :]
    inv = inv.reshape(8, seqs, sub, 128)
    ups = gather8(after(upstream.reshape(tokens, D), qkv))
    qkv = qkv.reshape(8, seqs, sub, PAYLOAD)
    st = sds((seqs, 2, FROWS, 128), BF16)
    near = 4 * seqs * span * span * 160
    far = 4 * seqs * span * FPAD * 300
    (state,) = attention_call(
        state_kernel, meta, [qkv, seg_row, feat_c, rows_c, align_c], "sqccc", [(st, "q")], far
    )
    mine = pick(is0, half_columns(gw, uw, 0, n_main, n_mid), half_columns(gw, uw, 1, n_main, n_mid))
    theirs = pick(is0, half_columns(gw, uw, 1, n_main, n_mid), half_columns(gw, uw, 0, n_main, n_mid))
    got = swap(after(theirs, xs[6][0], xs[7][0]), "col")
    got = after(got, state)
    gu_rows = jnp.concatenate([pick(is0, mine, got), pick(is0, got, mine)], 0)
    w_gu = lax.all_gather(gu_rows, "row", axis=0, tiled=True)
    down0 = dw[: n_main + n_mid]
    down1 = jnp.concatenate([dw[n_main + 2 * n_mid :], dw[n_main + n_mid : n_main + 2 * n_mid]], 0)
    d_mine, d_theirs = pick(is0, down0, down1), pick(is0, down1, down0)
    d_got = swap(after(d_theirs, got), "col")
    d_cols = jnp.stack([pick(is0, d_mine, d_got), pick(is0, d_got, d_mine)])
    w_down = lax.all_gather(d_cols, "row", axis=0, tiled=True)
    fold = shards // 8
    w_down = (
        w_down.reshape(8, fold, half_ff, D // shards).transpose(0, 2, 1, 3).reshape(8, half_ff, D // 8)
    )

    num, den_in = attention_call(
        intra_kernel, meta, [qkv, seg_row, align_c], "sqc",
        [(sds((seqs, span, 256), F32), "q"), (sds((seqs, span, 8), F32), "q")], near,
    )
    forth = walk_steps(state, lambda d: same(row - d, here), lambda d: same(row - d, before), True)
    _, came = next(forth)
    came, num, den_in = meet(came, num, den_in)
    state_in = finish(forth, came)
    o, den = attention_call(
        output_kernel, meta, [qkv, seg_row, feat_c, rows_c, align_c, num, den_in, state_in], "sqcccqqq",
        [(sds((8, seqs, sub, 256), BF16), "s"), (sds((seqs, span, 8), F32), "q")], far,
        [ups[6][0], ups[7][0], d_got],
    )
    o_rows = o.reshape(8, tokens, 256)
    residual, a2_own = row_call(
        residual_kernel, scatter8(parts_call(o_rows, w_proj, "nn", mib=28)), [x, gain_two], [F32, BF16]
    )

    ff_flops = 2 * every * D * half_ff
    steps = gather_steps(a2_own)
    wide = [
        sds((8, tokens, ff), BF16),
        sds((8, tokens, half_ff + n_mid), BF16),
        sds((8, half_ff + n_mid, tokens), BF16),
    ]
    hidden = slot_call(ffn_in_kernel, next(steps), [(w_gu, False)], wide, 2 * ff_flops, slots=(0, 2))
    hidden = slot_call(
        ffn_in_kernel, steps.send(hidden[:1]), [(w_gu, False)], wide, 2 * ff_flops, slots=(2, 6), into=hidden
    )
    a2 = finish(steps, hidden[:1])
    gu, h, h_turned = slot_call(
        ffn_in_kernel, a2, [(w_gu, False)], wide, 2 * ff_flops, slots=(6, 8), into=hidden
    )
    (down_g,) = grad_call(
        down_grad_kernel, ups, 256, [h_turned], [],
        [(sds((8, half_ff, 256), BF16), (1, half_ff, 256), lambda i: (i, 0, 0))], ff_flops,
    )
    late = {}

    def ffn_back(slots, into, deps=()):
        return slot_call(
            ffn_back_kernel, ups, [(w_down, False), (gu, True)], [sds((8, tokens, ff), BF16)], ff_flops, deps,
            slots=slots, into=into,
        )[0]

    half = tokens // 2
    dgu = ffn_back((0, 8), (), [down_g])
    own, other, y, yc, x_, xc, xy, xyc = parts_call(dgu, w_gu, "nt")
    other, yc, xc, xyc = (swap(part, "core") for part in (other, yc, xc, xyc))
    to_x = pair_sum(xy, xyc, 0, half).astype(BF16)
    to_y = pair_sum(xy, xyc, half, tokens).astype(BF16)
    near_x = pair_sum(x_, xc, 0, half).astype(BF16)
    near_y = pair_sum(y, yc, half, tokens).astype(BF16)
    down_g = (
        down_g.reshape(8, half_ff, fold, D // shards).transpose(0, 2, 1, 3).reshape(shards * half_ff, -1)
    )
    down_g = lax.psum_scatter(down_g, "row", scatter_dimension=0, tiled=True)
    block = D // shards
    gu_gs, gains = [], []

    def gu_half(x_bit):
        def run(sent):
            one, gain = grad_call(
                gu_grad_kernel, a2, 256, [dgu], [(w_gu, (256, ff), lambda i: (2 * i + x_bit, 0))],
                [
                    (sds((D // 2, ff), BF16), (256, ff), lambda i: (i, 0)),
                    (sds((D // 2, 128), F32), (256, 128), lambda i: (i, 0)),
                ],
                ff_flops, lambda i: 2 * i + x_bit, 4, sent,
            )
            gu_gs.append(one)
            gains.append(gain)
            return [one]

        return run

    gu_half(0)([to_x, to_y, near_x, near_y])
    from_x, from_y, first_x, first_y, gu_gs[0] = meet(
        swap(to_x, "col"), swap(to_y, "hi"), swap(near_x, "col"), swap(near_y, "hi"), gu_gs[0]
    )
    far_x = (pair_sum(x_, xc, half, tokens) + from_y.astype(F32)).astype(BF16)
    far_y = (pair_sum(y, yc, 0, half) + from_x.astype(F32)).astype(BF16)
    gu_half(1)([far_x, far_y, gu_gs[0]])
    last_x, last_y, gu_gs[1] = meet(swap(far_x, "col"), swap(far_y, "hi"), gu_gs[1])
    grad_r, datt_own = row_call(
        residual_back_kernel, [own, other, first_x, last_y, last_x, first_y],
        [upstream.reshape(tokens, D), residual, gain_two], [F32, BF16],
    )
    over_x, over_y, over_c, *down_parts = meet(
        swap(datt_own, "col"), swap(datt_own, "hi"), swap(datt_own, "core"),
        *parts_call(h, w_down, "blocks", [datt_own]),
    )
    to_x, to_y = over_y[:half], over_x[half:]
    over_yc, over_xc = swap(over_y, "core"), swap(over_x, "core")
    datt = [(datt_own, 0, 0), (over_c, 1, 0), (over_y, 2, 0), (over_yc, 3, 0), (over_x, 4, 0), (over_xc, 5, 0)]
    do_out = [sds((8, tokens, 256), BF16)]
    do_flops = 2 * every * D * 256
    (do,) = slot_call(do_kernel, datt, [(w_proj, False)], do_out, do_flops, [to_x, to_y], slots=(0, 6))
    top, low, do = meet(swap(to_x, "col"), swap(to_y, "hi"), do)
    datt += [(top, 6, 0), (low, 6, half), (swap(top, "core"), 7, 0), (swap(low, "core"), 7, half)]
    (do,) = slot_call(do_kernel, datt, [(w_proj, False)], do_out, do_flops, [down_g], slots=(6, 8), into=[do])
    gain_part = jnp.stack([g.reshape(4, 256, 128) for g in gains], 1).reshape(D, 128)
    if fold > 1:
        natural = jnp.stack([g.reshape(4, 256, ff) for g in gu_gs], 1)
        by_col = natural.reshape(rows, 2, block, ff).transpose(1, 0, 2, 3)
        gu_gs = [by_col[0].reshape(D // 2, ff), by_col[1].reshape(D // 2, ff)]
    gu_r = [lax.psum_scatter(g, "row", scatter_dimension=0, tiled=True) for g in gu_gs]

    do = do.reshape(8, seqs, sub, 256)

    (dstate,) = attention_call(
        back_state_kernel, meta, [qkv, seg_row, feat_c, rows_c, align_c, o, do, den], "sqcccssq",
        [(st, "q")], far,
    )
    part = sds((seqs, span, 256), F32)

    back = walk_steps(
        dstate,
        lambda d: same(row + d - 1, before) * (row + d < rows),
        lambda d: same(row + d - 1, here) * (row + d < rows),
        False,
    )
    _, came = next(back)
    own, other, y, yc, x_, xc, xy, xyc = down_parts
    other, yc, xc, xyc = (after(swap(part, "core"), dstate) for part in (other, yc, xc, xyc))
    to_x = pair_sum(xy, xyc, 0, half).astype(BF16)
    to_y = pair_sum(xy, xyc, half, tokens).astype(BF16)
    near_x = pair_sum(x_, xc, 0, half).astype(BF16)
    near_y = pair_sum(y, yc, half, tokens).astype(BF16)
    intra = attention_call(
        back_intra_kernel, meta, [qkv, seg_row, feat_c, rows_c, align_c, o, do, den, state_in],
        "sqcccssqq", [(part, "q")] * 3, 3 * near + far, [dstate, to_x, to_y, near_x, near_y, gu_r[0]],
    )
    dq, dk, dv = intra
    came, from_x, from_y, first_x, first_y, dq = meet(
        came, swap(to_x, "col"), swap(to_y, "hi"), swap(near_x, "col"), swap(near_y, "hi"), dq
    )
    far_x = (pair_sum(x_, xc, half, tokens) + from_y.astype(F32)).astype(BF16)
    far_y = (pair_sum(y, yc, 0, half) + from_x.astype(F32)).astype(BF16)
    step = back.send(came)
    now = None
    if step is not None:
        now, came = step
    (proj_g,) = grad_call(
        proj_grad_kernel, datt, 1024, [o_rows], [],
        [(sds((256, D), BF16), (256, 1024), lambda i: (0, i))], 2 * every * D * 256, deps=[far_x, far_y, now], mib=24,
    )
    down_r = down_g.reshape(2, half_ff, D // shards)
    d_keep, d_send = pick(is0, down_r[0], down_r[1]), pick(is0, down_r[1], down_r[0])
    g_keep = pick(is0, gu_r[0], gu_r[1])
    g_send = pick(is0, gu_r[1], gu_r[0])
    came, last_x, last_y, d_got, proj_g = meet(
        came, swap(far_x, "col"), swap(far_y, "hi"), swap(d_send, "col"), proj_g
    )
    (outputs,) = row_call(
        output_rows_kernel, [own, other, first_x, last_y, last_x, first_y], [residual], [BF16]
    )
    dstate_out = finish(back, came)
    proj_r = lax.psum_scatter(proj_g, "row", scatter_dimension=0, tiled=True)
    row_out = sds((8, seqs, sub, PAYLOAD), BF16)
    dqkv, scaled = attention_call(
        back_output_kernel, meta, [qkv, seg_row, feat_c, rows_c, align_c, dstate_out, dq, dk, dv, inv],
        "sqcccqqqqs", [(row_out, "s")] * 2, 2 * far, [outputs, gu_r[1]],
    )

    def qkv_side(sent):
        (late["qkv"],) = grad_call(
            qkv_grad_kernel, xs, 512, [scaled.reshape(8, tokens, PAYLOAD)],
            [(gain_part, (512, 128), lambda i: (i, 0))],
            [
                (
                    sds((rows, 4, 2 * n_rows, PAYLOAD), BF16),
                    (rows, 1, 2 * n_rows, PAYLOAD),
                    lambda i: (0, i, 0, 0),
                )
            ],
            2 * every * D * PAYLOAD, deps=sent, mib=24,
        )
        return [late["qkv"]]

    qkv_g = qkv_side([proj_r])[0]
    own, other, y, yc, x_, xc, xy, xyc = parts_call(
        dqkv.reshape(8, tokens, PAYLOAD), w_qkv, "nt", [qkv_g], 28
    )
    other, yc, xc, xyc = (swap(part, "core") for part in (other, yc, xc, xyc))
    to_x = pair_sum(xy, xyc, 0, half).astype(BF16)
    to_y = pair_sum(xy, xyc, half, tokens).astype(BF16)
    near_x = pair_sum(x_, xc, 0, half).astype(BF16)
    near_y = pair_sum(y, yc, half, tokens).astype(BF16)
    from_x, from_y, first_x, first_y = (
        swap(to_x, "col"), swap(to_y, "hi"), swap(near_x, "col"), swap(near_y, "hi")
    )
    far_x = (pair_sum(x_, xc, half, tokens) + from_y.astype(F32)).astype(BF16)
    far_y = (pair_sum(y, yc, 0, half) + from_x.astype(F32)).astype(BF16)
    g_got = swap(after(g_send, far_x), "col")
    f_pieces = [own, other, first_x, swap(far_y, "hi"), swap(far_x, "col"), first_y]
    qkv_g = lax.psum_scatter(qkv_g.reshape(D, PAYLOAD), "row", scatter_dimension=0, tiled=True)
    project_grad = lax.ppermute(
        after(proj_r, qkv_g), ("row", "col"), [(b, a) for a, b in shard_pairs]
    ).astype(F32)
    qkv_g = lax.all_to_all(
        qkv_g.reshape(8, n_rows, PAYLOAD), GROUP, split_axis=0, concat_axis=0, tiled=True
    )
    (inputs_grad,) = row_call(input_back_kernel, f_pieces, [x, grad_r], [F32], [qkv_g])
    v_g, q_g, k_g, both_gains = weights_call(
        qkv_g, vw, qw, kw, jnp.stack([again.astype(F32), fgain.astype(F32)], 1)
    )
    attend_grad, forward_grad = both_gains[:, 0], both_gains[:, 1]
    d0, d1 = pick(is0, d_keep, d_got).astype(F32), pick(is0, d_got, d_keep).astype(F32)
    down_grad = jnp.concatenate([d0, d1[n_main:], d1[:n_main]], 0)
    g0, g1 = pick(is0, g_keep, g_got).astype(F32), pick(is0, g_got, g_keep).astype(F32)
    m = 2 * n_main
    gate_grad = jnp.concatenate(
        [g0[:, :n_main], g0[:, m : m + n_mid], g1[:, m : m + n_mid], g1[:, :n_main]], 1
    )
    up_grad = jnp.concatenate(
        [g0[:, n_main:m], g0[:, m + n_mid :], g1[:, m + n_mid :], g1[:, n_main:m]], 1
    )
    return (
        outputs.reshape(inputs.shape),
        inputs_grad.reshape(inputs.shape),
        q_g,
        k_g,
        v_g,
        project_grad,
        attend_grad,
        gate_grad,
        up_grad,
        down_grad,
        forward_grad,
    )


def solution(mesh):
    heads, shards = mesh.devices.shape
    fine = Mesh(mesh.devices.reshape(heads // 2, 2, shards // 2, 2), ("hi", "core", "row", "col"))
    h, s = ("hi", "core"), ("row", "col")
    every = P(h + s)
    tokens = P(None, s, h)
    return jax.shard_map(
        body,
        mesh=fine,
        in_specs=(
            tokens, P(None, s), every, every, every, every, every, P(s, h), P(s, h), P(h, s), every, tokens,
        ),
        out_specs=(
            tokens, tokens, every, every, every, every, every, P(s, h), P(s, h), P(h, s), every,
        ),
        check_vma=False,
    )
```

```python
import math

import numpy as np

import jax
import jax.numpy as jnp
from jax import lax
from jax.experimental import pallas as pl
from jax.experimental.pallas import tpu as pltpu
from jax.sharding import Mesh
from jax.sharding import PartitionSpec as P

D = 2048
HEADS = 16
QK = 16
VD = 128
EPS = 1e-05
F32 = jnp.float32
BF16 = jnp.bfloat16
GROUP = ("hi", "core", "col")
FEAT = 1 + QK + QK * (QK + 1) // 2
FPAD = 256
FROWS = 160
PAYLOAD = 384


def feature_constants():
    left = np.zeros((128, FPAD), np.float32)
    right = np.zeros((128, FPAD), np.float32)
    rows = np.zeros((8, 2 * FPAD), np.float32)
    at = 0
    for i in range(QK):
        for j in range(i, QK):
            left[i, at] = 1.0
            right[j, at] = 1.0
            rows[1, at] = (1.0 if i == j else math.sqrt(2.0)) / math.sqrt(2.0 * QK)
            at += 1
    for i in range(QK):
        left[i, at] = 1.0
        rows[0, FPAD + at] = 1.0
        rows[1, at] = QK ** (-0.25)
        at += 1
    rows[0, at] = 1.0
    rows[0, FPAD + at] = 1.0
    rows[1, at] = 1.0
    align = np.zeros((4, 128, 128), np.float32)
    for part in range(4):
        for i in range(QK):
            align[part, part * QK + i, i] = 1.0
    return (
        jnp.asarray(np.concatenate([left, right], 1), BF16),
        jnp.asarray(rows, F32),
        jnp.asarray(align.transpose(1, 0, 2).reshape(128, 512), BF16),
    )


def dot(a, b):
    return jnp.dot(a, b, preferred_element_type=F32)


def dot_t(a, b):
    return lax.dot_general(a, b, (((1,), (1,)), ((), ())), preferred_element_type=F32)


def t_dot(a, b):
    return lax.dot_general(a, b, (((0,), (0,)), ((), ())), preferred_element_type=F32)


def swap(value, axis):
    return lax.ppermute(value, axis, [(0, 1), (1, 0)])


def after(value, *others):
    if not others:
        return value

    def gate(*refs):
        pass

    return pl.pallas_call(
        gate,
        in_specs=[pl.BlockSpec(memory_space=pl.ANY)] * (1 + len(others)),
        out_specs=pl.BlockSpec(memory_space=pl.ANY),
        out_shape=jax.ShapeDtypeStruct(value.shape, value.dtype),
        input_output_aliases={0: 0},
        cost_estimate=pl.CostEstimate(flops=0, transcendentals=0, bytes_accessed=0),
        name="gate",
    )(value, *others)


def meet(*values):
    def gate(*refs):
        pass

    return pl.pallas_call(
        gate,
        in_specs=[pl.BlockSpec(memory_space=pl.ANY)] * len(values),
        out_specs=[pl.BlockSpec(memory_space=pl.ANY)] * len(values),
        out_shape=[jax.ShapeDtypeStruct(v.shape, v.dtype) for v in values],
        input_output_aliases={i: i for i in range(len(values))},
        cost_estimate=pl.CostEstimate(flops=0, transcendentals=0, bytes_accessed=0),
        name="meet",
    )(*values)


def gather_steps(own):
    half = own.shape[0] // 2
    over_x = swap(own, "col")
    over_y = swap(own, "hi")
    rows = [(own, 0, 0), (swap(own, "core"), 1, 0)]
    done = yield rows
    over_x, over_y = after(over_x, *done), after(over_y, *done)
    top = swap(over_y[:half], "col")
    low = swap(over_x[half:], "hi")
    near = [(over_y, 2, 0), (swap(over_y, "core"), 3, 0), (over_x, 4, 0), (swap(over_x, "core"), 5, 0)]
    done = yield near
    top, low = after(top, *done), after(low, *done)
    far = [(top, 6, 0), (low, 6, half), (swap(top, "core"), 7, 0), (swap(low, "core"), 7, half)]
    return rows + near + far


def gather8(own):
    steps = gather_steps(own)
    next(steps)
    return finish(steps)


def scatter_steps(parts):
    def both(one, two, start, end):
        return one[start:end].astype(F32) + two[start:end].astype(F32)

    own, other, y, yc, x, xc, xy, xyc = parts
    n = xy.shape[0]
    half = n // 2
    xyc = swap(xyc, "core")
    xc = swap(xc, "core")
    yc = swap(yc, "core")
    other = swap(other, "core")
    to_x = both(xy, xyc, 0, half).astype(BF16)
    to_y = both(xy, xyc, half, n).astype(BF16)
    near_x = both(x, xc, 0, half).astype(BF16)
    near_y = both(y, yc, half, n).astype(BF16)
    from_x, from_y = swap(to_x, "col"), swap(to_y, "hi")
    first_x, first_y = swap(near_x, "col"), swap(near_y, "hi")
    done = yield [to_x, to_y, near_x, near_y]
    from_x, from_y = after(from_x, *done), after(from_y, *done)
    far_x = (both(x, xc, half, n) + from_y.astype(F32)).astype(BF16)
    far_y = (both(y, yc, 0, half) + from_x.astype(F32)).astype(BF16)
    last_x, last_y = swap(far_x, "col"), swap(far_y, "hi")
    done = yield [far_x, far_y]
    last_x, last_y = after(last_x, *done), after(last_y, *done)
    return own, other, first_x, last_y, last_x, first_y


def walk_steps(value, linked, joined, up):
    rows = lax.axis_size("row")
    total = None
    now = value
    step = 1
    while step < rows:
        pairs = [(i, i + step) if up else (i + step, i) for i in range(rows - step)]
        came = lax.ppermute(now, "row", pairs)
        wide = (yield now, came).astype(F32)
        term = joined(step)[:, None, None, None] * wide
        total = term if total is None else total + term
        if 2 * step < rows:
            now = (now.astype(F32) + linked(step)[:, None, None, None] * wide).astype(BF16)
        step = 2 * step
    return total


def finish(steps, done=()):
    try:
        step = steps.send(done)
        while True:
            step = steps.send(step[1] if isinstance(step, tuple) else ())
    except StopIteration as end:
        return end.value


def pair_sum(one, two, start, end):
    return one[start:end].astype(F32) + two[start:end].astype(F32)


def scatter8(parts, *kernels):
    steps = scatter_steps(parts)
    sent = next(steps)
    for i, kernel in enumerate(kernels):
        done = kernel(sent)
        if i == 1:
            return finish(steps, done)
        sent = steps.send(done)
    return finish(steps)


def far_in(values):
    return [pltpu.with_memory_space_constraint(v, pltpu.HBM) if math.prod(v.shape) >= 65536 else v for v in values]


def far_out(shapes, far=False):
    if not far:
        return list(shapes)
    return [pltpu.HBM(a.shape, a.dtype) if math.prod(a.shape) >= 65536 else a for a in shapes]


def params(mib=60):
    return pltpu.CompilerParams(dimension_semantics=("arbitrary",), vmem_limit_bytes=mib * 1024 * 1024)


def cost(flops, *arrays):
    return pl.CostEstimate(
        flops=int(flops),
        transcendentals=0,
        bytes_accessed=int(sum(math.prod(a.shape) * a.dtype.itemsize for a in arrays)),
    )


def slot_call(kernel, pieces, ins, outs, flops, deps=(), whole=(), slots=(0, 8), into=(), mib=60):
    first, count = slots[0], slots[1] - slots[0]
    pieces = [p for p in pieces if slots[0] <= p[1] < slots[1]]
    n = len(pieces)
    per, width = outs[0].shape[1], pieces[0][0].shape[1]
    extra = list(deps) + list(into)

    def wrapped(*refs):
        rows = refs[:n]
        at = n + len(ins)
        rest = refs[n:at] + refs[at + len(extra) : at + len(extra) + len(outs) + len(whole)]
        buf, sem = refs[-2:]
        i = pl.program_id(0)

        @pl.when(i == 0)
        def _():
            for (a, slot, start), ref in zip(pieces, rows):
                there = buf.at[slot - first, pl.ds(start, a.shape[0])]
                pltpu.make_async_copy(ref, there, sem.at[slot - first]).start()

        pltpu.make_async_copy(buf.at[i], buf.at[i], sem.at[i]).wait()
        kernel(buf.at[i], *rest)

    def spec(a, by_slot):
        rest = len(a.shape) - 1
        if by_slot:
            return pl.BlockSpec((None,) + a.shape[1:], lambda i: (i + first,) + (0,) * rest)
        return pl.BlockSpec(a.shape, lambda i: (0,) * (rest + 1))

    at = n + len(ins) + len(deps)
    return pl.pallas_call(
        wrapped,
        grid=(count,),
        in_specs=[pl.BlockSpec(memory_space=pltpu.HBM)] * n
        + [spec(a, k) for a, k in ins]
        + [pl.BlockSpec(memory_space=pl.ANY)] * len(extra),
        out_specs=[spec(a, True) for a in outs] + [spec(a, False) for a in whole],
        out_shape=far_out(list(outs) + list(whole)),
        scratch_shapes=[pltpu.VMEM((count, per, width), BF16), pltpu.SemaphoreType.DMA((count,))],
        input_output_aliases={at + i: i for i in range(len(into))},
        compiler_params=params(mib),
        cost_estimate=cost(
            flops * count // 8, *[a for a, _, _ in pieces], *[a for a, k in ins if not k], *outs[:count // 4], *whole
        ),
        name=kernel.__name__,
    )(*[a for a, _, _ in pieces], *far_in([a for a, _ in ins]), *extra)


def grad_call(kernel, pieces, tile, whole, ins, outs, flops, index=lambda i: i, steps=None, deps=(), mib=60):
    n = len(pieces)
    width = pieces[0][0].shape[1]
    places = [(slot, start, a.shape[0]) for a, slot, start in pieces]

    def wrapped(*refs):
        at = n + len(whole) + len(ins)
        kernel(list(zip(refs[:n], places)), *refs[n:at], *refs[at + len(deps) :])

    def fixed(a):
        rest = len(a.shape)
        return pl.BlockSpec(a.shape, lambda i: (0,) * rest)

    return pl.pallas_call(
        wrapped,
        grid=(steps or width // tile,),
        in_specs=[pl.BlockSpec((a.shape[0], tile), lambda i: (0, index(i))) for a, _, _ in pieces]
        + [fixed(a) for a in whole]
        + [pl.BlockSpec(block, where) for _, block, where in ins]
        + [pl.BlockSpec(memory_space=pl.ANY)] * len(deps),
        out_specs=[pl.BlockSpec(block, where) for _, block, where in outs],
        out_shape=far_out([a for a, _, _ in outs]),
        compiler_params=params(mib),
        cost_estimate=cost(
            flops, *[a for a, _, _ in pieces], *whole, *[a for a, _, _ in ins], *[a for a, _, _ in outs]
        ),
        name=kernel.__name__,
    )(*far_in([*[a for a, _, _ in pieces], *whole, *[a for a, _, _ in ins]]), *deps)


def summed(rows, right):
    total = None
    for ref, (slot, start, n) in rows:
        term = t_dot(ref[...], right[slot, start : start + n, :])
        total = term if total is None else total + term
    return total


def qkv_kernel(x_ref, given_ref, qkv_ref, inv_ref, w_ref):
    @pl.when(pl.program_id(0) == 0)
    def _():
        rows, groups, n, _ = given_ref.shape
        for g in range(groups):
            for r in range(rows):
                w_ref[pl.ds((g * rows + r) * n, n), :] = given_ref[r, g]

    x = x_ref[...]
    wide = x.astype(F32)
    inv = lax.rsqrt(jnp.sum(wide * wide, 1, keepdims=True) * (1.0 / x.shape[1]) + EPS)
    qkv_ref[...] = (dot(x, w_ref[...]) * inv).astype(BF16)
    inv_ref[...] = jnp.broadcast_to(inv, inv_ref.shape)


def ffn_in_kernel(a_ref, w_ref, gu_ref, h_ref, turned_ref):
    gu = dot(a_ref[...], w_ref[...])
    gu_ref[...] = gu.astype(BF16)
    m = (gu.shape[1] - 128) // 2
    g, u = gu[:, :m], gu[:, m : 2 * m]
    h_ref[:, :m] = (g * jax.nn.sigmoid(g) * u).astype(BF16)
    g = gu[:, 2 * m :]
    u = pltpu.roll(g, 64, 1)
    first = lax.broadcasted_iota(jnp.int32, g.shape, 1) < 64
    h_ref[:, m:] = jnp.where(first, g * jax.nn.sigmoid(g) * u, 0.0).astype(BF16)
    turned_ref[...] = jnp.transpose(h_ref[...])


def ffn_back_kernel(up_ref, w_ref, gu_ref, out_ref):
    up = up_ref[...]
    total = None
    for i in range(8):
        term = dot_t(up[:, i * 256 : (i + 1) * 256], w_ref[i])
        total = term if total is None else total + term
    m = total.shape[1] - 64

    def both(g, u, dh):
        s = jax.nn.sigmoid(g)
        return dh * u * (s * (1.0 + g * (1.0 - s))), dh * (g * s)

    gu = gu_ref[...].astype(F32)
    dg, du = both(gu[:, :m], gu[:, m : 2 * m], total[:, :m])
    out_ref[:, :m] = dg.astype(BF16)
    out_ref[:, m : 2 * m] = du.astype(BF16)
    mid = gu[:, 2 * m :]
    other = pltpu.roll(mid, 64, 1)
    first = lax.broadcasted_iota(jnp.int32, mid.shape, 1) < 64
    dh = jnp.concatenate([total[:, m:], total[:, m:]], 1)
    dg, du = both(jnp.where(first, mid, other), jnp.where(first, other, mid), dh)
    out_ref[:, 2 * m :] = jnp.where(first, dg, du).astype(BF16)


def down_grad_kernel(rows, h_ref, out_ref):
    total = None
    for ref, (slot, start, n) in rows:
        term = dot(h_ref[slot, : out_ref.shape[1], start : start + n], ref[...])
        total = term if total is None else total + term
    out_ref[0] = total.astype(BF16)


def gu_grad_kernel(rows, right_ref, w_ref, out_ref, gain_ref):
    total = summed(rows, right_ref)
    out_ref[...] = total.astype(BF16)
    gain_ref[...] = jnp.broadcast_to(
        jnp.sum(total * w_ref[...].astype(F32), 1, keepdims=True), gain_ref.shape
    )


def do_kernel(d_ref, w_ref, out_ref):
    out_ref[...] = dot_t(d_ref[...], w_ref[...]).astype(BF16)


def proj_grad_kernel(rows, o_ref, out_ref):
    total = None
    for ref, (slot, start, n) in rows:
        term = t_dot(o_ref[slot, start : start + n, :], ref[...])
        total = term if total is None else total + term
    out_ref[...] = total.astype(BF16)


def qkv_grad_kernel(rows, right_ref, gain_ref, out_ref):
    total = summed(rows, right_ref)
    lane = lax.broadcasted_iota(jnp.int32, (1, 128), 1)
    total = jnp.concatenate([total[:, :256], jnp.where(lane == 64, gain_ref[...], total[:, 256:])], 1)
    out_ref[...] = total.astype(BF16).reshape(out_ref.shape)


def row_sum(refs):
    own, other, first_x, last_y, last_x, first_y = [ref[...].astype(F32) for ref in refs]
    return own + other + jnp.concatenate([first_x + last_y, last_x + first_y], 0)


def scaled_rows(rows):
    inv = lax.rsqrt(jnp.sum(rows * rows, 1, keepdims=True) * (1.0 / rows.shape[1]) + EPS)
    return rows * inv, inv


def norm_back(normed, inv, grad):
    return inv * (grad - normed * (jnp.sum(grad * normed, 1, keepdims=True) * (1.0 / grad.shape[1])))


def residual_kernel(refs, x_ref, gain_ref, sum_ref, a_ref):
    rows = x_ref[...].astype(F32) + row_sum(refs)
    sum_ref[...] = rows
    a_ref[...] = (scaled_rows(rows)[0] * gain_ref[...]).astype(BF16)


def output_rows_kernel(refs, sum_ref, out_ref):
    out_ref[...] = (sum_ref[...] + row_sum(refs)).astype(BF16)


def residual_back_kernel(refs, up_ref, sum_ref, gain_ref, grad_ref, low_ref):
    normed, inv = scaled_rows(sum_ref[...])
    grad = up_ref[...].astype(F32) + norm_back(normed, inv, row_sum(refs) * gain_ref[...])
    grad_ref[...] = grad
    low_ref[...] = grad.astype(BF16)


def input_back_kernel(refs, x_ref, grad_ref, out_ref):
    normed, inv = scaled_rows(x_ref[...].astype(F32))
    out_ref[...] = grad_ref[...] + norm_back(normed, inv, row_sum(refs))


def weights_kernel(got_ref, place_ref, vw_ref, qw_ref, kw_ref, gain_ref, v_ref, q_ref, k_ref, gains_ref):
    gain = gain_ref[:, 0:1]
    attend = jnp.zeros(gain.shape, F32)
    forward = jnp.zeros(gain.shape, F32)
    heads = None
    lane = lax.broadcasted_iota(jnp.int32, (1, 128), 1)
    for d in range(8):
        lanes = slice(256 * d, 256 * (d + 1))
        part = got_ref[d, :, :256].astype(F32)
        attend = attend + jnp.sum(part * vw_ref[:, lanes].astype(F32), 1, keepdims=True)
        v_ref[:, lanes] = part * gain
        tail = got_ref[d, :, 256:]
        forward = forward + jnp.sum(jnp.where(lane == 64, tail.astype(F32), 0.0), 1, keepdims=True)
        term = dot(tail, place_ref[d])
        heads = term if heads is None else heads + term
    q, k = heads[:, :256], heads[:, 256:]
    attend = attend + jnp.sum(q * qw_ref[...].astype(F32) + k * kw_ref[...].astype(F32), 1, keepdims=True)
    q_ref[...] = q * gain
    k_ref[...] = k * gain
    gains_ref[...] = jnp.where(lane == 0, attend, forward / gain_ref[:, 1:2])


def weights_call(got, vw, qw, kw, gains):
    place = np.zeros((8, 128, 512), np.float32)
    for d in range(8):
        for i in range(32):
            place[d, i, 32 * d + i] = 1.0
            place[d, 32 + i, 256 + 32 * d + i] = 1.0
    n = got.shape[1]
    outs = [jax.ShapeDtypeStruct((n, c), F32) for c in (vw.shape[1], qw.shape[1], kw.shape[1], 128)]
    return pl.pallas_call(
        weights_kernel, out_shape=outs, compiler_params=pltpu.CompilerParams(vmem_limit_bytes=16 * 1024 * 1024),
        name="weights_kernel",
    )(got, jnp.asarray(place, BF16), vw, qw, kw, gains)


def row_call(kernel, pieces, ins, kinds, deps=()):
    shape = pieces[0].shape
    outs = [jax.ShapeDtypeStruct(shape, kind) for kind in kinds]

    def wrapped(*refs):
        at = 6 + len(ins)
        kernel(refs[:6], *refs[6:at], *refs[at + len(deps) :])

    return pl.pallas_call(
        wrapped,
        in_specs=[pl.BlockSpec(memory_space=pltpu.VMEM)] * (6 + len(ins))
        + [pl.BlockSpec(memory_space=pl.ANY)] * len(deps),
        out_specs=[pl.BlockSpec(memory_space=pltpu.VMEM)] * len(outs),
        out_shape=outs,
        compiler_params=pltpu.CompilerParams(vmem_limit_bytes=24 * 1024 * 1024),
        cost_estimate=cost(20 * math.prod(shape), *pieces, *ins, *outs),
        name=kernel.__name__,
    )(*pieces, *ins, *deps)


def parts_call(a, w, kind, deps=(), mib=60, pairs=(0, 1, 2, 3)):
    _, per, k = a.shape
    n, slots = len(pairs), 2 * len(pairs)
    if kind == "blocks":
        tile, depth = w.shape[2], w.shape[1]
        width = w.shape[0] * tile
        w_spec = pl.BlockSpec((1, depth, tile), lambda i: (i, 0, 0))
    elif kind == "nn":
        tile, depth, width = 512, k, w.shape[1]
        w_spec = pl.BlockSpec((k, tile), lambda i: (0, i))
    else:
        tile, depth, width = 512, k, w.shape[0]
        w_spec = pl.BlockSpec((tile, k), lambda i: (i, 0))

    def kernel(*refs):
        w_ref = refs[n]
        right = w_ref[0] if kind == "blocks" else w_ref[...]
        for slot, out_ref in enumerate(refs[-slots:]):
            left = refs[slot // 2][slot % 2, :, :depth]
            out_ref[...] = (dot_t if kind == "nt" else dot)(left, right).astype(BF16)

    out = jax.ShapeDtypeStruct((per, width), BF16)
    return pl.pallas_call(
        kernel,
        grid=(width // tile,),
        in_specs=[pl.BlockSpec((2, per, k), lambda i, p=p: (p, 0, 0)) for p in pairs]
        + [w_spec]
        + [pl.BlockSpec(memory_space=pl.ANY)] * len(deps),
        out_specs=[pl.BlockSpec((per, tile), lambda i: (0, i))] * slots,
        out_shape=far_out([out] * slots),
        compiler_params=params(mib),
        cost_estimate=cost(2 * slots * per * depth * width, w, *[out] * slots),
        name="parts_" + kind,
    )(*far_in([*[a] * n, w]), *deps)


def ordered(ref, me, lanes=slice(None)):
    return jnp.concatenate([ref[p ^ me, 0, :, lanes] for p in range(8)], 0)


def put_ordered(ref, me, value, lanes=slice(None)):
    sub = value.shape[0] // 8
    for p in range(8):
        ref[p ^ me, 0, :, lanes] = value[p * sub : (p + 1) * sub]


def phi(aligned, feat, rows):
    both = dot(aligned, feat) + rows[0:1, :]
    a, b = both[:, :FPAD], both[:, FPAD:]
    return a, b, a * b * rows[1:2, :FPAD]


def phi_back(a, b, grad, feat, rows):
    scaled = grad * rows[1:2, :FPAD]
    return dot_t((scaled * b).astype(BF16), feat[:, :FPAD]) + dot_t(
        (scaled * a).astype(BF16), feat[:, FPAD:]
    )


def put_state(ref, head, state, norm):
    ref[0, head] = state[:FROWS].astype(BF16)
    high = norm.astype(BF16)
    low = (norm - high.astype(F32)).astype(BF16)
    ref[0, head, FEAT : FEAT + 1, :] = high[:, :128]
    ref[0, head, FEAT + 1 : FEAT + 2, :] = low[:, :128]
    ref[0, head, FEAT + 2 : FEAT + 3, :] = high[:, 128:]
    ref[0, head, FEAT + 3 : FEAT + 4, :] = low[:, 128:]


def get_state(ref, head):
    whole = ref[0, head]
    state = jnp.concatenate([whole, jnp.zeros((FPAD - FROWS, 128), F32)], 0)
    norm = jnp.concatenate(
        [
            whole[FEAT : FEAT + 1] + whole[FEAT + 1 : FEAT + 2],
            whole[FEAT + 2 : FEAT + 3] + whole[FEAT + 3 : FEAT + 4],
        ],
        1,
    )
    return state.astype(BF16), norm


def align4(qk, align_ref):
    out = dot(qk, align_ref[...]).astype(BF16)
    return [out[:, i * 128 : (i + 1) * 128] for i in range(4)]


def column(seg_ref):
    row = seg_ref[0]
    return jnp.transpose(jnp.broadcast_to(row, (128, row.shape[1])))[:, 0:1]


def mask_of(seg_ref, meta_ref, which):
    at = 1 + which * pl.num_programs(0) + pl.program_id(0)
    return jnp.where(column(seg_ref) == meta_ref[at].astype(F32), 1.0, 0.0)


def visible(seg_ref):
    t = seg_ref.shape[2]
    causal = lax.broadcasted_iota(jnp.int32, (t, t), 0) >= lax.broadcasted_iota(jnp.int32, (t, t), 1)
    return causal & (column(seg_ref) == seg_ref[0])


def state_kernel(me_ref, qkv_ref, seg_ref, feat_ref, rows_ref, align_ref, out_ref):
    me = me_ref[0]
    qk = ordered(qkv_ref, me, slice(256, 384))
    v = ordered(qkv_ref, me, slice(0, 256))
    last = mask_of(seg_ref, me_ref, 1)
    parts = align4(qk, align_ref)
    for head in range(2):
        _, _, feat = phi(parts[2 + head], feat_ref[...], rows_ref[...])
        feat = feat * last
        state = t_dot(feat.astype(BF16), v[:, head * 128 : (head + 1) * 128])
        put_state(out_ref, head, state, jnp.sum(feat, 0, keepdims=True))


def intra_kernel(me_ref, qkv_ref, seg_ref, align_ref, num_ref, den_ref):
    me = me_ref[0]
    qk = ordered(qkv_ref, me, slice(256, 384))
    v = ordered(qkv_ref, me, slice(0, 256))
    see = visible(seg_ref)
    parts = align4(qk, align_ref)
    den_ref[0] = jnp.zeros(den_ref.shape[1:], F32)
    for head in range(2):
        z = dot_t(parts[head], parts[2 + head])
        w = jnp.where(see, 1.0 + z * (0.25 + 0.03125 * z), 0.0)
        num_ref[0, :, head * 128 : (head + 1) * 128] = dot(
            w.astype(BF16), v[:, head * 128 : (head + 1) * 128]
        )
        den_ref[0, :, head : head + 1] = jnp.sum(w, 1, keepdims=True)


def output_kernel(
    me_ref, qkv_ref, seg_ref, feat_ref, rows_ref, align_ref, num_ref, den_ref, state_ref, o_ref, all_ref
):
    me = me_ref[0]
    qk = ordered(qkv_ref, me, slice(256, 384))
    use = mask_of(seg_ref, me_ref, 0)
    parts = align4(qk, align_ref)
    all_ref[0] = jnp.zeros(all_ref.shape[1:], F32)
    for head in range(2):
        lanes = slice(head * 128, (head + 1) * 128)
        _, _, feat = phi(parts[head], feat_ref[...], rows_ref[...])
        state, norm = get_state(state_ref, head)
        num = num_ref[0, :, lanes] + use * dot(feat.astype(BF16), state)
        den = den_ref[0, :, head : head + 1] + use * jnp.sum(feat * norm, 1, keepdims=True)
        all_ref[0, :, head : head + 1] = den
        put_ordered(o_ref, me, (num / den).astype(BF16), lanes)


def back_parts(me, o_ref, do_ref, den_ref, head):
    lanes = slice(head * 128, (head + 1) * 128)
    inv = 1.0 / den_ref[0, :, head : head + 1]
    do = ordered(do_ref, me, lanes).astype(F32)
    o = ordered(o_ref, me, lanes).astype(F32)
    return (do * inv).astype(BF16), -jnp.sum(do * o, 1, keepdims=True) * inv


def back_state_kernel(
    me_ref, qkv_ref, seg_ref, feat_ref, rows_ref, align_ref, o_ref, do_ref, den_ref, out_ref
):
    me = me_ref[0]
    qk = ordered(qkv_ref, me, slice(256, 384))
    use = mask_of(seg_ref, me_ref, 0)
    parts = align4(qk, align_ref)
    for head in range(2):
        g, c = back_parts(me, o_ref, do_ref, den_ref, head)
        _, _, feat = phi(parts[head], feat_ref[...], rows_ref[...])
        feat = feat * use
        put_state(out_ref, head, t_dot(feat.astype(BF16), g), jnp.sum(feat * c, 0, keepdims=True))


def back_intra_kernel(
    me_ref, qkv_ref, seg_ref, feat_ref, rows_ref, align_ref, o_ref, do_ref, den_ref, state_ref,
    dq_ref, dk_ref, dv_ref,
):
    me = me_ref[0]
    qk = ordered(qkv_ref, me, slice(256, 384))
    v = ordered(qkv_ref, me, slice(0, 256))
    use = mask_of(seg_ref, me_ref, 0)
    see = visible(seg_ref)
    parts = align4(qk, align_ref)
    for head in range(2):
        lanes = slice(head * 128, (head + 1) * 128)
        g, c = back_parts(me, o_ref, do_ref, den_ref, head)
        z = dot_t(parts[head], parts[2 + head])
        w = jnp.where(see, 1.0 + z * (0.25 + 0.03125 * z), 0.0)
        dv_ref[0, :, lanes] = t_dot(w.astype(BF16), g)
        dw = dot_t(g, v[:, lanes]) + c
        dz = jnp.where(see, dw * (0.25 + 0.0625 * z), 0.0).astype(BF16)
        a, b, _ = phi(parts[head], feat_ref[...], rows_ref[...])
        state, norm = get_state(state_ref, head)
        grad = use * (dot_t(g, state) + c * norm)
        dq_ref[0, :, lanes] = dot(dz, parts[2 + head]) + phi_back(a, b, grad, feat_ref[...], rows_ref[...])
        dk_ref[0, :, lanes] = t_dot(dz, parts[head])


def back_output_kernel(
    me_ref, qkv_ref, seg_ref, feat_ref, rows_ref, align_ref, state_ref, dq_ref, dk_ref, dv_ref, inv_ref, out_ref, scaled_ref
):
    me = me_ref[0]
    qk = ordered(qkv_ref, me, slice(256, 384))
    v = ordered(qkv_ref, me, slice(0, 256))
    last = mask_of(seg_ref, me_ref, 1)
    parts = align4(qk, align_ref)
    inv = ordered(inv_ref, me)
    packed = None
    for head in range(2):
        lanes = slice(head * 128, (head + 1) * 128)
        a, b, feat = phi(parts[2 + head], feat_ref[...], rows_ref[...])
        state, norm = get_state(state_ref, head)
        grad = last * (dot_t(v[:, lanes], state) + norm)
        dk = dk_ref[0, :, lanes] + phi_back(a, b, grad, feat_ref[...], rows_ref[...])
        dv = dv_ref[0, :, lanes] + last * dot(feat.astype(BF16), state)
        put_ordered(out_ref, me, dv.astype(BF16), lanes)
        put_ordered(scaled_ref, me, (dv * inv).astype(BF16), lanes)
        place = align_ref[...]
        term = dot_t(dq_ref[0, :, lanes].astype(BF16), place[:, head * 128 : (head + 1) * 128]) + dot_t(
            dk.astype(BF16), place[:, (2 + head) * 128 : (3 + head) * 128]
        )
        packed = term if packed is None else packed + term
    put_ordered(out_ref, me, packed.astype(BF16), slice(256, 384))
    put_ordered(scaled_ref, me, (packed * inv).astype(BF16), slice(256, 384))


def attention_call(kernel, me, ins, kinds, outs, flops, deps=()):
    def spec(a, kind):
        if kind == "s":
            return pl.BlockSpec((8, 1) + a.shape[2:], lambda i, m: (0, i, 0, 0))
        rest = len(a.shape) - 1
        if kind == "q":
            return pl.BlockSpec((1,) + a.shape[1:], lambda i, m: (i,) + (0,) * rest)
        return pl.BlockSpec(a.shape, lambda i, m: (0,) * (rest + 1))

    seqs = ins[0].shape[1]
    n = 1 + len(ins)

    def wrapped(*refs):
        kernel(*refs[:n], *refs[n + len(deps) :])

    return pl.pallas_call(
        wrapped,
        out_shape=far_out([a for a, _ in outs], kernel is back_intra_kernel),
        grid_spec=pltpu.PrefetchScalarGridSpec(
            num_scalar_prefetch=1,
            grid=(seqs,),
            in_specs=[spec(a, k) for a, k in zip(ins, kinds)] + [pl.BlockSpec(memory_space=pl.ANY)] * len(deps),
            out_specs=[spec(a, k) for a, k in outs],
        ),
        compiler_params=params(28),
        cost_estimate=cost(flops, *ins, *[a for a, _ in outs]),
        name=kernel.__name__,
    )(me, *far_in(ins), *deps)


def pick(cond, a, b):
    return jnp.where(cond, a, b)


def half_columns(gate, up, which, n_main, n_mid):
    mid = slice(n_main, n_main + 2 * n_mid)
    main = slice(0, n_main) if which == 0 else slice(n_main + 2 * n_mid, None)
    part = slice(0, n_mid) if which == 0 else slice(n_mid, None)
    return jnp.concatenate([gate[:, main], up[:, main], gate[:, mid][:, part], up[:, mid][:, part]], 1)


def body(inputs, segments, qw, kw, vw, pw, again, gw, uw, dw, fgain, upstream):
    hi, core, row, col = (lax.axis_index(a) for a in ("hi", "core", "row", "col"))
    rows = lax.axis_size("row")
    shards = 2 * rows
    seqs, sub = inputs.shape[0], inputs.shape[3]
    tokens = seqs * sub
    span = 8 * sub
    n_rows = qw.shape[0]
    is0 = col == 0
    ff = gw.shape[1]
    half_ff = ff // 2
    n_mid = 64
    n_main = half_ff - n_mid
    feat_c, rows_c, align_c = feature_constants()
    sds = jax.ShapeDtypeStruct
    x = inputs.reshape(tokens, D)

    shard_pairs = [(s, (s % rows) * 2 + s // rows) for s in range(shards)]
    moved = lax.ppermute(pw, ("row", "col"), shard_pairs)

    gain_one = again.astype(F32)[:, None]
    seg_own = segments.reshape(seqs, 4 * sub)

    def by_dest(w, scale):
        return (w.astype(F32) * scale).astype(BF16).reshape(n_rows, 8, -1)

    lane = lax.broadcasted_iota(jnp.int32, (n_rows, PAYLOAD - 320), 1)
    ends = jnp.pad(seg_own[:, -1], (0, n_rows - seqs)).astype(F32)[:, None]
    tens = jnp.floor(ends * (1.0 / 128.0))
    extra = jnp.where(
        lane == 0,
        fgain.astype(F32)[:, None],
        jnp.where(lane == 1, tens, jnp.where(lane == 2, ends - 128.0 * tens, 0.0)),
    ).astype(BF16)
    payload = jnp.concatenate(
        [
            by_dest(vw, gain_one),
            by_dest(qw, gain_one),
            by_dest(kw, gain_one),
            jnp.broadcast_to(extra[:, None], (n_rows, 8, PAYLOAD - 320)),
        ],
        2,
    ).transpose(1, 0, 2)
    payload = lax.all_to_all(payload, GROUP, split_axis=0, concat_axis=0, tiled=True)
    x_own = after(x, payload)
    xs = gather8(x_own)
    w_proj = lax.all_gather(moved, "row", axis=0, tiled=True)
    gathered = lax.all_gather(after(payload, moved), "row", axis=0, tiled=False)
    lasts = gathered[:, 1, :seqs, 321:323].astype(F32)
    lasts = (lasts[:, :, 0] * 128.0 + lasts[:, :, 1]).astype(jnp.int32)

    seg_other = swap(seg_own, "col")
    seg = jnp.concatenate([pick(is0, seg_own, seg_other), pick(is0, seg_other, seg_own)], 1)
    seg_row = seg.astype(F32)[:, None, :]
    before = jnp.where(row > 0, lasts[jnp.maximum(row - 1, 0)], -1)
    here = lasts[row]
    me3 = (4 * col + 2 * hi + core).astype(jnp.int32)
    meta = jnp.concatenate([me3[None], before, here])

    ends = jnp.concatenate([lasts, jnp.full((1, seqs), -1, jnp.int32)])

    def end_of(r):
        return ends[jnp.where((r >= 0) & (r < rows), r, rows)]

    def same(r, other):
        return ((end_of(r) == other) & (r >= 0) & (r < rows)).astype(F32)

    every = 8 * tokens
    qkv, inv, w_qkv = slot_call(
        qkv_kernel, xs, [(gathered.reshape(rows, 4, 2 * n_rows, PAYLOAD), False)],
        [sds((8, tokens, PAYLOAD), BF16), sds((8, tokens, 128), F32)], 2 * every * D * PAYLOAD,
        deps=[seg_row], whole=[sds((D, PAYLOAD), BF16)],
    )
    gain_two = w_qkv[:, 320].astype(F32)[None, :]
    inv = inv.reshape(8, seqs, sub, 128)
    ups = gather8(after(upstream.reshape(tokens, D), qkv))
    qkv = qkv.reshape(8, seqs, sub, PAYLOAD)
    st = sds((seqs, 2, FROWS, 128), BF16)
    near = 4 * seqs * span * span * 160
    far = 4 * seqs * span * FPAD * 300
    (state,) = attention_call(
        state_kernel, meta, [qkv, seg_row, feat_c, rows_c, align_c], "sqccc", [(st, "q")], far
    )
    mine = pick(is0, half_columns(gw, uw, 0, n_main, n_mid), half_columns(gw, uw, 1, n_main, n_mid))
    theirs = pick(is0, half_columns(gw, uw, 1, n_main, n_mid), half_columns(gw, uw, 0, n_main, n_mid))
    got = swap(after(theirs, xs[6][0], xs[7][0]), "col")
    got = after(got, state)
    gu_rows = jnp.concatenate([pick(is0, mine, got), pick(is0, got, mine)], 0)
    w_gu = lax.all_gather(gu_rows, "row", axis=0, tiled=True)
    down0 = dw[: n_main + n_mid]
    down1 = jnp.concatenate([dw[n_main + 2 * n_mid :], dw[n_main + n_mid : n_main + 2 * n_mid]], 0)
    d_mine, d_theirs = pick(is0, down0, down1), pick(is0, down1, down0)
    d_got = swap(after(d_theirs, got), "col")
    d_cols = jnp.stack([pick(is0, d_mine, d_got), pick(is0, d_got, d_mine)])
    w_down = lax.all_gather(d_cols, "row", axis=0, tiled=True)
    fold = shards // 8
    w_down = (
        w_down.reshape(8, fold, half_ff, D // shards).transpose(0, 2, 1, 3).reshape(8, half_ff, D // 8)
    )

    num, den_in = attention_call(
        intra_kernel, meta, [qkv, seg_row, align_c], "sqc",
        [(sds((seqs, span, 256), F32), "q"), (sds((seqs, span, 8), F32), "q")], near,
    )
    forth = walk_steps(state, lambda d: same(row - d, here), lambda d: same(row - d, before), True)
    _, came = next(forth)
    came, num, den_in = meet(came, num, den_in)
    state_in = finish(forth, came)
    o, den = attention_call(
        output_kernel, meta, [qkv, seg_row, feat_c, rows_c, align_c, num, den_in, state_in], "sqcccqqq",
        [(sds((8, seqs, sub, 256), BF16), "s"), (sds((seqs, span, 8), F32), "q")], far,
        [ups[6][0], ups[7][0], d_got],
    )
    o_rows = o.reshape(8, tokens, 256)
    residual, a2_own = row_call(
        residual_kernel, scatter8(parts_call(o_rows, w_proj, "nn", mib=28)), [x, gain_two], [F32, BF16]
    )

    ff_flops = 2 * every * D * half_ff
    steps = gather_steps(a2_own)
    wide = [
        sds((8, tokens, ff), BF16),
        sds((8, tokens, half_ff + n_mid), BF16),
        sds((8, half_ff + n_mid, tokens), BF16),
    ]
    hidden = slot_call(ffn_in_kernel, next(steps), [(w_gu, False)], wide, 2 * ff_flops, slots=(0, 2))
    hidden = slot_call(
        ffn_in_kernel, steps.send(hidden[:1]), [(w_gu, False)], wide, 2 * ff_flops, slots=(2, 6), into=hidden
    )
    a2 = finish(steps, hidden[:1])
    gu, h, h_turned = slot_call(
        ffn_in_kernel, a2, [(w_gu, False)], wide, 2 * ff_flops, slots=(6, 8), into=hidden
    )
    (down_g,) = grad_call(
        down_grad_kernel, ups, 256, [h_turned], [],
        [(sds((8, half_ff, 256), BF16), (1, half_ff, 256), lambda i: (i, 0, 0))], ff_flops,
    )
    late = {}

    def ffn_back(slots, into, deps=()):
        return slot_call(
            ffn_back_kernel, ups, [(w_down, False), (gu, True)], [sds((8, tokens, ff), BF16)], ff_flops, deps,
            slots=slots, into=into,
        )[0]

    half = tokens // 2
    dgu = ffn_back((0, 8), (), [down_g])
    own, other, y, yc, x_, xc, xy, xyc = parts_call(dgu, w_gu, "nt")
    other, yc, xc, xyc = (swap(part, "core") for part in (other, yc, xc, xyc))
    to_x = pair_sum(xy, xyc, 0, half).astype(BF16)
    to_y = pair_sum(xy, xyc, half, tokens).astype(BF16)
    near_x = pair_sum(x_, xc, 0, half).astype(BF16)
    near_y = pair_sum(y, yc, half, tokens).astype(BF16)
    down_g = (
        down_g.reshape(8, half_ff, fold, D // shards).transpose(0, 2, 1, 3).reshape(shards * half_ff, -1)
    )
    down_g = lax.psum_scatter(down_g, "row", scatter_dimension=0, tiled=True)
    block = D // shards
    gu_gs, gains = [], []

    def gu_half(x_bit):
        def run(sent):
            one, gain = grad_call(
                gu_grad_kernel, a2, 256, [dgu], [(w_gu, (256, ff), lambda i: (2 * i + x_bit, 0))],
                [
                    (sds((D // 2, ff), BF16), (256, ff), lambda i: (i, 0)),
                    (sds((D // 2, 128), F32), (256, 128), lambda i: (i, 0)),
                ],
                ff_flops, lambda i: 2 * i + x_bit, 4, sent,
            )
            gu_gs.append(one)
            gains.append(gain)
            return [one]

        return run

    gu_half(0)([to_x, to_y, near_x, near_y])
    from_x, from_y, first_x, first_y, gu_gs[0] = meet(
        swap(to_x, "col"), swap(to_y, "hi"), swap(near_x, "col"), swap(near_y, "hi"), gu_gs[0]
    )
    far_x = (pair_sum(x_, xc, half, tokens) + from_y.astype(F32)).astype(BF16)
    far_y = (pair_sum(y, yc, 0, half) + from_x.astype(F32)).astype(BF16)
    gu_half(1)([far_x, far_y, gu_gs[0]])
    last_x, last_y, gu_gs[1] = meet(swap(far_x, "col"), swap(far_y, "hi"), gu_gs[1])
    grad_r, datt_own = row_call(
        residual_back_kernel, [own, other, first_x, last_y, last_x, first_y],
        [upstream.reshape(tokens, D), residual, gain_two], [F32, BF16],
    )
    over_x, over_y, over_c, *down_parts = meet(
        swap(datt_own, "col"), swap(datt_own, "hi"), swap(datt_own, "core"),
        *parts_call(h, w_down, "blocks", [datt_own]),
    )
    to_x, to_y = over_y[:half], over_x[half:]
    over_yc, over_xc = swap(over_y, "core"), swap(over_x, "core")
    datt = [(datt_own, 0, 0), (over_c, 1, 0), (over_y, 2, 0), (over_yc, 3, 0), (over_x, 4, 0), (over_xc, 5, 0)]
    do_out = [sds((8, tokens, 256), BF16)]
    do_flops = 2 * every * D * 256
    (do,) = slot_call(do_kernel, datt, [(w_proj, False)], do_out, do_flops, [to_x, to_y], slots=(0, 6))
    top, low, do = meet(swap(to_x, "col"), swap(to_y, "hi"), do)
    datt += [(top, 6, 0), (low, 6, half), (swap(top, "core"), 7, 0), (swap(low, "core"), 7, half)]
    (do,) = slot_call(do_kernel, datt, [(w_proj, False)], do_out, do_flops, [down_g], slots=(6, 8), into=[do])
    gain_part = jnp.stack([g.reshape(4, 256, 128) for g in gains], 1).reshape(D, 128)
    if fold > 1:
        natural = jnp.stack([g.reshape(4, 256, ff) for g in gu_gs], 1)
        by_col = natural.reshape(rows, 2, block, ff).transpose(1, 0, 2, 3)
        gu_gs = [by_col[0].reshape(D // 2, ff), by_col[1].reshape(D // 2, ff)]
    gu_r = [lax.psum_scatter(g, "row", scatter_dimension=0, tiled=True) for g in gu_gs]

    do = do.reshape(8, seqs, sub, 256)

    (dstate,) = attention_call(
        back_state_kernel, meta, [qkv, seg_row, feat_c, rows_c, align_c, o, do, den], "sqcccssq",
        [(st, "q")], far,
    )
    part = sds((seqs, span, 256), F32)

    back = walk_steps(
        dstate,
        lambda d: same(row + d - 1, before) * (row + d < rows),
        lambda d: same(row + d - 1, here) * (row + d < rows),
        False,
    )
    _, came = next(back)
    own, other, y, yc, x_, xc, xy, xyc = down_parts
    other, yc, xc, xyc = (after(swap(part, "core"), dstate) for part in (other, yc, xc, xyc))
    to_x = pair_sum(xy, xyc, 0, half).astype(BF16)
    to_y = pair_sum(xy, xyc, half, tokens).astype(BF16)
    near_x = pair_sum(x_, xc, 0, half).astype(BF16)
    near_y = pair_sum(y, yc, half, tokens).astype(BF16)
    intra = attention_call(
        back_intra_kernel, meta, [qkv, seg_row, feat_c, rows_c, align_c, o, do, den, state_in],
        "sqcccssqq", [(part, "q")] * 3, 3 * near + far, [dstate, to_x, to_y, near_x, near_y, gu_r[0]],
    )
    dq, dk, dv = intra
    came, from_x, from_y, first_x, first_y, dq = meet(
        came, swap(to_x, "col"), swap(to_y, "hi"), swap(near_x, "col"), swap(near_y, "hi"), dq
    )
    far_x = (pair_sum(x_, xc, half, tokens) + from_y.astype(F32)).astype(BF16)
    far_y = (pair_sum(y, yc, 0, half) + from_x.astype(F32)).astype(BF16)
    step = back.send(came)
    now = None
    if step is not None:
        now, came = step
    (proj_g,) = grad_call(
        proj_grad_kernel, datt, 1024, [o_rows], [],
        [(sds((256, D), BF16), (256, 1024), lambda i: (0, i))], 2 * every * D * 256, deps=[far_x, far_y, now], mib=24,
    )
    down_r = down_g.reshape(2, half_ff, D // shards)
    d_keep, d_send = pick(is0, down_r[0], down_r[1]), pick(is0, down_r[1], down_r[0])
    g_keep = pick(is0, gu_r[0], gu_r[1])
    g_send = pick(is0, gu_r[1], gu_r[0])
    came, last_x, last_y, d_got, proj_g = meet(
        came, swap(far_x, "col"), swap(far_y, "hi"), swap(d_send, "col"), proj_g
    )
    (outputs,) = row_call(
        output_rows_kernel, [own, other, first_x, last_y, last_x, first_y], [residual], [BF16]
    )
    dstate_out = finish(back, came)
    proj_r = lax.psum_scatter(proj_g, "row", scatter_dimension=0, tiled=True)
    row_out = sds((8, seqs, sub, PAYLOAD), BF16)
    dqkv, scaled = attention_call(
        back_output_kernel, meta, [qkv, seg_row, feat_c, rows_c, align_c, dstate_out, dq, dk, dv, inv],
        "sqcccqqqqs", [(row_out, "s")] * 2, 2 * far, [outputs, gu_r[1]],
    )
    g_got, dqkv, scaled = meet(swap(g_send, "col"), dqkv, scaled)

    def qkv_side(sent):
        (late["qkv"],) = grad_call(
            qkv_grad_kernel, xs, 512, [scaled.reshape(8, tokens, PAYLOAD)],
            [(gain_part, (512, 128), lambda i: (i, 0))],
            [
                (
                    sds((rows, 4, 2 * n_rows, PAYLOAD), BF16),
                    (rows, 1, 2 * n_rows, PAYLOAD),
                    lambda i: (0, i, 0, 0),
                )
            ],
            2 * every * D * PAYLOAD, deps=sent, mib=24,
        )
        return [late["qkv"]]

    qkv_g = qkv_side([proj_r])[0]
    own, other, y, yc, x_, xc, xy, xyc = parts_call(
        dqkv.reshape(8, tokens, PAYLOAD), w_qkv, "nt", [qkv_g], 28
    )
    other, yc, xc, xyc = (swap(part, "core") for part in (other, yc, xc, xyc))
    to_x = pair_sum(xy, xyc, 0, half).astype(BF16)
    to_y = pair_sum(xy, xyc, half, tokens).astype(BF16)
    near_x = pair_sum(x_, xc, 0, half).astype(BF16)
    near_y = pair_sum(y, yc, half, tokens).astype(BF16)
    from_x, from_y, first_x, first_y = (
        swap(to_x, "col"), swap(to_y, "hi"), swap(near_x, "col"), swap(near_y, "hi")
    )
    far_x = (pair_sum(x_, xc, half, tokens) + from_y.astype(F32)).astype(BF16)
    far_y = (pair_sum(y, yc, 0, half) + from_x.astype(F32)).astype(BF16)
    f_pieces = [own, other, first_x, swap(far_y, "hi"), swap(far_x, "col"), first_y]
    qkv_g = lax.psum_scatter(qkv_g.reshape(D, PAYLOAD), "row", scatter_dimension=0, tiled=True)
    project_grad = lax.ppermute(
        after(proj_r, f_pieces[5]), ("row", "col"), [(b, a) for a, b in shard_pairs]
    ).astype(F32)
    qkv_g = lax.all_to_all(
        qkv_g.reshape(8, n_rows, PAYLOAD), GROUP, split_axis=0, concat_axis=0, tiled=True
    )
    (inputs_grad,) = row_call(input_back_kernel, f_pieces, [x, grad_r], [F32])
    v_g, q_g, k_g, both_gains = weights_call(
        qkv_g, vw, qw, kw, jnp.stack([again.astype(F32), fgain.astype(F32)], 1)
    )
    attend_grad, forward_grad = both_gains[:, 0], both_gains[:, 1]
    d0, d1 = pick(is0, d_keep, d_got).astype(F32), pick(is0, d_got, d_keep).astype(F32)
    down_grad = jnp.concatenate([d0, d1[n_main:], d1[:n_main]], 0)
    g0, g1 = pick(is0, g_keep, g_got).astype(F32), pick(is0, g_got, g_keep).astype(F32)
    m = 2 * n_main
    gate_grad = jnp.concatenate(
        [g0[:, :n_main], g0[:, m : m + n_mid], g1[:, m : m + n_mid], g1[:, :n_main]], 1
    )
    up_grad = jnp.concatenate(
        [g0[:, n_main:m], g0[:, m + n_mid :], g1[:, m + n_mid :], g1[:, n_main:m]], 1
    )
    return (
        outputs.reshape(inputs.shape),
        inputs_grad.reshape(inputs.shape),
        q_g,
        k_g,
        v_g,
        project_grad,
        attend_grad,
        gate_grad,
        up_grad,
        down_grad,
        forward_grad,
    )


def solution(mesh):
    heads, shards = mesh.devices.shape
    fine = Mesh(mesh.devices.reshape(heads // 2, 2, shards // 2, 2), ("hi", "core", "row", "col"))
    h, s = ("hi", "core"), ("row", "col")
    every = P(h + s)
    tokens = P(None, s, h)
    return jax.shard_map(
        body,
        mesh=fine,
        in_specs=(
            tokens, P(None, s), every, every, every, every, every, P(s, h), P(s, h), P(h, s), every, tokens,
        ),
        out_specs=(
            tokens, tokens, every, every, every, every, every, P(s, h), P(s, h), P(h, s), every,
        ),
        check_vma=False,
    )
```

```python
import math

import numpy as np

import jax
import jax.numpy as jnp
from jax import lax
from jax.experimental import pallas as pl
from jax.experimental.pallas import tpu as pltpu
from jax.sharding import Mesh
from jax.sharding import PartitionSpec as P

D = 2048
HEADS = 16
QK = 16
VD = 128
EPS = 1e-05
F32 = jnp.float32
BF16 = jnp.bfloat16
GROUP = ("hi", "core", "col")
FEAT = 1 + QK + QK * (QK + 1) // 2
FPAD = 256
FROWS = 160
PAYLOAD = 384


def feature_constants():
    left = np.zeros((128, FPAD), np.float32)
    right = np.zeros((128, FPAD), np.float32)
    rows = np.zeros((8, 2 * FPAD), np.float32)
    at = 0
    for i in range(QK):
        for j in range(i, QK):
            left[i, at] = 1.0
            right[j, at] = 1.0
            rows[1, at] = (1.0 if i == j else math.sqrt(2.0)) / math.sqrt(2.0 * QK)
            at += 1
    for i in range(QK):
        left[i, at] = 1.0
        rows[0, FPAD + at] = 1.0
        rows[1, at] = QK ** (-0.25)
        at += 1
    rows[0, at] = 1.0
    rows[0, FPAD + at] = 1.0
    rows[1, at] = 1.0
    align = np.zeros((4, 128, 128), np.float32)
    for part in range(4):
        for i in range(QK):
            align[part, part * QK + i, i] = 1.0
    return (
        jnp.asarray(np.concatenate([left, right], 1), BF16),
        jnp.asarray(rows, F32),
        jnp.asarray(align.transpose(1, 0, 2).reshape(128, 512), BF16),
    )


def dot(a, b):
    return jnp.dot(a, b, preferred_element_type=F32)


def dot_t(a, b):
    return lax.dot_general(a, b, (((1,), (1,)), ((), ())), preferred_element_type=F32)


def t_dot(a, b):
    return lax.dot_general(a, b, (((0,), (0,)), ((), ())), preferred_element_type=F32)


def swap(value, axis):
    return lax.ppermute(value, axis, [(0, 1), (1, 0)])


def after(value, *others):
    if not others:
        return value

    def gate(*refs):
        pass

    return pl.pallas_call(
        gate,
        in_specs=[pl.BlockSpec(memory_space=pl.ANY)] * (1 + len(others)),
        out_specs=pl.BlockSpec(memory_space=pl.ANY),
        out_shape=jax.ShapeDtypeStruct(value.shape, value.dtype),
        input_output_aliases={0: 0},
        cost_estimate=pl.CostEstimate(flops=0, transcendentals=0, bytes_accessed=0),
        name="gate",
    )(value, *others)


def meet(*values):
    def gate(*refs):
        pass

    return pl.pallas_call(
        gate,
        in_specs=[pl.BlockSpec(memory_space=pl.ANY)] * len(values),
        out_specs=[pl.BlockSpec(memory_space=pl.ANY)] * len(values),
        out_shape=[jax.ShapeDtypeStruct(v.shape, v.dtype) for v in values],
        input_output_aliases={i: i for i in range(len(values))},
        cost_estimate=pl.CostEstimate(flops=0, transcendentals=0, bytes_accessed=0),
        name="meet",
    )(*values)


def gather_steps(own):
    half = own.shape[0] // 2
    over_x = swap(own, "col")
    over_y = swap(own, "hi")
    rows = [(own, 0, 0), (swap(own, "core"), 1, 0)]
    done = yield rows
    over_x, over_y = after(over_x, *done), after(over_y, *done)
    top = swap(over_y[:half], "col")
    low = swap(over_x[half:], "hi")
    near = [(over_y, 2, 0), (swap(over_y, "core"), 3, 0), (over_x, 4, 0), (swap(over_x, "core"), 5, 0)]
    done = yield near
    top, low = after(top, *done), after(low, *done)
    far = [(top, 6, 0), (low, 6, half), (swap(top, "core"), 7, 0), (swap(low, "core"), 7, half)]
    return rows + near + far


def gather8(own):
    steps = gather_steps(own)
    next(steps)
    return finish(steps)


def scatter_steps(parts):
    def both(one, two, start, end):
        return one[start:end].astype(F32) + two[start:end].astype(F32)

    own, other, y, yc, x, xc, xy, xyc = parts
    n = xy.shape[0]
    half = n // 2
    xyc = swap(xyc, "core")
    xc = swap(xc, "core")
    yc = swap(yc, "core")
    other = swap(other, "core")
    to_x = both(xy, xyc, 0, half).astype(BF16)
    to_y = both(xy, xyc, half, n).astype(BF16)
    near_x = both(x, xc, 0, half).astype(BF16)
    near_y = both(y, yc, half, n).astype(BF16)
    from_x, from_y = swap(to_x, "col"), swap(to_y, "hi")
    first_x, first_y = swap(near_x, "col"), swap(near_y, "hi")
    done = yield [to_x, to_y, near_x, near_y]
    from_x, from_y = after(from_x, *done), after(from_y, *done)
    far_x = (both(x, xc, half, n) + from_y.astype(F32)).astype(BF16)
    far_y = (both(y, yc, 0, half) + from_x.astype(F32)).astype(BF16)
    last_x, last_y = swap(far_x, "col"), swap(far_y, "hi")
    done = yield [far_x, far_y]
    last_x, last_y = after(last_x, *done), after(last_y, *done)
    return own, other, first_x, last_y, last_x, first_y


def walk_steps(value, linked, joined, up):
    rows = lax.axis_size("row")
    total = None
    now = value
    step = 1
    while step < rows:
        pairs = [(i, i + step) if up else (i + step, i) for i in range(rows - step)]
        came = lax.ppermute(now, "row", pairs)
        wide = (yield now, came).astype(F32)
        term = joined(step)[:, None, None, None] * wide
        total = term if total is None else total + term
        if 2 * step < rows:
            now = (now.astype(F32) + linked(step)[:, None, None, None] * wide).astype(BF16)
        step = 2 * step
    return total


def finish(steps, done=()):
    try:
        step = steps.send(done)
        while True:
            step = steps.send(step[1] if isinstance(step, tuple) else ())
    except StopIteration as end:
        return end.value


def pair_sum(one, two, start, end):
    return one[start:end].astype(F32) + two[start:end].astype(F32)


def scatter8(parts, *kernels):
    steps = scatter_steps(parts)
    sent = next(steps)
    for i, kernel in enumerate(kernels):
        done = kernel(sent)
        if i == 1:
            return finish(steps, done)
        sent = steps.send(done)
    return finish(steps)


def far_in(values):
    return [pltpu.with_memory_space_constraint(v, pltpu.HBM) if math.prod(v.shape) >= 65536 else v for v in values]


def far_out(shapes, far=False):
    if not far:
        return list(shapes)
    return [pltpu.HBM(a.shape, a.dtype) if math.prod(a.shape) >= 65536 else a for a in shapes]


def params(mib=60):
    return pltpu.CompilerParams(dimension_semantics=("arbitrary",), vmem_limit_bytes=mib * 1024 * 1024)


def cost(flops, *arrays):
    return pl.CostEstimate(
        flops=int(flops),
        transcendentals=0,
        bytes_accessed=int(sum(math.prod(a.shape) * a.dtype.itemsize for a in arrays)),
    )


def slot_call(kernel, pieces, ins, outs, flops, deps=(), whole=(), slots=(0, 8), into=(), mib=60):
    first, count = slots[0], slots[1] - slots[0]
    pieces = [p for p in pieces if slots[0] <= p[1] < slots[1]]
    n = len(pieces)
    per, width = outs[0].shape[1], pieces[0][0].shape[1]
    extra = list(deps) + list(into)

    def wrapped(*refs):
        rows = refs[:n]
        at = n + len(ins)
        rest = refs[n:at] + refs[at + len(extra) : at + len(extra) + len(outs) + len(whole)]
        buf, sem = refs[-2:]
        i = pl.program_id(0)

        @pl.when(i == 0)
        def _():
            for (a, slot, start), ref in zip(pieces, rows):
                there = buf.at[slot - first, pl.ds(start, a.shape[0])]
                pltpu.make_async_copy(ref, there, sem.at[slot - first]).start()

        pltpu.make_async_copy(buf.at[i], buf.at[i], sem.at[i]).wait()
        kernel(buf.at[i], *rest)

    def spec(a, by_slot):
        rest = len(a.shape) - 1
        if by_slot:
            return pl.BlockSpec((None,) + a.shape[1:], lambda i: (i + first,) + (0,) * rest)
        return pl.BlockSpec(a.shape, lambda i: (0,) * (rest + 1))

    at = n + len(ins) + len(deps)
    return pl.pallas_call(
        wrapped,
        grid=(count,),
        in_specs=[pl.BlockSpec(memory_space=pltpu.HBM)] * n
        + [spec(a, k) for a, k in ins]
        + [pl.BlockSpec(memory_space=pl.ANY)] * len(extra),
        out_specs=[spec(a, True) for a in outs] + [spec(a, False) for a in whole],
        out_shape=far_out(list(outs) + list(whole)),
        scratch_shapes=[pltpu.VMEM((count, per, width), BF16), pltpu.SemaphoreType.DMA((count,))],
        input_output_aliases={at + i: i for i in range(len(into))},
        compiler_params=params(mib),
        cost_estimate=cost(
            flops * count // 8, *[a for a, _, _ in pieces], *[a for a, k in ins if not k], *outs[:count // 4], *whole
        ),
        name=kernel.__name__,
    )(*[a for a, _, _ in pieces], *far_in([a for a, _ in ins]), *extra)


def grad_call(kernel, pieces, tile, whole, ins, outs, flops, index=lambda i: i, steps=None, deps=(), mib=60):
    n = len(pieces)
    width = pieces[0][0].shape[1]
    places = [(slot, start, a.shape[0]) for a, slot, start in pieces]

    def wrapped(*refs):
        at = n + len(whole) + len(ins)
        kernel(list(zip(refs[:n], places)), *refs[n:at], *refs[at + len(deps) :])

    def fixed(a):
        rest = len(a.shape)
        return pl.BlockSpec(a.shape, lambda i: (0,) * rest)

    return pl.pallas_call(
        wrapped,
        grid=(steps or width // tile,),
        in_specs=[pl.BlockSpec((a.shape[0], tile), lambda i: (0, index(i))) for a, _, _ in pieces]
        + [fixed(a) for a in whole]
        + [pl.BlockSpec(block, where) for _, block, where in ins]
        + [pl.BlockSpec(memory_space=pl.ANY)] * len(deps),
        out_specs=[pl.BlockSpec(block, where) for _, block, where in outs],
        out_shape=far_out([a for a, _, _ in outs]),
        compiler_params=params(mib),
        cost_estimate=cost(
            flops, *[a for a, _, _ in pieces], *whole, *[a for a, _, _ in ins], *[a for a, _, _ in outs]
        ),
        name=kernel.__name__,
    )(*far_in([*[a for a, _, _ in pieces], *whole, *[a for a, _, _ in ins]]), *deps)


def summed(rows, right):
    total = None
    for ref, (slot, start, n) in rows:
        term = t_dot(ref[...], right[slot, start : start + n, :])
        total = term if total is None else total + term
    return total


def qkv_kernel(x_ref, given_ref, qkv_ref, inv_ref, w_ref):
    @pl.when(pl.program_id(0) == 0)
    def _():
        rows, groups, n, _ = given_ref.shape
        for g in range(groups):
            for r in range(rows):
                w_ref[pl.ds((g * rows + r) * n, n), :] = given_ref[r, g]

    x = x_ref[...]
    wide = x.astype(F32)
    inv = lax.rsqrt(jnp.sum(wide * wide, 1, keepdims=True) * (1.0 / x.shape[1]) + EPS)
    qkv_ref[...] = (dot(x, w_ref[...]) * inv).astype(BF16)
    inv_ref[...] = jnp.broadcast_to(inv, inv_ref.shape)


def ffn_in_kernel(a_ref, w_ref, gu_ref, h_ref, turned_ref):
    gu = dot(a_ref[...], w_ref[...])
    gu_ref[...] = gu.astype(BF16)
    m = (gu.shape[1] - 128) // 2
    g, u = gu[:, :m], gu[:, m : 2 * m]
    h_ref[:, :m] = (g * jax.nn.sigmoid(g) * u).astype(BF16)
    g = gu[:, 2 * m :]
    u = pltpu.roll(g, 64, 1)
    first = lax.broadcasted_iota(jnp.int32, g.shape, 1) < 64
    h_ref[:, m:] = jnp.where(first, g * jax.nn.sigmoid(g) * u, 0.0).astype(BF16)
    turned_ref[...] = jnp.transpose(h_ref[...])


def ffn_back_kernel(up_ref, w_ref, gu_ref, out_ref):
    up = up_ref[...]
    total = None
    for i in range(8):
        term = dot_t(up[:, i * 256 : (i + 1) * 256], w_ref[i])
        total = term if total is None else total + term
    m = total.shape[1] - 64

    def both(g, u, dh):
        s = jax.nn.sigmoid(g)
        return dh * u * (s * (1.0 + g * (1.0 - s))), dh * (g * s)

    gu = gu_ref[...].astype(F32)
    dg, du = both(gu[:, :m], gu[:, m : 2 * m], total[:, :m])
    out_ref[:, :m] = dg.astype(BF16)
    out_ref[:, m : 2 * m] = du.astype(BF16)
    mid = gu[:, 2 * m :]
    other = pltpu.roll(mid, 64, 1)
    first = lax.broadcasted_iota(jnp.int32, mid.shape, 1) < 64
    dh = jnp.concatenate([total[:, m:], total[:, m:]], 1)
    dg, du = both(jnp.where(first, mid, other), jnp.where(first, other, mid), dh)
    out_ref[:, 2 * m :] = jnp.where(first, dg, du).astype(BF16)


def down_grad_kernel(rows, h_ref, out_ref):
    total = None
    for ref, (slot, start, n) in rows:
        term = dot(h_ref[slot, : out_ref.shape[1], start : start + n], ref[...])
        total = term if total is None else total + term
    out_ref[0] = total.astype(BF16)


def gu_grad_kernel(rows, right_ref, w_ref, out_ref, gain_ref):
    total = summed(rows, right_ref)
    out_ref[...] = total.astype(BF16)
    gain_ref[...] = jnp.broadcast_to(
        jnp.sum(total * w_ref[...].astype(F32), 1, keepdims=True), gain_ref.shape
    )


def do_kernel(d_ref, w_ref, out_ref):
    out_ref[...] = dot_t(d_ref[...], w_ref[...]).astype(BF16)


def proj_grad_kernel(rows, o_ref, out_ref):
    total = None
    for ref, (slot, start, n) in rows:
        term = t_dot(o_ref[slot, start : start + n, :], ref[...])
        total = term if total is None else total + term
    out_ref[...] = total.astype(BF16)


def qkv_grad_kernel(rows, right_ref, gain_ref, out_ref):
    total = summed(rows, right_ref)
    lane = lax.broadcasted_iota(jnp.int32, (1, 128), 1)
    total = jnp.concatenate([total[:, :256], jnp.where(lane == 64, gain_ref[...], total[:, 256:])], 1)
    out_ref[...] = total.astype(BF16).reshape(out_ref.shape)


def row_sum(refs):
    own, other, first_x, last_y, last_x, first_y = [ref[...].astype(F32) for ref in refs]
    return own + other + jnp.concatenate([first_x + last_y, last_x + first_y], 0)


def scaled_rows(rows):
    inv = lax.rsqrt(jnp.sum(rows * rows, 1, keepdims=True) * (1.0 / rows.shape[1]) + EPS)
    return rows * inv, inv


def norm_back(normed, inv, grad):
    return inv * (grad - normed * (jnp.sum(grad * normed, 1, keepdims=True) * (1.0 / grad.shape[1])))


def residual_kernel(refs, x_ref, gain_ref, sum_ref, a_ref):
    rows = x_ref[...].astype(F32) + row_sum(refs)
    sum_ref[...] = rows
    a_ref[...] = (scaled_rows(rows)[0] * gain_ref[...]).astype(BF16)


def output_rows_kernel(refs, sum_ref, out_ref):
    out_ref[...] = (sum_ref[...] + row_sum(refs)).astype(BF16)


def residual_back_kernel(refs, up_ref, sum_ref, gain_ref, grad_ref, low_ref):
    normed, inv = scaled_rows(sum_ref[...])
    grad = up_ref[...].astype(F32) + norm_back(normed, inv, row_sum(refs) * gain_ref[...])
    grad_ref[...] = grad
    low_ref[...] = grad.astype(BF16)


def input_back_kernel(refs, x_ref, grad_ref, out_ref):
    normed, inv = scaled_rows(x_ref[...].astype(F32))
    out_ref[...] = grad_ref[...] + norm_back(normed, inv, row_sum(refs))


def weights_kernel(got_ref, place_ref, vw_ref, qw_ref, kw_ref, gain_ref, v_ref, q_ref, k_ref, gains_ref):
    gain = gain_ref[:, 0:1]
    attend = jnp.zeros(gain.shape, F32)
    forward = jnp.zeros(gain.shape, F32)
    heads = None
    lane = lax.broadcasted_iota(jnp.int32, (1, 128), 1)
    for d in range(8):
        lanes = slice(256 * d, 256 * (d + 1))
        part = got_ref[d, :, :256].astype(F32)
        attend = attend + jnp.sum(part * vw_ref[:, lanes].astype(F32), 1, keepdims=True)
        v_ref[:, lanes] = part * gain
        tail = got_ref[d, :, 256:]
        forward = forward + jnp.sum(jnp.where(lane == 64, tail.astype(F32), 0.0), 1, keepdims=True)
        term = dot(tail, place_ref[d])
        heads = term if heads is None else heads + term
    q, k = heads[:, :256], heads[:, 256:]
    attend = attend + jnp.sum(q * qw_ref[...].astype(F32) + k * kw_ref[...].astype(F32), 1, keepdims=True)
    q_ref[...] = q * gain
    k_ref[...] = k * gain
    gains_ref[...] = jnp.where(lane == 0, attend, forward / gain_ref[:, 1:2])


def weights_call(got, vw, qw, kw, gains):
    place = np.zeros((8, 128, 512), np.float32)
    for d in range(8):
        for i in range(32):
            place[d, i, 32 * d + i] = 1.0
            place[d, 32 + i, 256 + 32 * d + i] = 1.0
    n = got.shape[1]
    outs = [jax.ShapeDtypeStruct((n, c), F32) for c in (vw.shape[1], qw.shape[1], kw.shape[1], 128)]
    return pl.pallas_call(
        weights_kernel, out_shape=outs, compiler_params=pltpu.CompilerParams(vmem_limit_bytes=16 * 1024 * 1024),
        name="weights_kernel",
    )(got, jnp.asarray(place, BF16), vw, qw, kw, gains)


def row_call(kernel, pieces, ins, kinds, deps=()):
    shape = pieces[0].shape
    outs = [jax.ShapeDtypeStruct(shape, kind) for kind in kinds]

    def wrapped(*refs):
        at = 6 + len(ins)
        kernel(refs[:6], *refs[6:at], *refs[at + len(deps) :])

    return pl.pallas_call(
        wrapped,
        in_specs=[pl.BlockSpec(memory_space=pltpu.VMEM)] * (6 + len(ins))
        + [pl.BlockSpec(memory_space=pl.ANY)] * len(deps),
        out_specs=[pl.BlockSpec(memory_space=pltpu.VMEM)] * len(outs),
        out_shape=outs,
        compiler_params=pltpu.CompilerParams(vmem_limit_bytes=24 * 1024 * 1024),
        cost_estimate=cost(20 * math.prod(shape), *pieces, *ins, *outs),
        name=kernel.__name__,
    )(*pieces, *ins, *deps)


def parts_call(a, w, kind, deps=(), mib=60, pairs=(0, 1, 2, 3)):
    _, per, k = a.shape
    n, slots = len(pairs), 2 * len(pairs)
    if kind == "blocks":
        tile, depth = w.shape[2], w.shape[1]
        width = w.shape[0] * tile
        w_spec = pl.BlockSpec((1, depth, tile), lambda i: (i, 0, 0))
    elif kind == "nn":
        tile, depth, width = 512, k, w.shape[1]
        w_spec = pl.BlockSpec((k, tile), lambda i: (0, i))
    else:
        tile, depth, width = 512, k, w.shape[0]
        w_spec = pl.BlockSpec((tile, k), lambda i: (i, 0))

    def kernel(*refs):
        w_ref = refs[n]
        right = w_ref[0] if kind == "blocks" else w_ref[...]
        for slot, out_ref in enumerate(refs[-slots:]):
            left = refs[slot // 2][slot % 2, :, :depth]
            out_ref[...] = (dot_t if kind == "nt" else dot)(left, right).astype(BF16)

    out = jax.ShapeDtypeStruct((per, width), BF16)
    return pl.pallas_call(
        kernel,
        grid=(width // tile,),
        in_specs=[pl.BlockSpec((2, per, k), lambda i, p=p: (p, 0, 0)) for p in pairs]
        + [w_spec]
        + [pl.BlockSpec(memory_space=pl.ANY)] * len(deps),
        out_specs=[pl.BlockSpec((per, tile), lambda i: (0, i))] * slots,
        out_shape=far_out([out] * slots),
        compiler_params=params(mib),
        cost_estimate=cost(2 * slots * per * depth * width, w, *[out] * slots),
        name="parts_" + kind,
    )(*far_in([*[a] * n, w]), *deps)


def ordered(ref, me, lanes=slice(None)):
    return jnp.concatenate([ref[p ^ me, 0, :, lanes] for p in range(8)], 0)


def put_ordered(ref, me, value, lanes=slice(None)):
    sub = value.shape[0] // 8
    for p in range(8):
        ref[p ^ me, 0, :, lanes] = value[p * sub : (p + 1) * sub]


def phi(aligned, feat, rows):
    both = dot(aligned, feat) + rows[0:1, :]
    a, b = both[:, :FPAD], both[:, FPAD:]
    return a, b, a * b * rows[1:2, :FPAD]


def phi_back(a, b, grad, feat, rows):
    scaled = grad * rows[1:2, :FPAD]
    return dot_t((scaled * b).astype(BF16), feat[:, :FPAD]) + dot_t(
        (scaled * a).astype(BF16), feat[:, FPAD:]
    )


def put_state(ref, head, state, norm):
    ref[0, head] = state[:FROWS].astype(BF16)
    high = norm.astype(BF16)
    low = (norm - high.astype(F32)).astype(BF16)
    ref[0, head, FEAT : FEAT + 1, :] = high[:, :128]
    ref[0, head, FEAT + 1 : FEAT + 2, :] = low[:, :128]
    ref[0, head, FEAT + 2 : FEAT + 3, :] = high[:, 128:]
    ref[0, head, FEAT + 3 : FEAT + 4, :] = low[:, 128:]


def get_state(ref, head):
    whole = ref[0, head]
    state = jnp.concatenate([whole, jnp.zeros((FPAD - FROWS, 128), F32)], 0)
    norm = jnp.concatenate(
        [
            whole[FEAT : FEAT + 1] + whole[FEAT + 1 : FEAT + 2],
            whole[FEAT + 2 : FEAT + 3] + whole[FEAT + 3 : FEAT + 4],
        ],
        1,
    )
    return state.astype(BF16), norm


def align4(qk, align_ref):
    out = dot(qk, align_ref[...]).astype(BF16)
    return [out[:, i * 128 : (i + 1) * 128] for i in range(4)]


def column(seg_ref):
    row = seg_ref[0]
    return jnp.transpose(jnp.broadcast_to(row, (128, row.shape[1])))[:, 0:1]


def mask_of(seg_ref, meta_ref, which):
    at = 1 + which * pl.num_programs(0) + pl.program_id(0)
    return jnp.where(column(seg_ref) == meta_ref[at].astype(F32), 1.0, 0.0)


def visible(seg_ref):
    t = seg_ref.shape[2]
    causal = lax.broadcasted_iota(jnp.int32, (t, t), 0) >= lax.broadcasted_iota(jnp.int32, (t, t), 1)
    return causal & (column(seg_ref) == seg_ref[0])


def state_kernel(me_ref, qkv_ref, seg_ref, feat_ref, rows_ref, align_ref, out_ref):
    me = me_ref[0]
    qk = ordered(qkv_ref, me, slice(256, 384))
    v = ordered(qkv_ref, me, slice(0, 256))
    last = mask_of(seg_ref, me_ref, 1)
    parts = align4(qk, align_ref)
    for head in range(2):
        _, _, feat = phi(parts[2 + head], feat_ref[...], rows_ref[...])
        feat = feat * last
        state = t_dot(feat.astype(BF16), v[:, head * 128 : (head + 1) * 128])
        put_state(out_ref, head, state, jnp.sum(feat, 0, keepdims=True))


def intra_kernel(me_ref, qkv_ref, seg_ref, align_ref, num_ref, den_ref):
    me = me_ref[0]
    qk = ordered(qkv_ref, me, slice(256, 384))
    v = ordered(qkv_ref, me, slice(0, 256))
    see = visible(seg_ref)
    parts = align4(qk, align_ref)
    den_ref[0] = jnp.zeros(den_ref.shape[1:], F32)
    for head in range(2):
        z = dot_t(parts[head], parts[2 + head])
        w = jnp.where(see, 1.0 + z * (0.25 + 0.03125 * z), 0.0)
        num_ref[0, :, head * 128 : (head + 1) * 128] = dot(
            w.astype(BF16), v[:, head * 128 : (head + 1) * 128]
        )
        den_ref[0, :, head : head + 1] = jnp.sum(w, 1, keepdims=True)


def output_kernel(
    me_ref, qkv_ref, seg_ref, feat_ref, rows_ref, align_ref, num_ref, den_ref, state_ref, o_ref, all_ref
):
    me = me_ref[0]
    qk = ordered(qkv_ref, me, slice(256, 384))
    use = mask_of(seg_ref, me_ref, 0)
    parts = align4(qk, align_ref)
    all_ref[0] = jnp.zeros(all_ref.shape[1:], F32)
    for head in range(2):
        lanes = slice(head * 128, (head + 1) * 128)
        _, _, feat = phi(parts[head], feat_ref[...], rows_ref[...])
        state, norm = get_state(state_ref, head)
        num = num_ref[0, :, lanes] + use * dot(feat.astype(BF16), state)
        den = den_ref[0, :, head : head + 1] + use * jnp.sum(feat * norm, 1, keepdims=True)
        all_ref[0, :, head : head + 1] = den
        put_ordered(o_ref, me, (num / den).astype(BF16), lanes)


def back_parts(me, o_ref, do_ref, den_ref, head):
    lanes = slice(head * 128, (head + 1) * 128)
    inv = 1.0 / den_ref[0, :, head : head + 1]
    do = ordered(do_ref, me, lanes).astype(F32)
    o = ordered(o_ref, me, lanes).astype(F32)
    return (do * inv).astype(BF16), -jnp.sum(do * o, 1, keepdims=True) * inv


def back_state_kernel(
    me_ref, qkv_ref, seg_ref, feat_ref, rows_ref, align_ref, o_ref, do_ref, den_ref, out_ref
):
    me = me_ref[0]
    qk = ordered(qkv_ref, me, slice(256, 384))
    use = mask_of(seg_ref, me_ref, 0)
    parts = align4(qk, align_ref)
    for head in range(2):
        g, c = back_parts(me, o_ref, do_ref, den_ref, head)
        _, _, feat = phi(parts[head], feat_ref[...], rows_ref[...])
        feat = feat * use
        put_state(out_ref, head, t_dot(feat.astype(BF16), g), jnp.sum(feat * c, 0, keepdims=True))


def back_intra_kernel(
    me_ref, qkv_ref, seg_ref, feat_ref, rows_ref, align_ref, o_ref, do_ref, den_ref, state_ref,
    dq_ref, dk_ref, dv_ref,
):
    me = me_ref[0]
    qk = ordered(qkv_ref, me, slice(256, 384))
    v = ordered(qkv_ref, me, slice(0, 256))
    use = mask_of(seg_ref, me_ref, 0)
    see = visible(seg_ref)
    parts = align4(qk, align_ref)
    for head in range(2):
        lanes = slice(head * 128, (head + 1) * 128)
        g, c = back_parts(me, o_ref, do_ref, den_ref, head)
        z = dot_t(parts[head], parts[2 + head])
        w = jnp.where(see, 1.0 + z * (0.25 + 0.03125 * z), 0.0)
        dv_ref[0, :, lanes] = t_dot(w.astype(BF16), g)
        dw = dot_t(g, v[:, lanes]) + c
        dz = jnp.where(see, dw * (0.25 + 0.0625 * z), 0.0).astype(BF16)
        a, b, _ = phi(parts[head], feat_ref[...], rows_ref[...])
        state, norm = get_state(state_ref, head)
        grad = use * (dot_t(g, state) + c * norm)
        dq_ref[0, :, lanes] = dot(dz, parts[2 + head]) + phi_back(a, b, grad, feat_ref[...], rows_ref[...])
        dk_ref[0, :, lanes] = t_dot(dz, parts[head])


def back_output_kernel(
    me_ref, qkv_ref, seg_ref, feat_ref, rows_ref, align_ref, state_ref, dq_ref, dk_ref, dv_ref, inv_ref, out_ref, scaled_ref
):
    me = me_ref[0]
    qk = ordered(qkv_ref, me, slice(256, 384))
    v = ordered(qkv_ref, me, slice(0, 256))
    last = mask_of(seg_ref, me_ref, 1)
    parts = align4(qk, align_ref)
    inv = ordered(inv_ref, me)
    packed = None
    for head in range(2):
        lanes = slice(head * 128, (head + 1) * 128)
        a, b, feat = phi(parts[2 + head], feat_ref[...], rows_ref[...])
        state, norm = get_state(state_ref, head)
        grad = last * (dot_t(v[:, lanes], state) + norm)
        dk = dk_ref[0, :, lanes] + phi_back(a, b, grad, feat_ref[...], rows_ref[...])
        dv = dv_ref[0, :, lanes] + last * dot(feat.astype(BF16), state)
        put_ordered(out_ref, me, dv.astype(BF16), lanes)
        put_ordered(scaled_ref, me, (dv * inv).astype(BF16), lanes)
        place = align_ref[...]
        term = dot_t(dq_ref[0, :, lanes].astype(BF16), place[:, head * 128 : (head + 1) * 128]) + dot_t(
            dk.astype(BF16), place[:, (2 + head) * 128 : (3 + head) * 128]
        )
        packed = term if packed is None else packed + term
    put_ordered(out_ref, me, packed.astype(BF16), slice(256, 384))
    put_ordered(scaled_ref, me, (packed * inv).astype(BF16), slice(256, 384))


def attention_call(kernel, me, ins, kinds, outs, flops, deps=()):
    def spec(a, kind):
        if kind == "s":
            return pl.BlockSpec((8, 1) + a.shape[2:], lambda i, m: (0, i, 0, 0))
        rest = len(a.shape) - 1
        if kind == "q":
            return pl.BlockSpec((1,) + a.shape[1:], lambda i, m: (i,) + (0,) * rest)
        return pl.BlockSpec(a.shape, lambda i, m: (0,) * (rest + 1))

    seqs = ins[0].shape[1]
    n = 1 + len(ins)

    def wrapped(*refs):
        kernel(*refs[:n], *refs[n + len(deps) :])

    return pl.pallas_call(
        wrapped,
        out_shape=far_out([a for a, _ in outs], kernel is back_intra_kernel),
        grid_spec=pltpu.PrefetchScalarGridSpec(
            num_scalar_prefetch=1,
            grid=(seqs,),
            in_specs=[spec(a, k) for a, k in zip(ins, kinds)] + [pl.BlockSpec(memory_space=pl.ANY)] * len(deps),
            out_specs=[spec(a, k) for a, k in outs],
        ),
        compiler_params=params(28),
        cost_estimate=cost(flops, *ins, *[a for a, _ in outs]),
        name=kernel.__name__,
    )(me, *far_in(ins), *deps)


def pick(cond, a, b):
    return jnp.where(cond, a, b)


def half_columns(gate, up, which, n_main, n_mid):
    mid = slice(n_main, n_main + 2 * n_mid)
    main = slice(0, n_main) if which == 0 else slice(n_main + 2 * n_mid, None)
    part = slice(0, n_mid) if which == 0 else slice(n_mid, None)
    return jnp.concatenate([gate[:, main], up[:, main], gate[:, mid][:, part], up[:, mid][:, part]], 1)


def body(inputs, segments, qw, kw, vw, pw, again, gw, uw, dw, fgain, upstream):
    hi, core, row, col = (lax.axis_index(a) for a in ("hi", "core", "row", "col"))
    rows = lax.axis_size("row")
    shards = 2 * rows
    seqs, sub = inputs.shape[0], inputs.shape[3]
    tokens = seqs * sub
    span = 8 * sub
    n_rows = qw.shape[0]
    is0 = col == 0
    ff = gw.shape[1]
    half_ff = ff // 2
    n_mid = 64
    n_main = half_ff - n_mid
    feat_c, rows_c, align_c = feature_constants()
    sds = jax.ShapeDtypeStruct
    x = inputs.reshape(tokens, D)

    shard_pairs = [(s, (s % rows) * 2 + s // rows) for s in range(shards)]
    moved = lax.ppermute(pw, ("row", "col"), shard_pairs)

    gain_one = again.astype(F32)[:, None]
    seg_own = segments.reshape(seqs, 4 * sub)

    def by_dest(w, scale):
        return (w.astype(F32) * scale).astype(BF16).reshape(n_rows, 8, -1)

    lane = lax.broadcasted_iota(jnp.int32, (n_rows, PAYLOAD - 320), 1)
    ends = jnp.pad(seg_own[:, -1], (0, n_rows - seqs)).astype(F32)[:, None]
    tens = jnp.floor(ends * (1.0 / 128.0))
    extra = jnp.where(
        lane == 0,
        fgain.astype(F32)[:, None],
        jnp.where(lane == 1, tens, jnp.where(lane == 2, ends - 128.0 * tens, 0.0)),
    ).astype(BF16)
    payload = jnp.concatenate(
        [
            by_dest(vw, gain_one),
            by_dest(qw, gain_one),
            by_dest(kw, gain_one),
            jnp.broadcast_to(extra[:, None], (n_rows, 8, PAYLOAD - 320)),
        ],
        2,
    ).transpose(1, 0, 2)
    payload = lax.all_to_all(payload, GROUP, split_axis=0, concat_axis=0, tiled=True)
    x_own = after(x, payload)
    xs = gather8(x_own)
    w_proj = lax.all_gather(moved, "row", axis=0, tiled=True)
    gathered = lax.all_gather(after(payload, moved), "row", axis=0, tiled=False)
    lasts = gathered[:, 1, :seqs, 321:323].astype(F32)
    lasts = (lasts[:, :, 0] * 128.0 + lasts[:, :, 1]).astype(jnp.int32)

    seg_other = swap(seg_own, "col")
    seg = jnp.concatenate([pick(is0, seg_own, seg_other), pick(is0, seg_other, seg_own)], 1)
    seg_row = seg.astype(F32)[:, None, :]
    before = jnp.where(row > 0, lasts[jnp.maximum(row - 1, 0)], -1)
    here = lasts[row]
    me3 = (4 * col + 2 * hi + core).astype(jnp.int32)
    meta = jnp.concatenate([me3[None], before, here])

    ends = jnp.concatenate([lasts, jnp.full((1, seqs), -1, jnp.int32)])

    def end_of(r):
        return ends[jnp.where((r >= 0) & (r < rows), r, rows)]

    def same(r, other):
        return ((end_of(r) == other) & (r >= 0) & (r < rows)).astype(F32)

    every = 8 * tokens
    qkv, inv, w_qkv = slot_call(
        qkv_kernel, xs, [(gathered.reshape(rows, 4, 2 * n_rows, PAYLOAD), False)],
        [sds((8, tokens, PAYLOAD), BF16), sds((8, tokens, 128), F32)], 2 * every * D * PAYLOAD,
        deps=[seg_row], whole=[sds((D, PAYLOAD), BF16)],
    )
    gain_two = w_qkv[:, 320].astype(F32)[None, :]
    inv = inv.reshape(8, seqs, sub, 128)
    ups = gather8(after(upstream.reshape(tokens, D), qkv))
    qkv = qkv.reshape(8, seqs, sub, PAYLOAD)
    st = sds((seqs, 2, FROWS, 128), BF16)
    near = 4 * seqs * span * span * 160
    far = 4 * seqs * span * FPAD * 300
    (state,) = attention_call(
        state_kernel, meta, [qkv, seg_row, feat_c, rows_c, align_c], "sqccc", [(st, "q")], far
    )
    mine = pick(is0, half_columns(gw, uw, 0, n_main, n_mid), half_columns(gw, uw, 1, n_main, n_mid))
    theirs = pick(is0, half_columns(gw, uw, 1, n_main, n_mid), half_columns(gw, uw, 0, n_main, n_mid))
    got = swap(after(theirs, xs[6][0], xs[7][0]), "col")
    got = after(got, state)
    gu_rows = jnp.concatenate([pick(is0, mine, got), pick(is0, got, mine)], 0)
    w_gu = lax.all_gather(gu_rows, "row", axis=0, tiled=True)
    down0 = dw[: n_main + n_mid]
    down1 = jnp.concatenate([dw[n_main + 2 * n_mid :], dw[n_main + n_mid : n_main + 2 * n_mid]], 0)
    d_mine, d_theirs = pick(is0, down0, down1), pick(is0, down1, down0)
    d_got = swap(after(d_theirs, got), "col")
    d_cols = jnp.stack([pick(is0, d_mine, d_got), pick(is0, d_got, d_mine)])
    w_down = lax.all_gather(d_cols, "row", axis=0, tiled=True)
    fold = shards // 8
    w_down = (
        w_down.reshape(8, fold, half_ff, D // shards).transpose(0, 2, 1, 3).reshape(8, half_ff, D // 8)
    )

    num, den_in = attention_call(
        intra_kernel, meta, [qkv, seg_row, align_c], "sqc",
        [(sds((seqs, span, 256), F32), "q"), (sds((seqs, span, 8), F32), "q")], near,
    )
    forth = walk_steps(state, lambda d: same(row - d, here), lambda d: same(row - d, before), True)
    _, came = next(forth)
    came, num, den_in = meet(came, num, den_in)
    state_in = finish(forth, came)
    o, den = attention_call(
        output_kernel, meta, [qkv, seg_row, feat_c, rows_c, align_c, num, den_in, state_in], "sqcccqqq",
        [(sds((8, seqs, sub, 256), BF16), "s"), (sds((seqs, span, 8), F32), "q")], far,
        [ups[6][0], ups[7][0], d_got],
    )
    o_rows = o.reshape(8, tokens, 256)
    residual, a2_own = row_call(
        residual_kernel, scatter8(parts_call(o_rows, w_proj, "nn", mib=28)), [x, gain_two], [F32, BF16]
    )

    ff_flops = 2 * every * D * half_ff
    steps = gather_steps(a2_own)
    wide = [
        sds((8, tokens, ff), BF16),
        sds((8, tokens, half_ff + n_mid), BF16),
        sds((8, half_ff + n_mid, tokens), BF16),
    ]
    hidden = slot_call(ffn_in_kernel, next(steps), [(w_gu, False)], wide, 2 * ff_flops, slots=(0, 2))
    hidden = slot_call(
        ffn_in_kernel, steps.send(hidden[:1]), [(w_gu, False)], wide, 2 * ff_flops, slots=(2, 6), into=hidden
    )
    a2 = finish(steps, hidden[:1])
    gu, h, h_turned = slot_call(
        ffn_in_kernel, a2, [(w_gu, False)], wide, 2 * ff_flops, slots=(6, 8), into=hidden
    )
    (down_g,) = grad_call(
        down_grad_kernel, ups, 256, [h_turned], [],
        [(sds((8, half_ff, 256), BF16), (1, half_ff, 256), lambda i: (i, 0, 0))], ff_flops,
    )
    late = {}

    def ffn_back(slots, into, deps=()):
        return slot_call(
            ffn_back_kernel, ups, [(w_down, False), (gu, True)], [sds((8, tokens, ff), BF16)], ff_flops, deps,
            slots=slots, into=into,
        )[0]

    half = tokens // 2
    dgu = ffn_back((0, 8), (), [down_g])
    own, other, y, yc, x_, xc, xy, xyc = parts_call(dgu, w_gu, "nt")
    other, yc, xc, xyc = (swap(part, "core") for part in (other, yc, xc, xyc))
    to_x = pair_sum(xy, xyc, 0, half).astype(BF16)
    to_y = pair_sum(xy, xyc, half, tokens).astype(BF16)
    near_x = pair_sum(x_, xc, 0, half).astype(BF16)
    near_y = pair_sum(y, yc, half, tokens).astype(BF16)
    down_g = (
        down_g.reshape(8, half_ff, fold, D // shards).transpose(0, 2, 1, 3).reshape(shards * half_ff, -1)
    )
    down_g = lax.psum_scatter(down_g, "row", scatter_dimension=0, tiled=True)
    block = D // shards
    gu_gs, gains = [], []

    def gu_half(x_bit):
        def run(sent):
            one, gain = grad_call(
                gu_grad_kernel, a2, 256, [dgu], [(w_gu, (256, ff), lambda i: (2 * i + x_bit, 0))],
                [
                    (sds((D // 2, ff), BF16), (256, ff), lambda i: (i, 0)),
                    (sds((D // 2, 128), F32), (256, 128), lambda i: (i, 0)),
                ],
                ff_flops, lambda i: 2 * i + x_bit, 4, sent,
            )
            gu_gs.append(one)
            gains.append(gain)
            return [one]

        return run

    gu_half(0)([to_x, to_y, near_x, near_y])
    from_x, from_y, first_x, first_y, gu_gs[0] = meet(
        swap(to_x, "col"), swap(to_y, "hi"), swap(near_x, "col"), swap(near_y, "hi"), gu_gs[0]
    )
    far_x = (pair_sum(x_, xc, half, tokens) + from_y.astype(F32)).astype(BF16)
    far_y = (pair_sum(y, yc, 0, half) + from_x.astype(F32)).astype(BF16)
    gu_half(1)([far_x, far_y, gu_gs[0]])
    last_x, last_y, gu_gs[1] = meet(swap(far_x, "col"), swap(far_y, "hi"), gu_gs[1])
    grad_r, datt_own = row_call(
        residual_back_kernel, [own, other, first_x, last_y, last_x, first_y],
        [upstream.reshape(tokens, D), residual, gain_two], [F32, BF16],
    )
    over_x, over_y, over_c, *down_parts = meet(
        swap(datt_own, "col"), swap(datt_own, "hi"), swap(datt_own, "core"),
        *parts_call(h, w_down, "blocks", [datt_own]),
    )
    to_x, to_y = over_y[:half], over_x[half:]
    over_yc, over_xc = swap(over_y, "core"), swap(over_x, "core")
    datt = [(datt_own, 0, 0), (over_c, 1, 0), (over_y, 2, 0), (over_yc, 3, 0), (over_x, 4, 0), (over_xc, 5, 0)]
    do_out = [sds((8, tokens, 256), BF16)]
    do_flops = 2 * every * D * 256
    (do,) = slot_call(do_kernel, datt, [(w_proj, False)], do_out, do_flops, [to_x, to_y], slots=(0, 6))
    top, low, do = meet(swap(to_x, "col"), swap(to_y, "hi"), do)
    datt += [(top, 6, 0), (low, 6, half), (swap(top, "core"), 7, 0), (swap(low, "core"), 7, half)]
    (do,) = slot_call(do_kernel, datt, [(w_proj, False)], do_out, do_flops, [down_g], slots=(6, 8), into=[do])
    gain_part = jnp.stack([g.reshape(4, 256, 128) for g in gains], 1).reshape(D, 128)
    if fold > 1:
        natural = jnp.stack([g.reshape(4, 256, ff) for g in gu_gs], 1)
        by_col = natural.reshape(rows, 2, block, ff).transpose(1, 0, 2, 3)
        gu_gs = [by_col[0].reshape(D // 2, ff), by_col[1].reshape(D // 2, ff)]
    gu_r = [lax.psum_scatter(g, "row", scatter_dimension=0, tiled=True) for g in gu_gs]

    do = do.reshape(8, seqs, sub, 256)

    (dstate,) = attention_call(
        back_state_kernel, meta, [qkv, seg_row, feat_c, rows_c, align_c, o, do, den], "sqcccssq",
        [(st, "q")], far,
    )
    part = sds((seqs, span, 256), F32)

    back = walk_steps(
        dstate,
        lambda d: same(row + d - 1, before) * (row + d < rows),
        lambda d: same(row + d - 1, here) * (row + d < rows),
        False,
    )
    _, came = next(back)
    own, other, y, yc, x_, xc, xy, xyc = down_parts
    other, yc, xc, xyc = (after(swap(part, "core"), dstate) for part in (other, yc, xc, xyc))
    to_x = pair_sum(xy, xyc, 0, half).astype(BF16)
    to_y = pair_sum(xy, xyc, half, tokens).astype(BF16)
    near_x = pair_sum(x_, xc, 0, half).astype(BF16)
    near_y = pair_sum(y, yc, half, tokens).astype(BF16)
    intra = attention_call(
        back_intra_kernel, meta, [qkv, seg_row, feat_c, rows_c, align_c, o, do, den, state_in],
        "sqcccssqq", [(part, "q")] * 3, 3 * near + far, [dstate, to_x, to_y, near_x, near_y, gu_r[0]],
    )
    dq, dk, dv = intra
    came, from_x, from_y, first_x, first_y, dq = meet(
        came, swap(to_x, "col"), swap(to_y, "hi"), swap(near_x, "col"), swap(near_y, "hi"), dq
    )
    far_x = (pair_sum(x_, xc, half, tokens) + from_y.astype(F32)).astype(BF16)
    far_y = (pair_sum(y, yc, 0, half) + from_x.astype(F32)).astype(BF16)
    step = back.send(came)
    now = None
    if step is not None:
        now, came = step
    (proj_g,) = grad_call(
        proj_grad_kernel, datt, 1024, [o_rows], [],
        [(sds((256, D), BF16), (256, 1024), lambda i: (0, i))], 2 * every * D * 256, deps=[far_x, far_y, now], mib=24,
    )
    down_r = down_g.reshape(2, half_ff, D // shards)
    d_keep, d_send = pick(is0, down_r[0], down_r[1]), pick(is0, down_r[1], down_r[0])
    g_keep = pick(is0, gu_r[0], gu_r[1])
    g_send = pick(is0, gu_r[1], gu_r[0])
    came, last_x, last_y, d_got, proj_g = meet(
        came, swap(far_x, "col"), swap(far_y, "hi"), swap(d_send, "col"), proj_g
    )
    (outputs,) = row_call(
        output_rows_kernel, [own, other, first_x, last_y, last_x, first_y], [residual], [BF16]
    )
    dstate_out = finish(back, came)
    proj_r = lax.psum_scatter(proj_g, "row", scatter_dimension=0, tiled=True)
    row_out = sds((8, seqs, sub, PAYLOAD), BF16)
    dqkv, scaled = attention_call(
        back_output_kernel, meta, [qkv, seg_row, feat_c, rows_c, align_c, dstate_out, dq, dk, dv, inv],
        "sqcccqqqqs", [(row_out, "s")] * 2, 2 * far, [outputs, gu_r[1]],
    )
    g_got, dqkv, scaled = meet(swap(g_send, "col"), dqkv, scaled)

    def qkv_side(sent):
        (late["qkv"],) = grad_call(
            qkv_grad_kernel, xs, 512, [scaled.reshape(8, tokens, PAYLOAD)],
            [(gain_part, (512, 128), lambda i: (i, 0))],
            [
                (
                    sds((rows, 4, 2 * n_rows, PAYLOAD), BF16),
                    (rows, 1, 2 * n_rows, PAYLOAD),
                    lambda i: (0, i, 0, 0),
                )
            ],
            2 * every * D * PAYLOAD, deps=sent, mib=24,
        )
        return [late["qkv"]]

    qkv_g = qkv_side([])[0]
    own, other, y, yc, x_, xc, xy, xyc = parts_call(
        dqkv.reshape(8, tokens, PAYLOAD), w_qkv, "nt", [qkv_g, proj_r], 28
    )
    other, yc, xc, xyc = (swap(part, "core") for part in (other, yc, xc, xyc))
    to_x = pair_sum(xy, xyc, 0, half).astype(BF16)
    to_y = pair_sum(xy, xyc, half, tokens).astype(BF16)
    near_x = pair_sum(x_, xc, 0, half).astype(BF16)
    near_y = pair_sum(y, yc, half, tokens).astype(BF16)
    from_x, from_y, first_x, first_y = (
        swap(to_x, "col"), swap(to_y, "hi"), swap(near_x, "col"), swap(near_y, "hi")
    )
    far_x = (pair_sum(x_, xc, half, tokens) + from_y.astype(F32)).astype(BF16)
    far_y = (pair_sum(y, yc, 0, half) + from_x.astype(F32)).astype(BF16)
    f_pieces = [own, other, first_x, swap(far_y, "hi"), swap(far_x, "col"), first_y]
    qkv_g = lax.psum_scatter(qkv_g.reshape(D, PAYLOAD), "row", scatter_dimension=0, tiled=True)
    project_grad = lax.ppermute(
        after(proj_r, f_pieces[5]), ("row", "col"), [(b, a) for a, b in shard_pairs]
    ).astype(F32)
    qkv_g = lax.all_to_all(
        qkv_g.reshape(8, n_rows, PAYLOAD), GROUP, split_axis=0, concat_axis=0, tiled=True
    )
    (inputs_grad,) = row_call(input_back_kernel, f_pieces, [x, grad_r], [F32])
    v_g, q_g, k_g, both_gains = weights_call(
        qkv_g, vw, qw, kw, jnp.stack([again.astype(F32), fgain.astype(F32)], 1)
    )
    attend_grad, forward_grad = both_gains[:, 0], both_gains[:, 1]
    d0, d1 = pick(is0, d_keep, d_got).astype(F32), pick(is0, d_got, d_keep).astype(F32)
    down_grad = jnp.concatenate([d0, d1[n_main:], d1[:n_main]], 0)
    g0, g1 = pick(is0, g_keep, g_got).astype(F32), pick(is0, g_got, g_keep).astype(F32)
    m = 2 * n_main
    gate_grad = jnp.concatenate(
        [g0[:, :n_main], g0[:, m : m + n_mid], g1[:, m : m + n_mid], g1[:, :n_main]], 1
    )
    up_grad = jnp.concatenate(
        [g0[:, n_main:m], g0[:, m + n_mid :], g1[:, m + n_mid :], g1[:, n_main:m]], 1
    )
    return (
        outputs.reshape(inputs.shape),
        inputs_grad.reshape(inputs.shape),
        q_g,
        k_g,
        v_g,
        project_grad,
        attend_grad,
        gate_grad,
        up_grad,
        down_grad,
        forward_grad,
    )


def solution(mesh):
    heads, shards = mesh.devices.shape
    fine = Mesh(mesh.devices.reshape(heads // 2, 2, shards // 2, 2), ("hi", "core", "row", "col"))
    h, s = ("hi", "core"), ("row", "col")
    every = P(h + s)
    tokens = P(None, s, h)
    return jax.shard_map(
        body,
        mesh=fine,
        in_specs=(
            tokens, P(None, s), every, every, every, every, every, P(s, h), P(s, h), P(h, s), every, tokens,
        ),
        out_specs=(
            tokens, tokens, every, every, every, every, every, P(s, h), P(s, h), P(h, s), every,
        ),
        check_vma=False,
    )
```
